128 devices in a mesh: dom: 16 (over y, x), sub: 8 (over z, core).
Axes of the slice: x: 4, y: 4, z: 4, core: 2. Of those that a mesh axis runs over, the one named last changes fastest.
Arguments:
- positions: float32 [8192, 3, 128], P(('dom', 'sub')), may hold values from -1 to 1
- masses: float32 [8192, 128], P(('dom', 'sub')), may hold values from 0.003 to 0.03
- owner: int32 [8192, 1], P(('dom', 'sub')), may hold values from 0 to 7; in each aligned block of 64 rows (0 to 63, 64 to 127, ...) at most 16 rows name the same one
- operators: float32 [165, 165, 128], replicated, may hold values from -0.0024414062 to 0.0024414062
- m2l_target: int32 [128, 8, 64, 128], P(('dom', 'sub')), may hold values from 0 to 127
- far_source: int32 [128, 7, 64, 128], P(('dom', 'sub')), may hold values from 0 to 31
- local_source: int32 [128, 64, 128], P(('dom', 'sub')), may hold values from 0 to 127
- export_slots: int32 [128, 7, 32], P(('dom', 'sub')), may hold values from 0 to 127
- near_target: int32 [128, 128], P(('dom', 'sub')), may hold values from 0 to 127
- near_source: int32 [128, 128], P(('dom', 'sub')), may hold values from 0 to 127
- near_offset: int32 [128, 128], P(('dom', 'sub')), may hold values from 0 to 26
Outputs:
- accel: float32 [16384, 4, 128], P(('dom', 'sub'))
The draws below stay inside these ranges and needn't reach their ends.
Inputs may be any that keep to these rules, and one draw needn't show every extreme that they name: Among the 64 tiles of one device at most 16 share an owner, and some device has an owner named by exactly 16 of its tiles.
All inputs are finite; a program needn't handle non-finite values.
Results may differ from the reference program's by a relative error of at most 0.0003.
Values sent between devices are 32-bit elements; how exact they have to be, the bound alone decides.
No kernel may reach another device: no remote copies, remote signals or barrier semaphores. Data moves between devices by JAX's collectives and lax.ppermute only.
A program may use at most 256 MiB of HBM per device.

```python
import math
from functools import partial
import jax
import jax.numpy as jnp
import numpy as np
from jax import lax

NCELL = 64
TILE = 128
ORDER = 8
OPS = 128
TERMS = 165
CAP = 16
RSLOT = 128
KEXP = 32
PER = 64
NPAIR = 128
LEVELS = 7
N_DOM = 16
N_SUB = 8
DEVICES = 128


def place_ends(values, key, smallest, top_value):
    dims = values.shape
    index_at = [jax.random.randint(jax.random.fold_in(key, axis), (), 0, dims[axis]) for axis in range(len(dims))]
    values = values.at[tuple(index_at)].set(smallest)
    longest = dims.index(max(dims))
    index_at[longest] = (index_at[longest] + 1) % dims[longest]
    return values.at[tuple(index_at)].set(top_value)


def block_scale(rng, shape, pieces, smallest, top_value):
    gain = 1.0
    for axis_at, shards_of in pieces:
        heights = jax.random.uniform(jax.random.fold_in(jax.random.fold_in(rng, 6), axis_at), (shards_of,), jnp.float32, smallest / len(pieces), top_value / len(pieces))
        gain = gain * jnp.repeat(jnp.exp(heights), shape[axis_at] // shards_of).reshape((-1,) + (1,) * (len(shape) - 1 - axis_at))
    return gain


def assign_block(own_key, own, number, rows, count, top, most, slope):
    order = jax.random.permutation(own_key, count)
    packed, common = shares(count, rows * top, most, slope, True), shares(count, rows * top, most, slope, False)
    places = jnp.arange(count)

    def named(sizes, offset_by):
        used = int((sizes > 0).sum())
        fixed = max(1, used // 4)
        shifted = fixed + (places - fixed + offset_by * (used - fixed)) % max(1, count - fixed)
        return jnp.zeros((count,), jnp.int32).at[order[jnp.where(places < fixed, places, shifted)]].set(jnp.asarray(sizes, jnp.int32))

    sizes = jnp.where(number % 4 == 0, named(packed, number // 4), named(common, number - number // 4 - 1))
    mixed = jax.random.permutation(jax.random.fold_in(own, 3), count)
    giver, taker = mixed[0:count // 2 * 2:2], mixed[1:count // 2 * 2:2]
    slack = jnp.minimum(sizes[giver] - 1, most - sizes[taker]) // 2
    slack = jnp.where((giver == order[0]) | (taker == order[0]) | (sizes[taker] == 0), 0, jnp.maximum(slack, 0))
    shifted = jax.random.randint(jax.random.fold_in(own, 4), (count // 2,), 0, 1 << 20) % (slack + 1)
    sizes = sizes.at[giver].add(-shifted).at[taker].add(shifted)
    members = jnp.searchsorted(jnp.cumsum(sizes), jnp.arange(rows * top), side="right").astype(jnp.int32)
    listing = members.reshape(top, rows).T
    listing = listing[jax.random.permutation(jax.random.fold_in(own, 1), rows)]
    offset_by = jax.random.randint(jax.random.fold_in(own, 2), (rows, 1), 0, top)
    return jnp.take_along_axis(listing, (jnp.arange(top)[None, :] + offset_by) % top, axis=1)


def shares(amount, total, limit, skew, full):
    loads = [(1 << 20) // math.isqrt(grade ** skew) + 1 for grade in range(1, amount + 1)]
    largest = limit if full else min(limit, max(-(-total // amount), total * loads[0] // sum(loads)))
    least = 1 if total - largest >= amount - 1 else 0
    holding, rest = [largest] + [least] * (amount - 1), total - largest - least * (amount - 1)
    while rest > 0:
        movable = [i for i in range(1, amount) if holding[i] < largest] or [i for i in range(1, amount) if holding[i] < limit]
        whole, budget = sum([loads[i] for i in movable]), rest
        for i in movable:
            extra = min(limit - holding[i], max(1, budget * loads[i] // whole), rest)
            holding[i] = holding[i] + extra
            rest = rest - extra
    return np.array(holding)


def scatter_about(own_key, shape, deviation, reach, held_as=jnp.bfloat16):
    values = deviation * jax.random.normal(own_key, shape, jnp.float32)
    return jnp.clip(values, min=-reach, max=reach).astype(held_as)


def setup_inputs(seed: int = 0) -> dict:
    arg_keys = jax.random.split(jax.random.key(seed), 12)
    positions = jnp.clip(jax.random.uniform(arg_keys[0], (DEVICES * NCELL, 3, TILE), jnp.float32, -1.0, 1.0) * block_scale(arg_keys[0], (DEVICES * NCELL, 3, TILE), ((0, 128),), -0.4, 0.0), -1.0, 1.0)
    masses = jnp.clip(jnp.exp(math.log(0.03) - 2.3025851 * jax.random.uniform(arg_keys[1], (DEVICES * NCELL, TILE), jnp.float32) ** block_scale(arg_keys[1], (DEVICES * NCELL, TILE), ((0, 128),), -0.2, 0.2)), 0.003, 0.03)
    owner_keys = jax.random.split(jax.random.fold_in(arg_keys[2], 1), (DEVICES * NCELL) // NCELL)
    owner_turns = jax.random.permutation(jax.random.fold_in(arg_keys[2], 3), (DEVICES * NCELL) // NCELL)
    owner = jax.vmap(lambda own, number: assign_block(jax.random.fold_in(arg_keys[2], 2), own, number, NCELL, N_SUB, 1, CAP, 2))(owner_keys, owner_turns).reshape((DEVICES * NCELL, 1))
    operators = scatter_about(arg_keys[3], (TERMS, TERMS, OPS), (2 * TERMS * TERMS * OPS) ** -0.5, 0.0024414062, jnp.float32)
    m2l_target = place_ends(jax.random.randint(arg_keys[4], (DEVICES, LEVELS + 1, PER, OPS), 0, RSLOT), jax.random.fold_in(arg_keys[4], 1), 0, RSLOT - 1).astype(jnp.int32)
    far_source = place_ends(jax.random.randint(arg_keys[5], (DEVICES, LEVELS, PER, OPS), 0, KEXP), jax.random.fold_in(arg_keys[5], 1), 0, KEXP - 1).astype(jnp.int32)
    local_source = place_ends(jax.random.randint(arg_keys[6], (DEVICES, PER, OPS), 0, RSLOT), jax.random.fold_in(arg_keys[6], 1), 0, RSLOT - 1).astype(jnp.int32)
    export_slots = place_ends(jax.random.randint(arg_keys[7], (DEVICES, LEVELS, KEXP), 0, RSLOT), jax.random.fold_in(arg_keys[7], 1), 0, RSLOT - 1).astype(jnp.int32)
    near_target = place_ends(jax.random.randint(arg_keys[8], (DEVICES, NPAIR), 0, RSLOT), jax.random.fold_in(arg_keys[8], 1), 0, RSLOT - 1).astype(jnp.int32)
    near_source = place_ends(jax.random.randint(arg_keys[9], (DEVICES, NPAIR), 0, RSLOT), jax.random.fold_in(arg_keys[9], 1), 0, RSLOT - 1).astype(jnp.int32)
    near_offset = place_ends(jax.random.randint(arg_keys[10], (DEVICES, NPAIR), 0, 27), jax.random.fold_in(arg_keys[10], 1), 0, 26).astype(jnp.int32)
    return {"positions": positions, "masses": masses, "owner": owner, "operators": operators, "m2l_target": m2l_target, "far_source": far_source, "local_source": local_source, "export_slots": export_slots, "near_target": near_target, "near_source": near_source, "near_offset": near_offset}


softening = 0.01
highest = lax.Precision.HIGHEST

def term_tables():
    triples = []
    for degree in range(ORDER + 1):
        for power_x in range(degree, -1, -1):
            for power_y in range(degree - power_x, -1, -1):
                triples.append((power_x, power_y, degree - power_x - power_y))
    lookup = {triple: term_index for term_index, triple in enumerate(triples)}
    exponents = np.array(triples, dtype=np.int32)
    term_norms = np.sqrt(np.prod(2.0 * exponents + 1.0, axis=1))
    number_terms = len(triples)
    slopes = np.zeros((3, number_terms, number_terms), dtype=np.float32)
    for term_index, triple in enumerate(triples):
        for direction in range(3):
            raised = list(triple)
            raised[direction] += 1
            raised = tuple(raised)
            if raised in lookup:
                raised_index = lookup[raised]
                slopes[direction, term_index, raised_index] = raised[direction] * term_norms[raised_index] / term_norms[term_index]
    return (exponents, term_norms.astype(np.float32), slopes)

def basis_values(places, exponents, term_norms):
    tables = []
    for direction in range(3):
        values = places[:, direction]
        powers = [jnp.ones_like(values)]
        for degree in range(ORDER):
            powers.append(powers[-1] * values)
        tables.append(jnp.stack(powers))
    result = tables[0][exponents[:, 0]] * tables[1][exponents[:, 1]] * tables[2][exponents[:, 2]]
    return result * jnp.asarray(term_norms).reshape(-1, 1, 1)

def pack_tiles(owners, places, weights, peer_count, capacity):
    onehot = (owners[:, None] == jnp.arange(peer_count, dtype=jnp.int32)[None, :]).astype(jnp.int32)
    earlier = (jnp.cumsum(onehot, axis=0) - onehot).astype(jnp.int32)
    rank_in = lax.optimization_barrier(jnp.sum(earlier * onehot, axis=1)).astype(jnp.int32)
    slot_index = (owners * capacity + rank_in).astype(jnp.int32)
    sent_places = jnp.zeros((peer_count * capacity,) + places.shape[1:], jnp.float32).at[slot_index].set(places)
    sent_weights = jnp.zeros((peer_count * capacity,) + weights.shape[1:], jnp.float32).at[slot_index].set(weights)
    return (sent_places, sent_weights)

def device_multipoles(places, weights, exponents, term_norms):
    slot_count = places.shape[0]
    bodies = places.shape[2]
    blocks = slot_count // 16

    def one_block(inputs):
        values = basis_values(inputs[0], exponents, term_norms)
        return jnp.einsum('nst,st->sn', values, inputs[1], precision=highest)
    result = lax.map(one_block, (places.reshape(blocks, 16, 3, bodies), weights.reshape(blocks, 16, bodies)))
    return result.reshape(slot_count, result.shape[2])

def translate(expansion, sources, operators, targets, rows):
    gathered = jnp.take(sources, rows, axis=0)
    translated = jnp.einsum('ijc,pcj->pci', operators, gathered, precision=highest)
    return expansion.at[targets.reshape(-1)].add(translated.reshape(-1, translated.shape[2]))

def near_block(places, weights, targets, sources, classes):
    shifts = 2.0 * jnp.stack([classes // 9 - 1, classes // 3 % 3 - 1, classes % 3 - 1], axis=1).astype(jnp.float32)
    source_places = places[sources] + shifts[:, :, None]
    target_places = places[targets]
    source_weights = weights[sources]
    separation = source_places[:, :, None, :] - target_places[:, :, :, None]
    inverse = lax.rsqrt(lax.optimization_barrier(jnp.sum(separation * separation, axis=1)) + softening)
    weighted = source_weights[:, None, :] * inverse
    potential = -lax.optimization_barrier(jnp.sum(weighted, axis=2))
    cubed_inv = weighted * inverse * inverse
    pull_terms = lax.optimization_barrier(jnp.sum(separation * cubed_inv[:, None], axis=3))
    return jnp.concatenate([potential[:, None], pull_terms], axis=1)

def device_field(places, weights, expansion, targets, sources, classes, exponents, term_norms, slopes):
    slot_count = places.shape[0]
    bodies = places.shape[2]
    blocks = slot_count // 16
    terms_count = expansion.shape[1]
    gradients = jnp.einsum('aij,sj->asi', jnp.asarray(slopes), expansion, precision=highest)
    stacked = jnp.concatenate([expansion[None], -gradients], axis=0)
    stacked = jnp.moveaxis(stacked.reshape(4, blocks, 16, terms_count), 1, 0)

    def far_block(inputs):
        values = basis_values(inputs[0], exponents, term_norms)
        return jnp.einsum('csn,nst->sct', inputs[1], values, precision=highest)
    far_field = lax.map(far_block, (places.reshape(blocks, 16, 3, bodies), stacked)).reshape(slot_count, 4, bodies)
    pair_blocks = targets.shape[0] // 16

    def near_part(inputs):
        return near_block(places, weights, inputs[0], inputs[1], inputs[2])
    near_terms = lax.map(near_part, (targets.reshape(pair_blocks, 16), sources.reshape(pair_blocks, 16), classes.reshape(pair_blocks, 16)))
    near_field = jnp.zeros((slot_count, 4, bodies), jnp.float32).at[targets].add(near_terms.reshape(-1, 4, bodies))
    present = (weights[:, :1] > 0).astype(jnp.float32)[:, :, None]
    return (far_field + near_field) * present

def pick_rows(matrix, rows):
    return jnp.take(matrix, rows, axis=0)

def reference(positions, masses, owner, operators, m2l_target, far_source, local_source, export_slots, near_target, near_source, near_offset):
    exponents, term_norms, slopes = term_tables()
    grouped_places = positions.reshape(N_DOM, N_SUB, NCELL, 3, TILE)
    grouped_weights = masses.reshape(N_DOM, N_SUB, NCELL, TILE)
    grouped_owners = owner.reshape(N_DOM, N_SUB, NCELL)
    packer = jax.vmap(jax.vmap(partial(pack_tiles, peer_count=N_SUB, capacity=CAP)))
    sent_places, sent_weights = packer(grouped_owners, grouped_places, grouped_weights)
    tile_places = sent_places.reshape(N_DOM, N_SUB, N_SUB, CAP, 3, TILE).transpose(0, 2, 1, 3, 4, 5).reshape(DEVICES, RSLOT, 3, TILE)
    tile_masses = sent_weights.reshape(N_DOM, N_SUB, N_SUB, CAP, TILE).transpose(0, 2, 1, 3, 4).reshape(DEVICES, RSLOT, TILE)

    def multipole_of(inputs):
        return device_multipoles(inputs[0], inputs[1], exponents, term_norms)
    multipoles = lax.map(multipole_of, (tile_places, tile_masses))
    exported = jax.vmap(jax.vmap(pick_rows, in_axes=(None, 0)))(multipoles, export_slots)

    def expansion_of(device_index):
        accumulated = jnp.zeros((RSLOT, TERMS), jnp.float32)
        accumulated = translate(accumulated, multipoles[device_index], operators, m2l_target[device_index, LEVELS], local_source[device_index])
        for bit_level in range(LEVELS):
            partner = jnp.bitwise_xor(device_index, 1 << bit_level)
            accumulated = translate(accumulated, exported[partner, bit_level], operators, m2l_target[device_index, bit_level], far_source[device_index, bit_level])
        return accumulated
    expansions = lax.map(expansion_of, jnp.arange(DEVICES, dtype=jnp.int32))

    def field_of(inputs):
        return device_field(inputs[0], inputs[1], inputs[2], inputs[3], inputs[4], inputs[5], exponents, term_norms, slopes)
    fields = lax.map(field_of, (tile_places, tile_masses, expansions, near_target, near_source, near_offset))
    return fields.reshape(DEVICES * RSLOT, 4, TILE)
```

```python
import functools

import jax
import jax.numpy as jnp
import numpy as np
from jax import lax
from jax.experimental import pallas as pl
from jax.experimental.pallas import tpu as pltpu
from jax.sharding import PartitionSpec as P

ORDER = 8
TERMS = 165
ROWS = 168
SOFT = 0.01
SLOTS = 128
BODIES = 128
KEXP = 32
LEVELS = 7
CLASSES = 128
SOURCES = SLOTS + LEVELS * KEXP
f32 = jnp.float32
bf16 = jnp.bfloat16
VMEM = pltpu.VMEM
SMEM = pltpu.SMEM


def term_list():
    triples = []
    for degree in range(ORDER + 1):
        for a in range(degree, -1, -1):
            for b in range(degree - a, -1, -1):
                triples.append((a, b, degree - a - b))
    return {t: n for n, t in enumerate(triples)}


TERM = term_list()
NORM = {t: float(np.float32(np.sqrt(np.prod(2.0 * np.array(t) + 1.0)))) for t in TERM}


def iota(shape, axis):
    return lax.broadcasted_iota(jnp.int32, shape, axis)


def dot(a, b):
    return jnp.dot(a, b, preferred_element_type=f32)


def dot_nt(a, b):
    return lax.dot_general(a, b, (((1,), (1,)), ((), ())), preferred_element_type=f32)


def dot_exact(a, b):
    return jnp.dot(a, b, preferred_element_type=f32, precision=lax.Precision.HIGHEST)


def pack_kernel(owner_ref, pos_ref, mass_ref, out_ref, count_ref, *slot_refs):
    for r in slot_refs:
        r[...] = jnp.zeros_like(r)
    for o in range(8):
        count_ref[o] = 0

    def step(i, carry):
        o = owner_ref[i, 0]
        rank = count_ref[o]
        count_ref[o] = rank + 1
        slot = o * 16 + rank
        tile = pos_ref[i]
        for a in range(3):
            slot_refs[a][pl.ds(slot, 1), :] = tile[a : a + 1, :]
        slot_refs[3][pl.ds(slot, 1), :] = mass_ref[pl.ds(i, 1), :]
        return carry

    lax.fori_loop(0, pos_ref.shape[0], step, 0)
    for a in range(4):
        out_ref[:, a * BODIES : (a + 1) * BODIES] = slot_refs[a][...]


def pack_tiles(owner, positions, masses):
    return pl.pallas_call(
        pack_kernel,
        out_shape=jax.ShapeDtypeStruct((SLOTS, 4 * BODIES), f32),
        in_specs=[
            pl.BlockSpec(memory_space=SMEM),
            pl.BlockSpec(memory_space=VMEM),
            pl.BlockSpec(memory_space=VMEM),
        ],
        out_specs=pl.BlockSpec(memory_space=VMEM),
        scratch_shapes=[pltpu.SMEM((8,), jnp.int32)] + [pltpu.VMEM((SLOTS, BODIES), f32)] * 4,
        name="pack",
    )(owner, positions, masses)


A_STEP = 8


def count_kernel(tgt_ref, far_ref, local_ref, out_ref, tt_ref, st_ref):
    step = pl.program_id(0)

    @pl.when(step == 0)
    def _():
        order = [7, 0, 1, 2, 3, 4, 5, 6]
        for pair in range(4):
            tgt, src = [], []
            for level in order[2 * pair : 2 * pair + 2]:
                tgt.append(tgt_ref[level].astype(f32))
                if level == 7:
                    src.append(local_ref[...].astype(f32))
                else:
                    offset = SLOTS + KEXP * level if level < 3 else KEXP * (level - 3)
                    src.append((far_ref[level] + offset).astype(f32))
            lanes = slice(pair * 128, pair * 128 + 128)
            tt_ref[:, lanes] = jnp.concatenate(tgt, axis=0).T
            st_ref[:, lanes] = jnp.concatenate(src, axis=0).T

    rows = pl.ds(pl.multiple_of(step * A_STEP, A_STEP), A_STEP)
    tt = tt_ref[rows, :]
    st = st_ref[rows, :]

    def onehot(row, size):
        ids = iota((size, 256), 0).astype(f32)
        return jnp.where(row == ids, 1.0, 0.0).astype(bf16)

    for k in range(A_STEP):
        for half, (first, size) in enumerate(((0, 224), (224, 128))):
            lanes = slice(half * 256, half * 256 + 256)
            target = onehot(tt[k : k + 1, lanes], 128)
            source = onehot(st[k : k + 1, lanes], size)
            counts = dot_nt(source, target)
            out_ref[k // 2, first : first + size, (k % 2) * 128 : (k % 2) * 128 + 128] = counts.astype(bf16)


def count_pairs(m2l_target, far_source, local_source):
    whole = lambda *shape: pl.BlockSpec(shape, lambda g: (0,) * len(shape))
    return pl.pallas_call(
        count_kernel,
        grid=(CLASSES // A_STEP,),
        out_shape=jax.ShapeDtypeStruct((CLASSES // 2, SOURCES, 256), bf16),
        in_specs=[whole(8, 64, 128), whole(7, 64, 128), whole(64, 128)],
        out_specs=pl.BlockSpec((A_STEP // 2, SOURCES, 256), lambda g: (g, 0, 0)),
        scratch_shapes=[pltpu.VMEM((128, 512), f32), pltpu.VMEM((128, 512), f32)],
        cost_estimate=pl.CostEstimate(flops=12 * 10**9, bytes_accessed=13 * 10**6, transcendentals=0),
        name="counts",
    )(m2l_target, far_source, local_source)


def multipole_kernel(recv_ref, slots_ref, mt_ref, post_ref, *rest):
    exp_refs, (acc_ref, m_ref, rows_ref) = rest[:LEVELS], rest[LEVELS:]
    for a in range(4):
        post_ref[a] = recv_ref[:, a * BODIES : (a + 1) * BODIES].T

    acc_ref[...] = jnp.zeros_like(acc_ref)

    def chunk(q, carry):
        rows = pl.ds(pl.multiple_of(q * 32, 32), 32)
        x, y, z, m = (post_ref[a, rows, :] for a in range(4))

        def fold(term, n):
            part = (term[0:8] + term[8:16]) + (term[16:24] + term[24:32])
            acc_ref[n] += part

        px = m
        for a in range(ORDER + 1):
            py = px
            for b in range(ORDER + 1 - a):
                pz = py
                for c in range(ORDER + 1 - a - b):
                    fold(pz, TERM[a, b, c])
                    if c < ORDER - a - b:
                        pz = pz * z
                if b < ORDER - a:
                    py = py * y
            if a < ORDER:
                px = px * x
        return carry

    lax.fori_loop(0, BODIES // 32, chunk, 0)
    mt_ref[TERMS - 5 :, :] = jnp.zeros((ROWS - TERMS + 5, SLOTS), f32)
    for (a, b, c), n in TERM.items():
        mt_ref[n : n + 1, :] = jnp.sum(acc_ref[n], axis=0, keepdims=True) * NORM[a, b, c]
    m_ref[0] = mt_ref[0:128, :].T
    m_ref[1] = jnp.concatenate([mt_ref[128:ROWS, :], jnp.zeros((256 - ROWS, SLOTS), f32)], axis=0).T
    for level in range(LEVELS):

        def row(k, carry):
            slot = slots_ref[level, k]
            for half in range(2):
                rows_ref[half, pl.ds(k, 1), :] = m_ref[half, pl.ds(slot, 1), :]
            return carry

        lax.fori_loop(0, KEXP, row, 0, unroll=8)
        for half in range(2):
            exp_refs[level][:, half * 128 : half * 128 + 128] = rows_ref[half]


def multipoles_of(recv, export_slots):
    vm = pl.BlockSpec(memory_space=VMEM)
    out = pl.pallas_call(
        multipole_kernel,
        out_shape=[
            jax.ShapeDtypeStruct((ROWS, SLOTS), f32),
            jax.ShapeDtypeStruct((4, BODIES, SLOTS), f32),
        ]
        + [jax.ShapeDtypeStruct((KEXP, 256), f32)] * LEVELS,
        in_specs=[vm, pl.BlockSpec(memory_space=SMEM)],
        out_specs=[vm] * (2 + LEVELS),
        scratch_shapes=[
            pltpu.VMEM((TERMS, 8, SLOTS), f32),
            pltpu.VMEM((2, SLOTS, 128), f32),
            pltpu.VMEM((2, KEXP, 128), f32),
        ],
        name="multipoles",
    )(recv, export_slots)
    return out[0], out[1], out[2:]


def near_kernel(recv_ref, tgt_ref, src_ref, off_ref, near_ref, s_ref, t_ref, a_ref):
    def column(ref):
        return jnp.broadcast_to(ref[...].astype(f32), (128, 128)).T

    lane = iota((128, 128), 1).astype(f32)
    pick_s = jnp.where(column(src_ref) == lane, 1.0, 0.0)
    pick_t = jnp.where(column(tgt_ref) == lane, 1.0, 0.0)
    s_ref[...] = dot_exact(pick_s, recv_ref[...])
    t_ref[...] = dot_exact(pick_t, recv_ref[:, 0:384])
    k = column(off_ref)
    one = jnp.ones_like(k)
    kx = jnp.where(k >= 9.0, one, 0.0) + jnp.where(k >= 18.0, one, 0.0)
    k = k - 9.0 * kx
    ky = jnp.where(k >= 3.0, one, 0.0) + jnp.where(k >= 6.0, one, 0.0)
    kz = k - 3.0 * ky
    for a, shift in enumerate((kx, ky, kz)):
        lanes = slice(a * 128, a * 128 + 128)
        s_ref[:, lanes] = s_ref[:, lanes] + 2.0 * (shift - 1.0)

    def group(g, carry):
        rows = pl.ds(pl.multiple_of(g * 32, 32), 32)
        tx, ty, tz = (t_ref[rows, a * 128 : a * 128 + 128] for a in range(3))

        def turn(i, state):
            sx, sy, sz, m, p, ax, ay, az = state
            rx, ry, rz = sx - tx, sy - ty, sz - tz
            inv = lax.rsqrt(rx * rx + ry * ry + rz * rz + SOFT)
            w = m * inv
            p = p - w
            w = w * inv * inv
            ax, ay, az = ax + rx * w, ay + ry * w, az + rz * w
            sx, sy, sz, m = (pltpu.roll(v, 1, 1) for v in (sx, sy, sz, m))
            return sx, sy, sz, m, p, ax, ay, az

        zero = jnp.zeros((32, 128), f32)
        start = tuple(s_ref[rows, a * 128 : a * 128 + 128] for a in range(4)) + (zero,) * 4
        done = lax.fori_loop(0, 128, turn, start, unroll=4)
        for a in range(4):
            a_ref[rows, a * 128 : a * 128 + 128] = done[4 + a]
        return carry

    lax.fori_loop(0, 4, group, 0)
    into = jnp.where(tgt_ref[...] == iota((128, 128), 0), 1.0, 0.0)
    near_ref[...] = dot_exact(into, a_ref[...])


def near_field(recv, target, source, offset):
    vm = pl.BlockSpec(memory_space=VMEM)
    return pl.pallas_call(
        near_kernel,
        out_shape=jax.ShapeDtypeStruct((SLOTS, 4 * BODIES), f32),
        in_specs=[vm] * 4,
        out_specs=vm,
        scratch_shapes=[
            pltpu.VMEM((128, 512), f32),
            pltpu.VMEM((128, 384), f32),
            pltpu.VMEM((128, 512), f32),
        ],
        cost_estimate=pl.CostEstimate(flops=8 * 10**9, bytes_accessed=10**6, transcendentals=2 * 10**6),
        name="near",
    )(recv, target, source, offset)


C_STEP = 4
PHASE1 = CLASSES // 2 // C_STEP
J_STEP = 8
PHASE2 = (TERMS + J_STEP - 1) // J_STEP


def split(v):
    high = v.astype(bf16)
    return high, (v - high.astype(f32)).astype(bf16)


def field_kernel(counts_ref, op_ref, mt_ref, *rest):
    far_refs, rest = rest[:LEVELS], rest[LEVELS:]
    post_ref, near_ref, recv_ref, out_ref, src_ref, bt_ref, acc_ref, e_ref, f_ref = rest
    step = pl.program_id(0)

    @pl.when(step == 0)
    def _():
        far = jnp.concatenate([r[...] for r in far_refs], axis=0)
        far = jnp.concatenate([far, jnp.zeros((32, 256), f32)], axis=0)
        own = mt_ref[...]
        parts = [own]
        for q in range(2):
            block = far[q * 128 : q * 128 + 128, :]
            parts.append(jnp.concatenate([block[:, 0:128].T, block[:, 128:256].T[0 : ROWS - 128]], axis=0))
        sources = jnp.concatenate(parts, axis=1)
        high = sources.astype(bf16).astype(f32)
        both = jnp.concatenate([high, sources - high], axis=0).astype(bf16)
        src_ref[...] = both[:, 0:SOURCES]

    @pl.when(step < PHASE1)
    def _():
        for q in range(C_STEP):
            moved = dot(src_ref[...], counts_ref[q])
            moved = moved[0:ROWS] + moved[ROWS : 2 * ROWS]
            for k in range(2):
                c = (step * C_STEP + q) * 2 + k
                bt_ref[pl.ds(c, ROWS, stride=CLASSES), :] = moved[:, k * 128 : k * 128 + 128]

    @pl.when(step >= PHASE1)
    def _():
        jb = step - PHASE1
        ops = op_ref.reshape(ROWS * J_STEP, CLASSES)
        left, right = [], []
        for j in range(J_STEP):
            o = ops[pl.ds(j, ROWS, stride=J_STEP), :]
            o = jnp.where(jb * J_STEP + j < TERMS, o, 0.0)
            high = o.astype(bf16).astype(f32)
            left.append(jnp.concatenate([high, o - high], axis=0).astype(bf16))
            b = bt_ref[pl.ds(pl.multiple_of((jb * J_STEP + j) * CLASSES, CLASSES), CLASSES), :]
            right.append(jnp.concatenate(split(b), axis=1))
        total = dot(jnp.concatenate(left, axis=1), jnp.concatenate(right, axis=0))

        @pl.when(jb == 0)
        def _():
            acc_ref[...] = total

        @pl.when(jb > 0)
        def _():
            acc_ref[...] += total

    @pl.when(step == PHASE1 + PHASE2 - 1)
    def _():
        acc = acc_ref[...]
        e_ref[...] = (acc[ROWS:, 128:] + acc[ROWS:, :128]) + acc[:ROWS, 128:] + acc[:ROWS, :128]

        def chunk(q, carry):
            rows = pl.ds(pl.multiple_of(q * 32, 32), 32)
            x, y, z = (post_ref[a, rows, :] for a in range(3))

            def coef(a, b, c):
                n = TERM[a, b, c]
                return jnp.broadcast_to(e_ref[n : n + 1, :] * NORM[a, b, c], (32, SLOTS))

            p = px = py = pz = None
            for a in range(ORDER, -1, -1):
                r = ry = rz = None
                for b in range(ORDER - a, -1, -1):
                    top = ORDER - a - b
                    v = coef(a, b, top)
                    vz = None
                    for c in range(top - 1, -1, -1):
                        vz = v if vz is None else vz * z + v
                        v = v * z + coef(a, b, c)
                    if r is None:
                        r = v
                    else:
                        ry = r if ry is None else ry * y + r
                        r = r * y + v
                        if vz is not None:
                            rz = vz if rz is None else rz * y + vz
                if p is None:
                    p = r
                else:
                    px = p if px is None else px * x + p
                    p = p * x + r
                    py = ry if py is None else py * x + ry
                    pz = rz if pz is None else pz * x + rz
            f_ref[0, rows, :] = p
            f_ref[1, rows, :] = -px
            f_ref[2, rows, :] = -py
            f_ref[3, rows, :] = -pz
            return carry

        lax.fori_loop(0, BODIES // 32, chunk, 0)
        present = recv_ref[:, 3 * BODIES : 3 * BODIES + 1] > 0.0
        present = jnp.where(present, jnp.ones((SLOTS, BODIES), f32), 0.0)
        for a in range(4):
            out_ref[:, a, :] = (f_ref[a].T + near_ref[:, a * BODIES : (a + 1) * BODIES]) * present


def field(counts, operators, mt, far, post, near, recv):
    whole = lambda *shape: pl.BlockSpec(shape, lambda g: (0,) * len(shape))
    return pl.pallas_call(
        field_kernel,
        grid=(PHASE1 + PHASE2,),
        out_shape=jax.ShapeDtypeStruct((SLOTS, 4, BODIES), f32),
        in_specs=[
            pl.BlockSpec((C_STEP, SOURCES, 256), lambda g: (jnp.minimum(g, PHASE1 - 1), 0, 0)),
            pl.BlockSpec((ROWS, J_STEP, CLASSES), lambda g: (0, jnp.maximum(g - PHASE1, 0), 0)),
            whole(ROWS, SLOTS),
        ]
        + [whole(KEXP, 256)] * LEVELS
        + [whole(4, BODIES, SLOTS), whole(SLOTS, 4 * BODIES), whole(SLOTS, 4 * BODIES)],
        out_specs=whole(SLOTS, 4, BODIES),
        scratch_shapes=[
            pltpu.VMEM((2 * ROWS, SOURCES), bf16),
            pltpu.VMEM((ROWS * CLASSES, SLOTS), f32),
            pltpu.VMEM((2 * ROWS, 256), f32),
            pltpu.VMEM((ROWS, SLOTS), f32),
            pltpu.VMEM((4, BODIES, SLOTS), f32),
        ],
        compiler_params=pltpu.CompilerParams(vmem_limit_bytes=48 * 2**20),
        cost_estimate=pl.CostEstimate(flops=40 * 10**9, bytes_accessed=26 * 10**6, transcendentals=0),
        name="field",
    )(counts, operators, mt, *far, post, near, recv)


def body(
    positions,
    masses,
    owner,
    operators,
    m2l_target,
    far_source,
    local_source,
    export_slots,
    near_target,
    near_source,
    near_offset,
):
    axes = ("dom", "sub")
    devices = lax.axis_size(axes)
    sent = pack_tiles(owner, positions, masses)
    recv = lax.all_to_all(sent, "sub", split_axis=0, concat_axis=0, tiled=True)
    counts = count_pairs(m2l_target[0], far_source[0], local_source[0])
    mt, post, exported = multipoles_of(recv, export_slots[0])
    far = [
        lax.ppermute(rows, axes, [(i, i ^ (1 << level)) for i in range(devices)])
        for level, rows in enumerate(exported)
    ]
    near = near_field(recv, near_target, near_source, near_offset)
    return field(counts, operators, mt, far, post, near, recv)


def solution(mesh):
    both = ("dom", "sub")
    in_specs = (
        P(both, None, None),
        P(both, None),
        P(both, None),
        P(),
        P(both, None, None, None),
        P(both, None, None, None),
        P(both, None, None),
        P(both, None, None),
        P(both, None),
        P(both, None),
        P(both, None),
    )
    out_specs = P(both, None, None)
    return jax.shard_map(body, mesh=mesh, in_specs=in_specs, out_specs=out_specs, check_vma=False)
```

```python
import functools

import jax
import jax.numpy as jnp
import numpy as np
from jax import lax
from jax.experimental import pallas as pl
from jax.experimental.pallas import tpu as pltpu
from jax.sharding import PartitionSpec as P

ORDER = 8
TERMS = 165
ROWS = 168
TERMS_PAD = ROWS
SOFT = 0.01
SLOTS = 128
BODIES = 128
KEXP = 32
LEVELS = 7
CLASSES = 128
SOURCES = SLOTS + LEVELS * KEXP
f32 = jnp.float32
bf16 = jnp.bfloat16
VMEM = pltpu.VMEM
SMEM = pltpu.SMEM


def term_list():
    triples = []
    for degree in range(ORDER + 1):
        for a in range(degree, -1, -1):
            for b in range(degree - a, -1, -1):
                triples.append((a, b, degree - a - b))
    return {t: n for n, t in enumerate(triples)}


TERM = term_list()
NORM = {t: float(np.float32(np.sqrt(np.prod(2.0 * np.array(t) + 1.0)))) for t in TERM}


def small(mib):
    return pltpu.CompilerParams(vmem_limit_bytes=mib * 2**20)


def iota(shape, axis):
    return lax.broadcasted_iota(jnp.int32, shape, axis)


def split(v):
    high = v.astype(bf16)
    return high, (v - high.astype(f32)).astype(bf16)


def dot(a, b):
    return jnp.dot(a, b, preferred_element_type=f32)


def dot_nt(a, b):
    return lax.dot_general(a, b, (((1,), (1,)), ((), ())), preferred_element_type=f32)


def dot_exact(a, b):
    return jnp.dot(a, b, preferred_element_type=f32, precision=lax.Precision.HIGHEST)


def pack_kernel(owner_ref, pos_ref, mass_ref, out_ref, count_ref, *slot_refs):
    for r in slot_refs:
        r[...] = jnp.zeros_like(r)
    for o in range(8):
        count_ref[o] = 0

    def step(i, carry):
        o = owner_ref[0, i]
        rank = count_ref[o]
        count_ref[o] = rank + 1
        slot = o * 16 + rank
        for a in range(3):
            slot_refs[a][pl.ds(slot, 1), :] = pos_ref[a, pl.ds(i, 1), :]
        slot_refs[3][pl.ds(slot, 1), :] = mass_ref[pl.ds(i, 1), :]
        return carry

    lax.fori_loop(0, mass_ref.shape[0], step, 0)
    for a in range(4):
        out_ref[:, a * BODIES : (a + 1) * BODIES] = slot_refs[a][...]


def pack_tiles(owner, positions, masses):
    return pl.pallas_call(
        pack_kernel,
        out_shape=pltpu.HBM((SLOTS, 4 * BODIES), f32),
        in_specs=[
            pl.BlockSpec(memory_space=SMEM),
            pl.BlockSpec(memory_space=VMEM),
            pl.BlockSpec(memory_space=VMEM),
        ],
        out_specs=pl.BlockSpec(memory_space=VMEM),
        scratch_shapes=[pltpu.SMEM((8,), jnp.int32)] + [pltpu.VMEM((SLOTS, BODIES), f32)] * 4,
        compiler_params=small(2),
        name="pack",
    )(owner.T, positions.transpose(1, 0, 2), masses)


I_STEP = 16
I_FULL = TERMS // I_STEP
I_ROWS = (I_FULL + 1) * I_STEP
J_STEP = 8
PITCH = CLASSES + 1
J_BLOCKS = ROWS // J_STEP


def prepare_kernel(tgt_ref, far_ref, local_ref, op_ref, counts_ref, left_ref, tt_ref, st_ref, buf_ref, sem):
    def copy(q, size):
        return pltpu.make_async_copy(
            op_ref.at[pl.ds(q * I_STEP, size)], buf_ref.at[q, pl.ds(0, size), pl.ds(0, TERMS)], sem.at[q]
        )

    for q in range(I_FULL):
        copy(q, I_STEP).start()
    copy(I_FULL, TERMS - I_FULL * I_STEP).start()

    order = [7, 0, 1, 2, 3, 4, 5, 6]
    for pair in range(4):
        tgt, src = [], []
        for level in order[2 * pair : 2 * pair + 2]:
            tgt.append(tgt_ref[level].astype(f32))
            if level == 7:
                src.append(local_ref[...].astype(f32))
            else:
                offset = {0: SLOTS, 1: 0, 2: KEXP, 3: 0, 4: KEXP, 5: 0, 6: KEXP}[level]
                src.append((far_ref[level] + offset).astype(f32))
        tt_ref[pair] = jnp.concatenate(tgt, axis=0).T
        st_ref[pair] = jnp.concatenate(src, axis=0).T

    ids = iota((160, 128), 0).astype(f32).astype(bf16)

    def onehot(ref, part, c, first, size, total):
        row = jnp.broadcast_to(ref[part, pl.ds(c, 1), :].astype(bf16), (size, 128))
        hits = jnp.where(row == ids[0:size], jnp.ones((), bf16), jnp.zeros((), bf16))
        zeros = lambda n: [jnp.zeros((n, 128), bf16)] if n else []
        return jnp.concatenate(zeros(first) + [hits] + zeros(total - first - size), axis=0)

    def classes(p, carry):
        for k in range(2):
            c = 2 * p + k
            for half, (first, size) in enumerate(((0, 224), (224, 128))):
                cut = 160 if half == 0 else 64
                target = jnp.concatenate([onehot(tt_ref, 2 * half + i, c, 0, 128, 128) for i in range(2)], axis=1)
                source = jnp.concatenate(
                    [
                        onehot(st_ref, 2 * half, c, 0, cut, size),
                        onehot(st_ref, 2 * half + 1, c, cut, size - cut, size),
                    ],
                    axis=1,
                )
                counts = dot_nt(source, target)
                counts_ref[p, first : first + size, k * 128 : k * 128 + 128] = counts.astype(bf16)
        return carry

    lax.fori_loop(0, CLASSES // 2, classes, 0, unroll=16)

    for j in range(TERMS, ROWS):
        left_ref[J_BLOCKS - 1, :, (j % J_STEP) * 128 : (j % J_STEP) * 128 + 128] = jnp.zeros((2 * I_ROWS, 128), bf16)

    def relay(q):
        rows = buf_ref.at[q].reshape(I_STEP * TERMS_PAD, CLASSES)
        at = pl.multiple_of(q * I_STEP, I_STEP)
        for j in range(TERMS):
            v = rows[pl.ds(j, I_STEP, stride=TERMS_PAD), :]
            high, low = split(v)
            lanes = slice((j % J_STEP) * 128, (j % J_STEP) * 128 + 128)
            left_ref[j // J_STEP, pl.ds(at, I_STEP), lanes] = high
            left_ref[j // J_STEP, pl.ds(at + I_ROWS, I_STEP), lanes] = low

    def chunk(q, carry):
        copy(q, I_STEP).wait()
        relay(q)
        return carry

    lax.fori_loop(0, I_FULL, chunk, 0)
    copy(I_FULL, TERMS - I_FULL * I_STEP).wait()
    relay(I_FULL)


def prepare(m2l_target, far_source, local_source, operators):
    vm = pl.BlockSpec(memory_space=VMEM)
    return pl.pallas_call(
        prepare_kernel,
        out_shape=[
            VMEM((CLASSES // 2, SOURCES, 256), bf16),
            VMEM((J_BLOCKS, 2 * I_ROWS, J_STEP * CLASSES), bf16),
        ],
        in_specs=[vm, vm, vm, pl.BlockSpec(memory_space=pl.ANY)],
        out_specs=[vm, vm],
        scratch_shapes=[
            VMEM((4, 128, 128), f32),
            VMEM((4, 128, 128), f32),
            VMEM((I_FULL + 1, I_STEP, TERMS_PAD, CLASSES), f32),
            pltpu.SemaphoreType.DMA((I_FULL + 1,)),
        ],
        compiler_params=small(20),
        cost_estimate=pl.CostEstimate(flops=12 * 10**9, bytes_accessed=14 * 10**6, transcendentals=0),
        name="prepare",
    )(m2l_target, far_source, local_source, operators)


def multipole_kernel(recv_ref, slots_ref, mt_ref, post_ref, *rest):
    exp_refs, (acc_ref, m_ref, rows_ref) = rest[:LEVELS], rest[LEVELS:]
    for a in range(4):
        post_ref[a] = recv_ref[:, a * BODIES : (a + 1) * BODIES].T

    acc_ref[...] = jnp.zeros_like(acc_ref)

    def chunk(q, carry):
        rows = pl.ds(pl.multiple_of(q * 32, 32), 32)
        x, y, z, m = (post_ref[a, rows, :] for a in range(4))

        def fold(term, n):
            part = (term[0:8] + term[8:16]) + (term[16:24] + term[24:32])
            acc_ref[n] += part

        px = m
        for a in range(ORDER + 1):
            py = px
            for b in range(ORDER + 1 - a):
                pz = py
                for c in range(ORDER + 1 - a - b):
                    fold(pz, TERM[a, b, c])
                    if c < ORDER - a - b:
                        pz = pz * z
                if b < ORDER - a:
                    py = py * y
            if a < ORDER:
                px = px * x
        return carry

    lax.fori_loop(0, BODIES // 32, chunk, 0)
    mt_ref[TERMS - 5 :, :] = jnp.zeros((ROWS - TERMS + 5, SLOTS), f32)
    for (a, b, c), n in TERM.items():
        mt_ref[n : n + 1, :] = jnp.sum(acc_ref[n], axis=0, keepdims=True) * NORM[a, b, c]
    m_ref[0] = mt_ref[0:128, :].T
    m_ref[1] = jnp.concatenate([mt_ref[128:ROWS, :], jnp.zeros((256 - ROWS, SLOTS), f32)], axis=0).T
    for level in range(LEVELS):

        def row(k, carry):
            slot = slots_ref[level, 0, k]
            for half in range(2):
                rows_ref[half, pl.ds(k, 1), :] = m_ref[half, pl.ds(slot, 1), :]
            return carry

        lax.fori_loop(0, KEXP, row, 0, unroll=8)
        for half in range(2):
            exp_refs[level][:, half * 128 : half * 128 + 128] = rows_ref[half]


def multipoles_of(recv, export_slots):
    vm = pl.BlockSpec(memory_space=VMEM)
    out = pl.pallas_call(
        multipole_kernel,
        out_shape=[
            jax.ShapeDtypeStruct((ROWS, SLOTS), f32),
            jax.ShapeDtypeStruct((4, BODIES, SLOTS), f32),
        ]
        + [jax.ShapeDtypeStruct((KEXP, 256), f32)] * LEVELS,
        in_specs=[vm, pl.BlockSpec(memory_space=SMEM)],
        out_specs=[vm] * (2 + LEVELS),
        scratch_shapes=[
            pltpu.VMEM((TERMS, 8, SLOTS), f32),
            pltpu.VMEM((2, SLOTS, 128), f32),
            pltpu.VMEM((2, KEXP, 128), f32),
        ],
        compiler_params=small(4),
        name="multipoles",
    )(recv, export_slots.transpose(1, 0, 2))
    return out[0], out[1], out[2:]


def near_kernel(post_ref, tgt_ref, src_ref, off_ref, near_ref, s_ref, t_ref, a_ref):
    row = iota((128, 128), 0)
    pick_s = jnp.where(src_ref[...] == row, 1.0, 0.0)
    pick_t = jnp.where(tgt_ref[...] == row, 1.0, 0.0)
    k = off_ref[...].astype(f32)
    one, zero = jnp.ones_like(k), jnp.zeros_like(k)
    kx = jnp.where(k >= 9.0, one, zero) + jnp.where(k >= 18.0, one, zero)
    k = k - 9.0 * kx
    ky = jnp.where(k >= 3.0, one, zero) + jnp.where(k >= 6.0, one, zero)
    kz = k - 3.0 * ky
    for a, shift in enumerate((kx, ky, kz)):
        s_ref[a] = dot_exact(post_ref[a], pick_s) + 2.0 * (shift - 1.0)
        t_ref[a] = dot_exact(post_ref[a], pick_t)
    s_ref[3] = dot_exact(post_ref[3], pick_s)

    def chunk(q, carry):
        rows = pl.ds(pl.multiple_of(q * 32, 32), 32)
        tx, ty, tz = (t_ref[a, rows, :] for a in range(3))

        def source(j, state):
            p, ax, ay, az = state
            sx, sy, sz, m = (s_ref[a, pl.ds(j, 1), :] for a in range(4))
            rx, ry, rz = sx - tx, sy - ty, sz - tz
            inv = lax.rsqrt(rx * rx + ry * ry + rz * rz + SOFT)
            w = m * inv
            p = p - w
            w = w * (inv * inv)
            return p, ax + rx * w, ay + ry * w, az + rz * w

        done = lax.fori_loop(0, 128, source, (jnp.zeros((32, 128), f32),) * 4, unroll=8)
        for a in range(4):
            a_ref[a, rows, :] = done[a]
        return carry

    lax.fori_loop(0, 4, chunk, 0)
    into = pick_t.T
    for a in range(4):
        near_ref[a] = dot_exact(a_ref[a], into)


def near_field(post, target, source, offset):
    vm = pl.BlockSpec(memory_space=VMEM)
    return pl.pallas_call(
        near_kernel,
        out_shape=jax.ShapeDtypeStruct((4, BODIES, SLOTS), f32),
        in_specs=[vm] * 4,
        out_specs=vm,
        scratch_shapes=[VMEM((4, 128, 128), f32), VMEM((3, 128, 128), f32), VMEM((4, 128, 128), f32)],
        compiler_params=small(4),
        cost_estimate=pl.CostEstimate(flops=8 * 10**9, bytes_accessed=10**6, transcendentals=2 * 10**6),
        name="near",
    )(post, target, source, offset)


def field_kernel(counts_ref, left_ref, mt_ref, *rest):
    far_refs, rest = rest[:LEVELS], rest[LEVELS:]
    post_ref, near_ref, out_ref, src_ref, bt_ref, acc_ref, e_ref, f_ref = rest

    far = jnp.concatenate([r[...] for r in far_refs], axis=0)
    far = jnp.concatenate([far, jnp.zeros((32, 256), f32)], axis=0)
    parts = [mt_ref[...]]
    for q in range(2):
        block = far[q * 128 : q * 128 + 128, :]
        parts.append(jnp.concatenate([block[:, 0:128].T, block[:, 128:256].T[0 : ROWS - 128]], axis=0))
    sources = jnp.concatenate(parts, axis=1)
    high = sources.astype(bf16).astype(f32)
    both = jnp.concatenate([high, sources - high], axis=0).astype(bf16)
    src_ref[...] = both[:, 0:SOURCES]

    def move(p, carry):
        moved = dot(src_ref[...], counts_ref[p])
        moved = moved[0:ROWS] + moved[ROWS : 2 * ROWS]
        for k in range(2):
            bt_ref[pl.ds(2 * p + k, ROWS, stride=PITCH), :] = moved[:, k * 128 : k * 128 + 128]
        return carry

    lax.fori_loop(0, CLASSES // 2, move, 0, unroll=16)

    acc_ref[...] = jnp.zeros_like(acc_ref)

    def contract(jb, carry):
        right = [
            jnp.concatenate(split(bt_ref[pl.ds((jb * J_STEP + j) * PITCH, CLASSES), :]), axis=1)
            for j in range(J_STEP)
        ]
        acc_ref[...] += dot(left_ref[jb], jnp.concatenate(right, axis=0))
        return carry

    lax.fori_loop(0, J_BLOCKS, contract, 0, unroll=21)
    acc = acc_ref[...]
    e = (acc[I_ROWS:, 128:] + acc[I_ROWS:, :128]) + acc[:I_ROWS, 128:] + acc[:I_ROWS, :128]
    e_ref[...] = e[0:ROWS]

    present = jnp.where(post_ref[3, 0:1, :] > 0.0, 1.0, 0.0)

    def chunk(q, carry):
        rows = pl.ds(pl.multiple_of(q * 32, 32), 32)
        x, y, z = (post_ref[a, rows, :] for a in range(3))

        def coef(a, b, c):
            n = TERM[a, b, c]
            return jnp.broadcast_to(e_ref[n : n + 1, :] * NORM[a, b, c], (32, SLOTS))

        p = px = py = pz = None
        for a in range(ORDER, -1, -1):
            r = ry = rz = None
            for b in range(ORDER - a, -1, -1):
                top = ORDER - a - b
                v = coef(a, b, top)
                vz = None
                for c in range(top - 1, -1, -1):
                    vz = v if vz is None else vz * z + v
                    v = v * z + coef(a, b, c)
                if r is None:
                    r = v
                else:
                    ry = r if ry is None else ry * y + r
                    r = r * y + v
                    if vz is not None:
                        rz = vz if rz is None else rz * y + vz
            if p is None:
                p = r
            else:
                px = p if px is None else px * x + p
                p = p * x + r
                py = ry if py is None else py * x + ry
                pz = rz if pz is None else pz * x + rz
        for a, v in enumerate((p, -px, -py, -pz)):
            f_ref[a, rows, :] = (v + near_ref[a, rows, :]) * present
        return carry

    lax.fori_loop(0, BODIES // 32, chunk, 0)
    for a in range(4):
        out_ref[:, a, :] = f_ref[a].T


def field(counts, left, mt, far, post, near):
    vm = pl.BlockSpec(memory_space=VMEM)
    return pl.pallas_call(
        field_kernel,
        out_shape=jax.ShapeDtypeStruct((SLOTS, 4, BODIES), f32),
        in_specs=[vm] * (5 + LEVELS),
        out_specs=vm,
        scratch_shapes=[
            VMEM((2 * ROWS, SOURCES), bf16),
            VMEM((ROWS * PITCH, SLOTS), f32),
            VMEM((2 * I_ROWS, 256), f32),
            VMEM((ROWS, SLOTS), f32),
            VMEM((4, BODIES, SLOTS), f32),
        ],
        compiler_params=small(20),
        cost_estimate=pl.CostEstimate(flops=40 * 10**9, bytes_accessed=26 * 10**6, transcendentals=0),
        name="field",
    )(counts, left, mt, *far, post, near)


def body(
    positions,
    masses,
    owner,
    operators,
    m2l_target,
    far_source,
    local_source,
    export_slots,
    near_target,
    near_source,
    near_offset,
):
    axes = ("dom", "sub")
    devices = lax.axis_size(axes)
    sent = pack_tiles(owner, positions, masses)
    recv = lax.all_to_all(sent, "sub", split_axis=0, concat_axis=0, tiled=True)
    counts, left = prepare(m2l_target[0], far_source[0], local_source[0], operators)
    mt, post, exported = multipoles_of(recv, export_slots)
    far = [
        lax.ppermute(rows, axes, [(i, i ^ (1 << level)) for i in range(devices)])
        for level, rows in enumerate(exported)
    ]
    near = near_field(post, near_target, near_source, near_offset)
    return field(counts, left, mt, far, post, near)


def solution(mesh):
    both = ("dom", "sub")
    in_specs = (
        P(both, None, None),
        P(both, None),
        P(both, None),
        P(),
        P(both, None, None, None),
        P(both, None, None, None),
        P(both, None, None),
        P(both, None, None),
        P(both, None),
        P(both, None),
        P(both, None),
    )
    out_specs = P(both, None, None)
    return jax.shard_map(body, mesh=mesh, in_specs=in_specs, out_specs=out_specs, check_vma=False)
```

```python
import functools

import jax
import jax.numpy as jnp
import numpy as np
from jax import lax
from jax.experimental import pallas as pl
from jax.experimental.pallas import tpu as pltpu
from jax.sharding import PartitionSpec as P

ORDER = 8
TERMS = 165
ROWS = 168
TERMS_PAD = ROWS
SOFT = 0.01
SLOTS = 128
BODIES = 128
KEXP = 32
LEVELS = 7
CLASSES = 128
SOURCES = SLOTS + LEVELS * KEXP
f32 = jnp.float32
bf16 = jnp.bfloat16
VMEM = pltpu.VMEM
SMEM = pltpu.SMEM


def term_list():
    triples = []
    for degree in range(ORDER + 1):
        for a in range(degree, -1, -1):
            for b in range(degree - a, -1, -1):
                triples.append((a, b, degree - a - b))
    return {t: n for n, t in enumerate(triples)}


TERM = term_list()
NORM = {t: float(np.float32(np.sqrt(np.prod(2.0 * np.array(t) + 1.0)))) for t in TERM}


def small(mib):
    return pltpu.CompilerParams(vmem_limit_bytes=mib * 2**20)


def in_hbm(x):
    return pltpu.with_memory_space_constraint(x, pltpu.HBM)


def iota(shape, axis):
    return lax.broadcasted_iota(jnp.int32, shape, axis)


def split(v):
    high = v.astype(bf16)
    return high, (v - high.astype(f32)).astype(bf16)


def dot(a, b):
    return jnp.dot(a, b, preferred_element_type=f32)


def dot_nt(a, b):
    return lax.dot_general(a, b, (((1,), (1,)), ((), ())), preferred_element_type=f32)


def dot_exact(a, b):
    return jnp.dot(a, b, preferred_element_type=f32, precision=lax.Precision.HIGHEST)


def pack_kernel(owner_hbm, pos_hbm, mass_hbm, out_ref, owner_ref, pos_ref, mass_ref, sem, count_ref, *slot_refs):
    copies = [
        pltpu.make_async_copy(a, b, sem.at[k])
        for k, (a, b) in enumerate(((owner_hbm, owner_ref), (pos_hbm, pos_ref), (mass_hbm, mass_ref)))
    ]
    for c in copies:
        c.start()
    for r in slot_refs:
        r[...] = jnp.zeros_like(r)
    for o in range(8):
        count_ref[o] = 0
    for c in copies:
        c.wait()

    def step(i, carry):
        o = owner_ref[0, i]
        rank = count_ref[o]
        count_ref[o] = rank + 1
        slot = o * 16 + rank
        for a in range(3):
            slot_refs[a][pl.ds(slot, 1), :] = pos_ref[a, pl.ds(i, 1), :]
        slot_refs[3][pl.ds(slot, 1), :] = mass_ref[pl.ds(i, 1), :]
        return carry

    lax.fori_loop(0, mass_ref.shape[0], step, 0)
    for a in range(4):
        out_ref[:, a * BODIES : (a + 1) * BODIES] = slot_refs[a][...]


def pack_tiles(owner, positions, masses):
    return pl.pallas_call(
        pack_kernel,
        out_shape=pltpu.HBM((SLOTS, 4 * BODIES), f32),
        in_specs=[pl.BlockSpec(memory_space=pltpu.HBM)] * 3,
        out_specs=pl.BlockSpec(memory_space=VMEM),
        scratch_shapes=[
            pltpu.SMEM((1, owner.shape[0]), jnp.int32),
            VMEM((3, owner.shape[0], BODIES), f32),
            VMEM((owner.shape[0], BODIES), f32),
            pltpu.SemaphoreType.DMA((3,)),
            pltpu.SMEM((8,), jnp.int32),
        ]
        + [VMEM((SLOTS, BODIES), f32)] * 4,
        compiler_params=small(2),
        name="pack",
    )(*map(in_hbm, (owner.T, positions.transpose(1, 0, 2), masses)))


I_STEP = 16
I_FULL = TERMS // I_STEP
PAIR_STEP = 16
GROUPS = CLASSES // 2 // PAIR_STEP
I_ROWS = (I_FULL + 1) * I_STEP
J_STEP = 8
PITCH = CLASSES + 1
J_BLOCKS = ROWS // J_STEP


def prepare_kernel(
    tgt_hbm, far_hbm, local_hbm, op_hbm, counts_hbm, left_hbm, done_ref,
    tgt_ref, far_ref, local_ref, tt_ref, st_ref, buf_ref, counts_ref, left_ref, in_sem, sem, counts_sem, left_sem,
):
    lists = [
        pltpu.make_async_copy(a, b, in_sem.at[k])
        for k, (a, b) in enumerate(((tgt_hbm, tgt_ref), (far_hbm, far_ref), (local_hbm, local_ref)))
    ]
    for c in lists:
        c.start()

    def copy(q, size):
        return pltpu.make_async_copy(
            op_hbm.at[pl.ds(q * I_STEP, size)], buf_ref.at[q, pl.ds(0, size), pl.ds(0, TERMS)], sem.at[q]
        )

    def counts_out(g):
        pairs = pl.ds(g * PAIR_STEP, PAIR_STEP)
        return pltpu.make_async_copy(counts_ref.at[pairs], counts_hbm.at[pairs], counts_sem.at[g])

    def left_out(q, part):
        rows = pl.ds(pl.multiple_of(part * I_ROWS + q * I_STEP, I_STEP), I_STEP)
        return pltpu.make_async_copy(left_ref.at[:, rows], left_hbm.at[:, rows], left_sem.at[part, q])

    for q in range(I_FULL):
        copy(q, I_STEP).start()
    copy(I_FULL, TERMS - I_FULL * I_STEP).start()
    for c in lists:
        c.wait()

    order = [7, 0, 1, 2, 3, 4, 5, 6]
    for pair in range(4):
        tgt, src = [], []
        for level in order[2 * pair : 2 * pair + 2]:
            tgt.append(tgt_ref[level].astype(f32))
            if level == 7:
                src.append(local_ref[...].astype(f32))
            else:
                offset = {0: SLOTS, 1: 0, 2: KEXP, 3: 0, 4: KEXP, 5: 0, 6: KEXP}[level]
                src.append((far_ref[level] + offset).astype(f32))
        tt_ref[pair] = jnp.concatenate(tgt, axis=0).T
        st_ref[pair] = jnp.concatenate(src, axis=0).T

    ids = iota((160, 128), 0).astype(f32).astype(bf16)

    def onehot(ref, part, c, first, size, total):
        row = jnp.broadcast_to(ref[part, pl.ds(c, 1), :].astype(bf16), (size, 128))
        hits = jnp.where(row == ids[0:size], jnp.ones((), bf16), jnp.zeros((), bf16))
        zeros = lambda n: [jnp.zeros((n, 128), bf16)] if n else []
        return jnp.concatenate(zeros(first) + [hits] + zeros(total - first - size), axis=0)

    def classes(p):
        for k in range(2):
            c = 2 * p + k
            for half, (first, size) in enumerate(((0, 224), (224, 128))):
                cut = 160 if half == 0 else 64
                target = jnp.concatenate([onehot(tt_ref, 2 * half + i, c, 0, 128, 128) for i in range(2)], axis=1)
                source = jnp.concatenate(
                    [
                        onehot(st_ref, 2 * half, c, 0, cut, size),
                        onehot(st_ref, 2 * half + 1, c, cut, size - cut, size),
                    ],
                    axis=1,
                )
                counts = dot_nt(source, target)
                counts_ref[p, first : first + size, k * 128 : k * 128 + 128] = counts.astype(bf16)

    def group(g, carry):
        for i in range(PAIR_STEP):
            classes(g * PAIR_STEP + i)
        counts_out(g).start()
        return carry

    lax.fori_loop(0, GROUPS - 1, group, 0)

    for j in range(TERMS, ROWS):
        left_ref[J_BLOCKS - 1, :, (j % J_STEP) * 128 : (j % J_STEP) * 128 + 128] = jnp.zeros((2 * I_ROWS, 128), bf16)

    def relay(q):
        rows = buf_ref.at[q].reshape(I_STEP * TERMS_PAD, CLASSES)
        at = pl.multiple_of(q * I_STEP, I_STEP)
        for j in range(TERMS):
            v = rows[pl.ds(j, I_STEP, stride=TERMS_PAD), :]
            high, low = split(v)
            lanes = slice((j % J_STEP) * 128, (j % J_STEP) * 128 + 128)
            left_ref[j // J_STEP, pl.ds(at, I_STEP), lanes] = high
            left_ref[j // J_STEP, pl.ds(at + I_ROWS, I_STEP), lanes] = low

    def chunk(q, carry):
        copy(q, I_STEP).wait()
        relay(q)
        for part in range(2):
            left_out(q, part).start()
        return carry

    lax.fori_loop(0, I_FULL, chunk, 0)
    copy(I_FULL, TERMS - I_FULL * I_STEP).wait()
    relay(I_FULL)
    for part in range(2):
        left_out(I_FULL, part).start()
    group(GROUPS - 1, 0)
    done_ref[...] = jnp.zeros_like(done_ref)
    for g in range(GROUPS):
        counts_out(g).wait()
    for part in range(2):
        for q in range(I_FULL + 1):
            left_out(q, part).wait()


def prepare(m2l_target, far_source, local_source, operators):
    hbm = pl.BlockSpec(memory_space=pltpu.HBM)
    counts, left = (CLASSES // 2, SOURCES, 256), (J_BLOCKS, 2 * I_ROWS, J_STEP * CLASSES)
    return pl.pallas_call(
        prepare_kernel,
        out_shape=[pltpu.HBM(counts, bf16), pltpu.HBM(left, bf16), jax.ShapeDtypeStruct((8, 128), f32)],
        in_specs=[hbm] * 4,
        out_specs=[hbm, hbm, pl.BlockSpec(memory_space=VMEM)],
        scratch_shapes=[
            VMEM(m2l_target.shape, jnp.int32),
            VMEM(far_source.shape, jnp.int32),
            VMEM(local_source.shape, jnp.int32),
            VMEM((4, 128, 128), f32),
            VMEM((4, 128, 128), f32),
            VMEM((I_FULL + 1, I_STEP, TERMS_PAD, CLASSES), f32),
            VMEM(counts, bf16),
            VMEM(left, bf16),
            pltpu.SemaphoreType.DMA((3,)),
            pltpu.SemaphoreType.DMA((I_FULL + 1,)),
            pltpu.SemaphoreType.DMA((GROUPS,)),
            pltpu.SemaphoreType.DMA((2, I_FULL + 1)),
        ],
        compiler_params=small(48),
        cost_estimate=pl.CostEstimate(flops=12 * 10**9, bytes_accessed=40 * 10**6, transcendentals=0),
        name="prepare",
    )(*map(in_hbm, (m2l_target, far_source, local_source, operators)))


def multipole_kernel(recv_ref, slots_hbm, done_ref, mt_ref, post_ref, *rest):
    exp_refs, (acc_ref, m_ref, rows_ref, slots_ref, sem) = rest[:LEVELS], rest[LEVELS:]
    slots_copy = pltpu.make_async_copy(slots_hbm, slots_ref, sem)
    slots_copy.start()
    for a in range(4):
        post_ref[a] = recv_ref[:, a * BODIES : (a + 1) * BODIES].T

    acc_ref[...] = jnp.zeros_like(acc_ref)

    def chunk(q, carry):
        rows = pl.ds(pl.multiple_of(q * 32, 32), 32)
        x, y, z, m = (post_ref[a, rows, :] for a in range(4))

        def fold(term, n):
            part = (term[0:8] + term[8:16]) + (term[16:24] + term[24:32])
            acc_ref[n] += part

        px = m
        for a in range(ORDER + 1):
            py = px
            for b in range(ORDER + 1 - a):
                pz = py
                for c in range(ORDER + 1 - a - b):
                    fold(pz, TERM[a, b, c])
                    if c < ORDER - a - b:
                        pz = pz * z
                if b < ORDER - a:
                    py = py * y
            if a < ORDER:
                px = px * x
        return carry

    lax.fori_loop(0, BODIES // 32, chunk, 0)
    mt_ref[TERMS - 5 :, :] = jnp.zeros((ROWS - TERMS + 5, SLOTS), f32)
    for (a, b, c), n in TERM.items():
        mt_ref[n : n + 1, :] = jnp.sum(acc_ref[n], axis=0, keepdims=True) * NORM[a, b, c]
    m_ref[0] = mt_ref[0:128, :].T
    m_ref[1] = jnp.concatenate([mt_ref[128:ROWS, :], jnp.zeros((256 - ROWS, SLOTS), f32)], axis=0).T
    slots_copy.wait()
    for level in range(LEVELS):

        def row(k, carry):
            slot = slots_ref[level, 0, k]
            for half in range(2):
                rows_ref[half, pl.ds(k, 1), :] = m_ref[half, pl.ds(slot, 1), :]
            return carry

        lax.fori_loop(0, KEXP, row, 0, unroll=8)
        for half in range(2):
            exp_refs[level][:, half * 128 : half * 128 + 128] = rows_ref[half]


def multipoles_of(recv, export_slots, after):
    vm = pl.BlockSpec(memory_space=VMEM)
    out = pl.pallas_call(
        multipole_kernel,
        out_shape=[
            jax.ShapeDtypeStruct((ROWS, SLOTS), f32),
            jax.ShapeDtypeStruct((4, BODIES, SLOTS), f32),
        ]
        + [jax.ShapeDtypeStruct((KEXP, 256), f32)] * LEVELS,
        in_specs=[vm, pl.BlockSpec(memory_space=pltpu.HBM), vm],
        out_specs=[vm] * (2 + LEVELS),
        scratch_shapes=[
            pltpu.VMEM((TERMS, 8, SLOTS), f32),
            pltpu.VMEM((2, SLOTS, 128), f32),
            pltpu.VMEM((2, KEXP, 128), f32),
            pltpu.SMEM((LEVELS, 1, KEXP), jnp.int32),
            pltpu.SemaphoreType.DMA,
        ],
        compiler_params=small(4),
        name="multipoles",
    )(recv, in_hbm(export_slots.transpose(1, 0, 2)), after)
    return out[0], out[1], out[2:]


def near_kernel(post_ref, tgt_ref, src_ref, off_ref, near_ref, s_ref, t_ref, a_ref):
    row = iota((128, 128), 0)
    pick_s = jnp.where(src_ref[...] == row, 1.0, 0.0)
    pick_t = jnp.where(tgt_ref[...] == row, 1.0, 0.0)
    k = off_ref[...].astype(f32)
    one, zero = jnp.ones_like(k), jnp.zeros_like(k)
    kx = jnp.where(k >= 9.0, one, zero) + jnp.where(k >= 18.0, one, zero)
    k = k - 9.0 * kx
    ky = jnp.where(k >= 3.0, one, zero) + jnp.where(k >= 6.0, one, zero)
    kz = k - 3.0 * ky
    for a, shift in enumerate((kx, ky, kz)):
        s_ref[a] = dot_exact(post_ref[a], pick_s) + 2.0 * (shift - 1.0)
        t_ref[a] = dot_exact(post_ref[a], pick_t)
    s_ref[3] = dot_exact(post_ref[3], pick_s)

    def chunk(q, carry):
        rows = pl.ds(pl.multiple_of(q * 32, 32), 32)
        tx, ty, tz = (t_ref[a, rows, :] for a in range(3))

        def source(j, state):
            p, ax, ay, az = state
            sx, sy, sz, m = (s_ref[a, pl.ds(j, 1), :] for a in range(4))
            rx, ry, rz = sx - tx, sy - ty, sz - tz
            inv = lax.rsqrt(rx * rx + ry * ry + rz * rz + SOFT)
            w = m * inv
            p = p - w
            w = w * (inv * inv)
            return p, ax + rx * w, ay + ry * w, az + rz * w

        done = lax.fori_loop(0, 128, source, (jnp.zeros((32, 128), f32),) * 4, unroll=8)
        for a in range(4):
            a_ref[a, rows, :] = done[a]
        return carry

    lax.fori_loop(0, 4, chunk, 0)
    into = pick_t.T
    for a in range(4):
        near_ref[a] = dot_exact(a_ref[a], into)


def near_field(post, target, source, offset):
    vm = pl.BlockSpec(memory_space=VMEM)
    return pl.pallas_call(
        near_kernel,
        out_shape=jax.ShapeDtypeStruct((4, BODIES, SLOTS), f32),
        in_specs=[vm] * 4,
        out_specs=vm,
        scratch_shapes=[VMEM((4, 128, 128), f32), VMEM((3, 128, 128), f32), VMEM((4, 128, 128), f32)],
        compiler_params=small(4),
        cost_estimate=pl.CostEstimate(flops=8 * 10**9, bytes_accessed=10**6, transcendentals=2 * 10**6),
        name="near",
    )(post, target, source, offset)


def field_kernel(counts_ref, left_ref, mt_ref, *rest):
    far_refs, rest = rest[:LEVELS], rest[LEVELS:]
    post_ref, near_ref, out_ref, src_ref, bt_ref, acc_ref, e_ref, f_ref = rest

    far = jnp.concatenate([r[...] for r in far_refs], axis=0)
    far = jnp.concatenate([far, jnp.zeros((32, 256), f32)], axis=0)
    parts = [mt_ref[...]]
    for q in range(2):
        block = far[q * 128 : q * 128 + 128, :]
        parts.append(jnp.concatenate([block[:, 0:128].T, block[:, 128:256].T[0 : ROWS - 128]], axis=0))
    sources = jnp.concatenate(parts, axis=1)
    high = sources.astype(bf16).astype(f32)
    both = jnp.concatenate([high, sources - high], axis=0).astype(bf16)
    src_ref[...] = both[:, 0:SOURCES]

    def move(p, carry):
        moved = dot(src_ref[...], counts_ref[p])
        moved = moved[0:ROWS] + moved[ROWS : 2 * ROWS]
        for k in range(2):
            bt_ref[pl.ds(2 * p + k, ROWS, stride=PITCH), :] = moved[:, k * 128 : k * 128 + 128]
        return carry

    lax.fori_loop(0, CLASSES // 2, move, 0, unroll=16)

    acc_ref[...] = jnp.zeros_like(acc_ref)

    def contract(jb, carry):
        right = [
            jnp.concatenate(split(bt_ref[pl.ds((jb * J_STEP + j) * PITCH, CLASSES), :]), axis=1)
            for j in range(J_STEP)
        ]
        acc_ref[...] += dot(left_ref[jb], jnp.concatenate(right, axis=0))
        return carry

    lax.fori_loop(0, J_BLOCKS, contract, 0, unroll=21)
    acc = acc_ref[...]
    e = (acc[I_ROWS:, 128:] + acc[I_ROWS:, :128]) + acc[:I_ROWS, 128:] + acc[:I_ROWS, :128]
    e_ref[...] = e[0:ROWS]

    present = jnp.where(post_ref[3, 0:1, :] > 0.0, 1.0, 0.0)

    def chunk(q, carry):
        rows = pl.ds(pl.multiple_of(q * 32, 32), 32)
        x, y, z = (post_ref[a, rows, :] for a in range(3))

        def coef(a, b, c):
            n = TERM[a, b, c]
            return jnp.broadcast_to(e_ref[n : n + 1, :] * NORM[a, b, c], (32, SLOTS))

        p = px = py = pz = None
        for a in range(ORDER, -1, -1):
            r = ry = rz = None
            for b in range(ORDER - a, -1, -1):
                top = ORDER - a - b
                v = coef(a, b, top)
                vz = None
                for c in range(top - 1, -1, -1):
                    vz = v if vz is None else vz * z + v
                    v = v * z + coef(a, b, c)
                if r is None:
                    r = v
                else:
                    ry = r if ry is None else ry * y + r
                    r = r * y + v
                    if vz is not None:
                        rz = vz if rz is None else rz * y + vz
            if p is None:
                p = r
            else:
                px = p if px is None else px * x + p
                p = p * x + r
                py = ry if py is None else py * x + ry
                pz = rz if pz is None else pz * x + rz
        for a, v in enumerate((p, -px, -py, -pz)):
            f_ref[a, rows, :] = (v + near_ref[a, rows, :]) * present
        return carry

    lax.fori_loop(0, BODIES // 32, chunk, 0)
    for a in range(4):
        out_ref[:, a, :] = f_ref[a].T


def field(counts, left, mt, far, post, near):
    vm = pl.BlockSpec(memory_space=VMEM)
    return pl.pallas_call(
        field_kernel,
        out_shape=jax.ShapeDtypeStruct((SLOTS, 4, BODIES), f32),
        in_specs=[vm] * (5 + LEVELS),
        out_specs=vm,
        scratch_shapes=[
            VMEM((2 * ROWS, SOURCES), bf16),
            VMEM((ROWS * PITCH, SLOTS), f32),
            VMEM((2 * I_ROWS, 256), f32),
            VMEM((ROWS, SLOTS), f32),
            VMEM((4, BODIES, SLOTS), f32),
        ],
        compiler_params=small(20),
        cost_estimate=pl.CostEstimate(flops=40 * 10**9, bytes_accessed=26 * 10**6, transcendentals=0),
        name="field",
    )(counts, left, mt, *far, post, near)


def body(
    positions,
    masses,
    owner,
    operators,
    m2l_target,
    far_source,
    local_source,
    export_slots,
    near_target,
    near_source,
    near_offset,
):
    axes = ("dom", "sub")
    devices = lax.axis_size(axes)
    sent = pack_tiles(owner, positions, masses)
    recv = lax.all_to_all(sent, "sub", split_axis=0, concat_axis=0, tiled=True)
    counts, left, done = prepare(m2l_target[0], far_source[0], local_source[0], operators)
    mt, post, exported = multipoles_of(recv, export_slots, done)
    far = [
        lax.ppermute(rows, axes, [(i, i ^ (1 << level)) for i in range(devices)])
        for level, rows in enumerate(exported)
    ]
    near = near_field(post, near_target, near_source, near_offset)
    return field(counts, left, mt, far, post, near)


def solution(mesh):
    both = ("dom", "sub")
    in_specs = (
        P(both, None, None),
        P(both, None),
        P(both, None),
        P(),
        P(both, None, None, None),
        P(both, None, None, None),
        P(both, None, None),
        P(both, None, None),
        P(both, None),
        P(both, None),
        P(both, None),
    )
    out_specs = P(both, None, None)
    return jax.shard_map(body, mesh=mesh, in_specs=in_specs, out_specs=out_specs, check_vma=False)
```

```python
import functools

import jax
import jax.numpy as jnp
import numpy as np
from jax import lax
from jax.experimental import pallas as pl
from jax.experimental.pallas import tpu as pltpu
from jax.sharding import PartitionSpec as P

ORDER = 8
TERMS = 165
ROWS = 168
TERMS_PAD = ROWS
SOFT = 0.01
SLOTS = 128
PEERS = 8
CAP = SLOTS // PEERS
BODIES = 128
KEXP = 32
LEVELS = 7
CLASSES = 128
SOURCES = SLOTS + LEVELS * KEXP
f32 = jnp.float32
bf16 = jnp.bfloat16
VMEM = pltpu.VMEM
SMEM = pltpu.SMEM


def term_list():
    triples = []
    for degree in range(ORDER + 1):
        for a in range(degree, -1, -1):
            for b in range(degree - a, -1, -1):
                triples.append((a, b, degree - a - b))
    return {t: n for n, t in enumerate(triples)}


TERM = term_list()
NORM = {t: float(np.float32(np.sqrt(np.prod(2.0 * np.array(t) + 1.0)))) for t in TERM}


def small(mib):
    return pltpu.CompilerParams(vmem_limit_bytes=mib * 2**20)


def in_hbm(x):
    return pltpu.with_memory_space_constraint(x, pltpu.HBM)


def iota(shape, axis):
    return lax.broadcasted_iota(jnp.int32, shape, axis)


def split(v):
    high = v.astype(bf16)
    return high, (v - high.astype(f32)).astype(bf16)


def dot(a, b):
    return jnp.dot(a, b, preferred_element_type=f32)


def dot_nt(a, b):
    return lax.dot_general(a, b, (((1,), (1,)), ((), ())), preferred_element_type=f32)


def dot_exact(a, b):
    return jnp.dot(a, b, preferred_element_type=f32, precision=lax.Precision.HIGHEST)


def pack_kernel(owner_hbm, pos_hbm, mass_hbm, *rest):
    out_refs, (owner_ref, pos_ref, mass_ref, sem, count_ref), slot_refs = rest[:PEERS], rest[PEERS:-4], rest[-4:]
    copies = [
        pltpu.make_async_copy(a, b, sem.at[k])
        for k, (a, b) in enumerate(((owner_hbm, owner_ref), (pos_hbm, pos_ref), (mass_hbm, mass_ref)))
    ]
    for c in copies:
        c.start()
    for r in slot_refs:
        r[...] = jnp.zeros_like(r)
    for o in range(PEERS):
        count_ref[o] = 0
    me = lax.axis_index("sub")
    for c in copies:
        c.wait()

    def step(i, carry):
        o = owner_ref[0, i]
        rank = count_ref[o]
        count_ref[o] = rank + 1
        slot = (o ^ me) * CAP + rank
        for a in range(3):
            slot_refs[a][pl.ds(slot, 1), :] = pos_ref[a, pl.ds(i, 1), :]
        slot_refs[3][pl.ds(slot, 1), :] = mass_ref[pl.ds(i, 1), :]
        return carry

    lax.fori_loop(0, mass_ref.shape[0], step, 0)
    for k in range(PEERS):
        for a in range(4):
            out_refs[k][:, a * BODIES : (a + 1) * BODIES] = slot_refs[a][k * CAP : (k + 1) * CAP, :]


def pack_tiles(owner, positions, masses):
    return pl.pallas_call(
        pack_kernel,
        out_shape=[jax.ShapeDtypeStruct((CAP, 4 * BODIES), f32)] * PEERS,
        in_specs=[pl.BlockSpec(memory_space=pltpu.HBM)] * 3,
        out_specs=[pl.BlockSpec(memory_space=VMEM)] * PEERS,
        scratch_shapes=[
            pltpu.SMEM((1, owner.shape[0]), jnp.int32),
            VMEM((3, owner.shape[0], BODIES), f32),
            VMEM((owner.shape[0], BODIES), f32),
            pltpu.SemaphoreType.DMA((3,)),
            pltpu.SMEM((PEERS,), jnp.int32),
        ]
        + [VMEM((SLOTS, BODIES), f32)] * 4,
        compiler_params=small(2),
        name="pack",
    )(*map(in_hbm, (owner.T, positions.transpose(1, 0, 2), masses)))


I_STEP = 16
I_FULL = TERMS // I_STEP
PAIR_STEP = 16
I_ROWS = (I_FULL + 1) * I_STEP
J_STEP = 8
PITCH = CLASSES + 1
J_BLOCKS = ROWS // J_STEP


def prepare_kernel(
    tgt_hbm, far_hbm, local_hbm, op_hbm, counts_ref, left_ref, done_ref,
    tgt_ref, far_ref, local_ref, tt_ref, st_ref, buf_ref, in_sem, sem,
):
    lists = [
        pltpu.make_async_copy(a, b, in_sem.at[k])
        for k, (a, b) in enumerate(((tgt_hbm, tgt_ref), (far_hbm, far_ref), (local_hbm, local_ref)))
    ]
    for c in lists:
        c.start()

    def copy(q, size):
        return pltpu.make_async_copy(
            op_hbm.at[pl.ds(q * I_STEP, size)], buf_ref.at[q, pl.ds(0, size), pl.ds(0, TERMS)], sem.at[q]
        )

    for q in range(I_FULL):
        copy(q, I_STEP).start()
    copy(I_FULL, TERMS - I_FULL * I_STEP).start()
    for c in lists:
        c.wait()

    order = [7, 0, 1, 2, 3, 4, 5, 6]
    for pair in range(4):
        tgt, src = [], []
        for level in order[2 * pair : 2 * pair + 2]:
            tgt.append(tgt_ref[level].astype(f32))
            if level == 7:
                src.append(local_ref[...].astype(f32))
            else:
                offset = {0: SLOTS, 1: 0, 2: KEXP, 3: 0, 4: KEXP, 5: 0, 6: KEXP}[level]
                src.append((far_ref[level] + offset).astype(f32))
        tt_ref[pair] = jnp.concatenate(tgt, axis=0).T
        st_ref[pair] = jnp.concatenate(src, axis=0).T

    ids = iota((160, 128), 0).astype(f32).astype(bf16)

    def onehot(ref, part, c, first, size, total):
        row = jnp.broadcast_to(ref[part, pl.ds(c, 1), :].astype(bf16), (size, 128))
        hits = jnp.where(row == ids[0:size], jnp.ones((), bf16), jnp.zeros((), bf16))
        zeros = lambda n: [jnp.zeros((n, 128), bf16)] if n else []
        return jnp.concatenate(zeros(first) + [hits] + zeros(total - first - size), axis=0)

    def classes(p):
        for k in range(2):
            c = 2 * p + k
            for half, (first, size) in enumerate(((0, 224), (224, 128))):
                cut = 160 if half == 0 else 64
                target = jnp.concatenate([onehot(tt_ref, 2 * half + i, c, 0, 128, 128) for i in range(2)], axis=1)
                source = jnp.concatenate(
                    [
                        onehot(st_ref, 2 * half, c, 0, cut, size),
                        onehot(st_ref, 2 * half + 1, c, cut, size - cut, size),
                    ],
                    axis=1,
                )
                counts = dot_nt(source, target)
                counts_ref[p, first : first + size, k * 128 : k * 128 + 128] = counts.astype(bf16)

    def group(g, carry):
        for i in range(PAIR_STEP):
            classes(g * PAIR_STEP + i)
        return carry

    lax.fori_loop(0, CLASSES // 2 // PAIR_STEP, group, 0)
    for j in range(TERMS, ROWS):
        left_ref[J_BLOCKS - 1, :, (j % J_STEP) * 128 : (j % J_STEP) * 128 + 128] = jnp.zeros((2 * I_ROWS, 128), bf16)

    def relay(q):
        rows = buf_ref.at[q].reshape(I_STEP * TERMS_PAD, CLASSES)
        at = pl.multiple_of(q * I_STEP, I_STEP)
        for j in range(TERMS):
            v = rows[pl.ds(j, I_STEP, stride=TERMS_PAD), :]
            high, low = split(v)
            lanes = slice((j % J_STEP) * 128, (j % J_STEP) * 128 + 128)
            left_ref[j // J_STEP, pl.ds(at, I_STEP), lanes] = high
            left_ref[j // J_STEP, pl.ds(at + I_ROWS, I_STEP), lanes] = low

    def chunk(q, carry):
        copy(q, I_STEP).wait()
        relay(q)
        return carry

    lax.fori_loop(0, I_FULL, chunk, 0)
    copy(I_FULL, TERMS - I_FULL * I_STEP).wait()
    relay(I_FULL)
    done_ref[...] = jnp.zeros_like(done_ref)


def prepare(m2l_target, far_source, local_source, operators):
    hbm = pl.BlockSpec(memory_space=pltpu.HBM)
    counts, left = (CLASSES // 2, SOURCES, 256), (J_BLOCKS, 2 * I_ROWS, J_STEP * CLASSES)
    return pl.pallas_call(
        prepare_kernel,
        out_shape=[VMEM(counts, bf16), VMEM(left, bf16), VMEM((8, 128), f32)],
        in_specs=[hbm] * 4,
        out_specs=[pl.BlockSpec(memory_space=VMEM)] * 3,
        scratch_shapes=[
            VMEM(m2l_target.shape, jnp.int32),
            VMEM(far_source.shape, jnp.int32),
            VMEM(local_source.shape, jnp.int32),
            VMEM((4, 128, 128), f32),
            VMEM((4, 128, 128), f32),
            VMEM((I_FULL + 1, I_STEP, TERMS_PAD, CLASSES), f32),
            pltpu.SemaphoreType.DMA((3,)),
            pltpu.SemaphoreType.DMA((I_FULL + 1,)),
        ],
        compiler_params=small(20),
        cost_estimate=pl.CostEstimate(flops=12 * 10**9, bytes_accessed=14 * 10**6, transcendentals=0),
        name="prepare",
    )(*map(in_hbm, (m2l_target, far_source, local_source, operators)))


def multipole_kernel(*refs):
    pieces, refs = refs[:PEERS], refs[PEERS:]
    slots_hbm, _, mt_ref, post_ref, *refs = refs
    exp_refs, (acc_ref, m_ref, rows_ref, slots_ref, sem, recv_ref) = refs[:LEVELS], refs[LEVELS:]
    slots_copy = pltpu.make_async_copy(slots_hbm, slots_ref, sem)
    slots_copy.start()
    me = lax.axis_index("sub")
    for k in range(PEERS):
        rows = pl.ds(pl.multiple_of((me ^ k) * CAP, CAP), CAP)
        for a in range(4):
            recv_ref[a, rows, :] = pieces[k][:, a * BODIES : (a + 1) * BODIES]
    for a in range(4):
        post_ref[a] = recv_ref[a].T

    acc_ref[...] = jnp.zeros_like(acc_ref)

    def chunk(q, carry):
        rows = pl.ds(pl.multiple_of(q * 32, 32), 32)
        x, y, z, m = (post_ref[a, rows, :] for a in range(4))

        def fold(term, n):
            part = (term[0:8] + term[8:16]) + (term[16:24] + term[24:32])
            acc_ref[n] += part

        px = m
        for a in range(ORDER + 1):
            py = px
            for b in range(ORDER + 1 - a):
                pz = py
                for c in range(ORDER + 1 - a - b):
                    fold(pz, TERM[a, b, c])
                    if c < ORDER - a - b:
                        pz = pz * z
                if b < ORDER - a:
                    py = py * y
            if a < ORDER:
                px = px * x
        return carry

    lax.fori_loop(0, BODIES // 32, chunk, 0)
    mt_ref[TERMS - 5 :, :] = jnp.zeros((ROWS - TERMS + 5, SLOTS), f32)
    for (a, b, c), n in TERM.items():
        mt_ref[n : n + 1, :] = jnp.sum(acc_ref[n], axis=0, keepdims=True) * NORM[a, b, c]
    m_ref[0] = mt_ref[0:128, :].T
    m_ref[1] = jnp.concatenate([mt_ref[128:ROWS, :], jnp.zeros((256 - ROWS, SLOTS), f32)], axis=0).T
    slots_copy.wait()
    for level in range(LEVELS):

        def row(k, carry):
            slot = slots_ref[level, 0, k]
            for half in range(2):
                rows_ref[half, pl.ds(k, 1), :] = m_ref[half, pl.ds(slot, 1), :]
            return carry

        lax.fori_loop(0, KEXP, row, 0, unroll=8)
        for half in range(2):
            exp_refs[level][:, half * 128 : half * 128 + 128] = rows_ref[half]


def multipoles_of(pieces, export_slots, after):
    vm = pl.BlockSpec(memory_space=VMEM)
    out = pl.pallas_call(
        multipole_kernel,
        out_shape=[
            jax.ShapeDtypeStruct((ROWS, SLOTS), f32),
            jax.ShapeDtypeStruct((4, BODIES, SLOTS), f32),
        ]
        + [jax.ShapeDtypeStruct((KEXP, 256), f32)] * LEVELS,
        in_specs=[vm] * PEERS + [pl.BlockSpec(memory_space=pltpu.HBM), vm],
        out_specs=[vm] * (2 + LEVELS),
        scratch_shapes=[
            pltpu.VMEM((TERMS, 8, SLOTS), f32),
            pltpu.VMEM((2, SLOTS, 128), f32),
            pltpu.VMEM((2, KEXP, 128), f32),
            pltpu.SMEM((LEVELS, 1, KEXP), jnp.int32),
            pltpu.SemaphoreType.DMA,
            VMEM((4, SLOTS, BODIES), f32),
        ],
        compiler_params=small(4),
        name="multipoles",
    )(*pieces, in_hbm(export_slots.transpose(1, 0, 2)), after)
    return out[0], out[1], out[2:]


def near_kernel(post_ref, tgt_ref, src_ref, off_ref, near_ref, s_ref, t_ref, a_ref):
    row = iota((128, 128), 0)
    pick_s = jnp.where(src_ref[...] == row, 1.0, 0.0)
    pick_t = jnp.where(tgt_ref[...] == row, 1.0, 0.0)
    k = off_ref[...].astype(f32)
    one, zero = jnp.ones_like(k), jnp.zeros_like(k)
    kx = jnp.where(k >= 9.0, one, zero) + jnp.where(k >= 18.0, one, zero)
    k = k - 9.0 * kx
    ky = jnp.where(k >= 3.0, one, zero) + jnp.where(k >= 6.0, one, zero)
    kz = k - 3.0 * ky
    for a, shift in enumerate((kx, ky, kz)):
        s_ref[a] = dot_exact(post_ref[a], pick_s) + 2.0 * (shift - 1.0)
        t_ref[a] = dot_exact(post_ref[a], pick_t)
    s_ref[3] = dot_exact(post_ref[3], pick_s)

    def chunk(q, carry):
        rows = pl.ds(pl.multiple_of(q * 32, 32), 32)
        tx, ty, tz = (t_ref[a, rows, :] for a in range(3))

        def source(j, state):
            p, ax, ay, az = state
            sx, sy, sz, m = (s_ref[a, pl.ds(j, 1), :] for a in range(4))
            rx, ry, rz = sx - tx, sy - ty, sz - tz
            inv = lax.rsqrt(rx * rx + ry * ry + rz * rz + SOFT)
            w = m * inv
            p = p - w
            w = w * (inv * inv)
            return p, ax + rx * w, ay + ry * w, az + rz * w

        done = lax.fori_loop(0, 128, source, (jnp.zeros((32, 128), f32),) * 4, unroll=8)
        for a in range(4):
            a_ref[a, rows, :] = done[a]
        return carry

    lax.fori_loop(0, 4, chunk, 0)
    into = pick_t.T
    for a in range(4):
        near_ref[a] = dot_exact(a_ref[a], into)


def near_field(post, target, source, offset):
    vm = pl.BlockSpec(memory_space=VMEM)
    return pl.pallas_call(
        near_kernel,
        out_shape=jax.ShapeDtypeStruct((4, BODIES, SLOTS), f32),
        in_specs=[vm] * 4,
        out_specs=vm,
        scratch_shapes=[VMEM((4, 128, 128), f32), VMEM((3, 128, 128), f32), VMEM((4, 128, 128), f32)],
        compiler_params=small(4),
        cost_estimate=pl.CostEstimate(flops=8 * 10**9, bytes_accessed=10**6, transcendentals=2 * 10**6),
        name="near",
    )(post, target, source, offset)


def field_kernel(counts_ref, left_ref, mt_ref, *rest):
    far_refs, rest = rest[:LEVELS], rest[LEVELS:]
    post_ref, near_ref, out_ref, src_ref, bt_ref, acc_ref, e_ref, f_ref = rest

    far = jnp.concatenate([r[...] for r in far_refs], axis=0)
    far = jnp.concatenate([far, jnp.zeros((32, 256), f32)], axis=0)
    parts = [mt_ref[...]]
    for q in range(2):
        block = far[q * 128 : q * 128 + 128, :]
        parts.append(jnp.concatenate([block[:, 0:128].T, block[:, 128:256].T[0 : ROWS - 128]], axis=0))
    sources = jnp.concatenate(parts, axis=1)
    high = sources.astype(bf16).astype(f32)
    both = jnp.concatenate([high, sources - high], axis=0).astype(bf16)
    src_ref[...] = both[:, 0:SOURCES]

    def move(p, carry):
        moved = dot(src_ref[...], counts_ref[p])
        moved = moved[0:ROWS] + moved[ROWS : 2 * ROWS]
        for k in range(2):
            bt_ref[pl.ds(2 * p + k, ROWS, stride=PITCH), :] = moved[:, k * 128 : k * 128 + 128]
        return carry

    lax.fori_loop(0, CLASSES // 2, move, 0, unroll=16)

    acc_ref[...] = jnp.zeros_like(acc_ref)

    def contract(jb, carry):
        right = [
            jnp.concatenate(split(bt_ref[pl.ds((jb * J_STEP + j) * PITCH, CLASSES), :]), axis=1)
            for j in range(J_STEP)
        ]
        acc_ref[...] += dot(left_ref[jb], jnp.concatenate(right, axis=0))
        return carry

    lax.fori_loop(0, J_BLOCKS, contract, 0, unroll=21)
    acc = acc_ref[...]
    e = (acc[I_ROWS:, 128:] + acc[I_ROWS:, :128]) + acc[:I_ROWS, 128:] + acc[:I_ROWS, :128]
    e_ref[...] = e[0:ROWS]

    present = jnp.where(post_ref[3, 0:1, :] > 0.0, 1.0, 0.0)

    def chunk(q, carry):
        rows = pl.ds(pl.multiple_of(q * 32, 32), 32)
        x, y, z = (post_ref[a, rows, :] for a in range(3))

        def coef(a, b, c):
            n = TERM[a, b, c]
            return jnp.broadcast_to(e_ref[n : n + 1, :] * NORM[a, b, c], (32, SLOTS))

        p = px = py = pz = None
        for a in range(ORDER, -1, -1):
            r = ry = rz = None
            for b in range(ORDER - a, -1, -1):
                top = ORDER - a - b
                v = coef(a, b, top)
                vz = None
                for c in range(top - 1, -1, -1):
                    vz = v if vz is None else vz * z + v
                    v = v * z + coef(a, b, c)
                if r is None:
                    r = v
                else:
                    ry = r if ry is None else ry * y + r
                    r = r * y + v
                    if vz is not None:
                        rz = vz if rz is None else rz * y + vz
            if p is None:
                p = r
            else:
                px = p if px is None else px * x + p
                p = p * x + r
                py = ry if py is None else py * x + ry
                pz = rz if pz is None else pz * x + rz
        for a, v in enumerate((p, -px, -py, -pz)):
            f_ref[a, rows, :] = (v + near_ref[a, rows, :]) * present
        return carry

    lax.fori_loop(0, BODIES // 32, chunk, 0)
    for a in range(4):
        out_ref[:, a, :] = f_ref[a].T


def field(counts, left, mt, far, post, near):
    vm = pl.BlockSpec(memory_space=VMEM)
    return pl.pallas_call(
        field_kernel,
        out_shape=jax.ShapeDtypeStruct((SLOTS, 4, BODIES), f32),
        in_specs=[vm] * (5 + LEVELS),
        out_specs=vm,
        scratch_shapes=[
            VMEM((2 * ROWS, SOURCES), bf16),
            VMEM((ROWS * PITCH, SLOTS), f32),
            VMEM((2 * I_ROWS, 256), f32),
            VMEM((ROWS, SLOTS), f32),
            VMEM((4, BODIES, SLOTS), f32),
        ],
        compiler_params=small(20),
        cost_estimate=pl.CostEstimate(flops=40 * 10**9, bytes_accessed=26 * 10**6, transcendentals=0),
        name="field",
    )(counts, left, mt, *far, post, near)


def body(
    positions,
    masses,
    owner,
    operators,
    m2l_target,
    far_source,
    local_source,
    export_slots,
    near_target,
    near_source,
    near_offset,
):
    axes = ("dom", "sub")
    devices = lax.axis_size(axes)
    pieces = pack_tiles(owner, positions, masses)
    pieces = list(pieces[:1]) + [
        lax.ppermute(pieces[k], "sub", [(i, i ^ k) for i in range(PEERS)]) for k in range(1, PEERS)
    ]
    counts, left, done = prepare(m2l_target[0], far_source[0], local_source[0], operators)
    mt, post, exported = multipoles_of(pieces, export_slots, done)
    far = [
        lax.ppermute(rows, axes, [(i, i ^ (1 << level)) for i in range(devices)])
        for level, rows in enumerate(exported)
    ]
    near = near_field(post, near_target, near_source, near_offset)
    return field(counts, left, mt, far, post, near)


def solution(mesh):
    both = ("dom", "sub")
    in_specs = (
        P(both, None, None),
        P(both, None),
        P(both, None),
        P(),
        P(both, None, None, None),
        P(both, None, None, None),
        P(both, None, None),
        P(both, None, None),
        P(both, None),
        P(both, None),
        P(both, None),
    )
    out_specs = P(both, None, None)
    return jax.shard_map(body, mesh=mesh, in_specs=in_specs, out_specs=out_specs, check_vma=False)
```

```python
import functools

import jax
import jax.numpy as jnp
import numpy as np
from jax import lax
from jax.experimental import pallas as pl
from jax.experimental.pallas import tpu as pltpu
from jax.sharding import PartitionSpec as P

ORDER = 8
TERMS = 165
ROWS = 168
TERMS_PAD = ROWS
SOFT = 0.01
SLOTS = 128
PEERS = 8
CAP = SLOTS // PEERS
BODIES = 128
KEXP = 32
LEVELS = 7
CLASSES = 128
SOURCES = SLOTS + LEVELS * KEXP
f32 = jnp.float32
bf16 = jnp.bfloat16
f8 = jnp.float8_e4m3fn
VMEM = pltpu.VMEM
SMEM = pltpu.SMEM


def term_list():
    triples = []
    for degree in range(ORDER + 1):
        for a in range(degree, -1, -1):
            for b in range(degree - a, -1, -1):
                triples.append((a, b, degree - a - b))
    return {t: n for n, t in enumerate(triples)}


TERM = term_list()
NORM = {t: float(np.float32(np.sqrt(np.prod(2.0 * np.array(t) + 1.0)))) for t in TERM}


def small(mib):
    return pltpu.CompilerParams(vmem_limit_bytes=mib * 2**20)


def in_hbm(x):
    return pltpu.with_memory_space_constraint(x, pltpu.HBM)


def iota(shape, axis):
    return lax.broadcasted_iota(jnp.int32, shape, axis)


def split(v):
    high = v.astype(bf16)
    return high, (v - high.astype(f32)).astype(bf16)


def dot(a, b):
    return jnp.dot(a, b, preferred_element_type=f32)


def dot_nt(a, b):
    return lax.dot_general(a, b, (((1,), (1,)), ((), ())), preferred_element_type=f32)


def dot_parts(a, b):
    high = a.astype(bf16).astype(f32)
    rest = a - high
    middle = rest.astype(bf16).astype(f32)
    parts = dot(jnp.concatenate([high, middle, rest - middle], axis=0).astype(bf16), b)
    n = a.shape[0]
    return (parts[2 * n :] + parts[n : 2 * n]) + parts[:n]


def pack_kernel(owner_hbm, pos_hbm, mass_hbm, tgt_hbm, far_hbm, local_hbm, *rest):
    list_refs, rest = rest[:3], rest[3:]
    out_refs, (owner_ref, pos_ref, mass_ref, sem, count_ref), slot_refs = rest[:PEERS], rest[PEERS:-4], rest[-4:]
    copies = [
        pltpu.make_async_copy(a, b, sem.at[k])
        for k, (a, b) in enumerate(((owner_hbm, owner_ref), (pos_hbm, pos_ref), (mass_hbm, mass_ref)))
    ]
    lists = [
        pltpu.make_async_copy(a, b, sem.at[3 + k])
        for k, (a, b) in enumerate(zip((tgt_hbm, far_hbm, local_hbm), list_refs))
    ]
    for c in copies + lists:
        c.start()
    for r in slot_refs:
        r[...] = jnp.zeros_like(r)
    for o in range(PEERS):
        count_ref[o] = 0
    me = lax.axis_index("sub")
    for c in copies:
        c.wait()

    def step(i, carry):
        o = owner_ref[0, i]
        rank = count_ref[o]
        count_ref[o] = rank + 1
        slot = (o ^ me) * CAP + rank
        for a in range(3):
            slot_refs[a][pl.ds(slot, 1), :] = pos_ref[a, pl.ds(i, 1), :]
        slot_refs[3][pl.ds(slot, 1), :] = mass_ref[pl.ds(i, 1), :]
        return carry

    lax.fori_loop(0, mass_ref.shape[0], step, 0)
    for k in range(PEERS):
        for a in range(4):
            out_refs[k][:, a * BODIES : (a + 1) * BODIES] = slot_refs[a][k * CAP : (k + 1) * CAP, :]
    for c in lists:
        c.wait()


def pack_tiles(owner, positions, masses, lists):
    out = pl.pallas_call(
        pack_kernel,
        out_shape=[VMEM(x.shape, x.dtype) for x in lists]
        + [jax.ShapeDtypeStruct((CAP, 4 * BODIES), f32)] * PEERS,
        in_specs=[pl.BlockSpec(memory_space=pltpu.HBM)] * 6,
        out_specs=[pl.BlockSpec(memory_space=VMEM)] * (3 + PEERS),
        scratch_shapes=[
            pltpu.SMEM((1, owner.shape[0]), jnp.int32),
            VMEM((3, owner.shape[0], BODIES), f32),
            VMEM((owner.shape[0], BODIES), f32),
            pltpu.SemaphoreType.DMA((6,)),
            pltpu.SMEM((PEERS,), jnp.int32),
        ]
        + [VMEM((SLOTS, BODIES), f32)] * 4,
        compiler_params=small(2),
        name="pack",
    )(*map(in_hbm, (owner.T, positions.transpose(1, 0, 2), masses, *lists)))
    return out[:3], list(out[3:])


I_STEP = 16
I_FULL = TERMS // I_STEP
PAIR_STEP = 32
I_ROWS = (I_FULL + 1) * I_STEP
J_STEP = 8
PITCH = CLASSES + 1
J_BLOCKS = ROWS // J_STEP


def prepare_kernel(
    tgt_ref, far_ref, local_ref, op_hbm, counts_ref, left_ref, done_ref, tt_ref, st_ref, buf_ref, sem
):
    def copy(q, size):
        return pltpu.make_async_copy(
            op_hbm.at[pl.ds(q * I_STEP, size)], buf_ref.at[q, pl.ds(0, size), pl.ds(0, TERMS)], sem.at[q]
        )

    for q in range(I_FULL):
        copy(q, I_STEP).start()
    copy(I_FULL, TERMS - I_FULL * I_STEP).start()

    order = [7, 0, 1, 2, 3, 4, 5, 6]
    for pair in range(4):
        tgt, src = [], []
        for level in order[2 * pair : 2 * pair + 2]:
            tgt.append(tgt_ref[level].astype(f32))
            if level == 7:
                src.append(local_ref[...].astype(f32))
            else:
                offset = {0: SLOTS, 1: 0, 2: KEXP, 3: 0, 4: KEXP, 5: 0, 6: KEXP}[level]
                src.append((far_ref[level] + offset).astype(f32))
        tt_ref[pair] = jnp.concatenate(tgt, axis=0).T
        st_ref[pair] = jnp.concatenate(src, axis=0).T

    ids = iota((160, 128), 0).astype(f32).astype(bf16)

    def onehot(ref, part, c, first, size, total):
        row = jnp.broadcast_to(ref[part, pl.ds(c, 1), :].astype(bf16), (size, 128))
        hits = jnp.where(row == ids[0:size], jnp.ones((), bf16), jnp.zeros((), bf16))
        zeros = lambda n: [jnp.zeros((n, 128), bf16)] if n else []
        return jnp.concatenate(zeros(first) + [hits] + zeros(total - first - size), axis=0)

    def classes(p):
        for k in range(2):
            c = 2 * p + k
            for half, (first, size) in enumerate(((0, 224), (224, 128))):
                cut = 160 if half == 0 else 64
                target = jnp.concatenate([onehot(tt_ref, 2 * half + i, c, 0, 128, 128) for i in range(2)], axis=1)
                source = jnp.concatenate(
                    [
                        onehot(st_ref, 2 * half, c, 0, cut, size),
                        onehot(st_ref, 2 * half + 1, c, cut, size - cut, size),
                    ],
                    axis=1,
                )
                counts = dot_nt(source.astype(f8), target.astype(f8))
                counts_ref[p, first : first + size, k * 128 : k * 128 + 128] = counts.astype(bf16)

    def group(g, carry):
        for i in range(PAIR_STEP):
            classes(g * PAIR_STEP + i)
        return carry

    lax.fori_loop(0, CLASSES // 2 // PAIR_STEP, group, 0)
    for j in range(TERMS, ROWS):
        left_ref[J_BLOCKS - 1, :, (j % J_STEP) * 128 : (j % J_STEP) * 128 + 128] = jnp.zeros((2 * I_ROWS, 128), bf16)

    def relay(q):
        rows = buf_ref.at[q].reshape(I_STEP * TERMS_PAD, CLASSES)
        at = pl.multiple_of(q * I_STEP, I_STEP)
        for j in range(TERMS):
            v = rows[pl.ds(j, I_STEP, stride=TERMS_PAD), :]
            high, low = split(v)
            lanes = slice((j % J_STEP) * 128, (j % J_STEP) * 128 + 128)
            left_ref[j // J_STEP, pl.ds(at, I_STEP), lanes] = high
            left_ref[j // J_STEP, pl.ds(at + I_ROWS, I_STEP), lanes] = low

    def chunk(q, carry):
        copy(q, I_STEP).wait()
        relay(q)
        return carry

    lax.fori_loop(0, I_FULL, chunk, 0)
    copy(I_FULL, TERMS - I_FULL * I_STEP).wait()
    relay(I_FULL)
    done_ref[...] = jnp.zeros_like(done_ref)


def prepare(m2l_target, far_source, local_source, operators):
    vm = pl.BlockSpec(memory_space=VMEM)
    counts, left = (CLASSES // 2, SOURCES, 256), (J_BLOCKS, 2 * I_ROWS, J_STEP * CLASSES)
    return pl.pallas_call(
        prepare_kernel,
        out_shape=[VMEM(counts, bf16), VMEM(left, bf16), VMEM((8, 128), f32)],
        in_specs=[vm] * 3 + [pl.BlockSpec(memory_space=pltpu.HBM)],
        out_specs=[vm] * 3,
        scratch_shapes=[
            VMEM((4, 128, 128), f32),
            VMEM((4, 128, 128), f32),
            VMEM((I_FULL + 1, I_STEP, TERMS_PAD, CLASSES), f32),
            pltpu.SemaphoreType.DMA((I_FULL + 1,)),
        ],
        compiler_params=small(20),
        cost_estimate=pl.CostEstimate(flops=12 * 10**9, bytes_accessed=14 * 10**6, transcendentals=0),
        name="prepare",
    )(m2l_target, far_source, local_source, in_hbm(operators))


def multipole_kernel(*refs):
    pieces, refs = refs[:PEERS], refs[PEERS:]
    slots_hbm, _, mt_ref, post_ref, *refs = refs
    exp_refs, (acc_ref, m_ref, rows_ref, slots_ref, sem, recv_ref) = refs[:LEVELS], refs[LEVELS:]
    slots_copy = pltpu.make_async_copy(slots_hbm, slots_ref, sem)
    slots_copy.start()
    me = lax.axis_index("sub")
    for k in range(PEERS):
        rows = pl.ds(pl.multiple_of((me ^ k) * CAP, CAP), CAP)
        for a in range(4):
            recv_ref[a, rows, :] = pieces[k][:, a * BODIES : (a + 1) * BODIES]
    for a in range(4):
        post_ref[a] = recv_ref[a].T

    acc_ref[...] = jnp.zeros_like(acc_ref)

    def chunk(q, carry):
        rows = pl.ds(pl.multiple_of(q * 32, 32), 32)
        x, y, z, m = (post_ref[a, rows, :] for a in range(4))

        def fold(term, n):
            part = (term[0:8] + term[8:16]) + (term[16:24] + term[24:32])
            acc_ref[n] += part

        px = m
        for a in range(ORDER + 1):
            py = px
            for b in range(ORDER + 1 - a):
                pz = py
                for c in range(ORDER + 1 - a - b):
                    fold(pz, TERM[a, b, c])
                    if c < ORDER - a - b:
                        pz = pz * z
                if b < ORDER - a:
                    py = py * y
            if a < ORDER:
                px = px * x
        return carry

    lax.fori_loop(0, BODIES // 32, chunk, 0)
    mt_ref[TERMS - 5 :, :] = jnp.zeros((ROWS - TERMS + 5, SLOTS), f32)
    for (a, b, c), n in TERM.items():
        mt_ref[n : n + 1, :] = jnp.sum(acc_ref[n], axis=0, keepdims=True) * NORM[a, b, c]
    m_ref[0] = mt_ref[0:128, :].T
    m_ref[1] = jnp.concatenate([mt_ref[128:ROWS, :], jnp.zeros((256 - ROWS, SLOTS), f32)], axis=0).T
    slots_copy.wait()
    for level in range(LEVELS):

        def row(k, carry):
            slot = slots_ref[level, 0, k]
            for half in range(2):
                rows_ref[half, pl.ds(k, 1), :] = m_ref[half, pl.ds(slot, 1), :]
            return carry

        lax.fori_loop(0, KEXP, row, 0, unroll=8)
        for half in range(2):
            exp_refs[level][:, half * 128 : half * 128 + 128] = rows_ref[half]


def multipoles_of(pieces, export_slots, after):
    vm = pl.BlockSpec(memory_space=VMEM)
    out = pl.pallas_call(
        multipole_kernel,
        out_shape=[
            jax.ShapeDtypeStruct((ROWS, SLOTS), f32),
            jax.ShapeDtypeStruct((4, BODIES, SLOTS), f32),
        ]
        + [jax.ShapeDtypeStruct((KEXP, 256), f32)] * LEVELS,
        in_specs=[vm] * PEERS + [pl.BlockSpec(memory_space=pltpu.HBM), vm],
        out_specs=[vm] * (2 + LEVELS),
        scratch_shapes=[
            pltpu.VMEM((TERMS, 8, SLOTS), f32),
            pltpu.VMEM((2, SLOTS, 128), f32),
            pltpu.VMEM((2, KEXP, 128), f32),
            pltpu.SMEM((LEVELS, 1, KEXP), jnp.int32),
            pltpu.SemaphoreType.DMA,
            VMEM((4, SLOTS, BODIES), f32),
        ],
        compiler_params=small(4),
        name="multipoles",
    )(*pieces, in_hbm(export_slots.transpose(1, 0, 2)), after)
    return out[0], out[1], out[2:]


def near_kernel(post_ref, tgt_ref, src_ref, off_ref, near_ref, s_ref, t_ref, a_ref):
    row = iota((128, 128), 0)
    pick_s = jnp.where(src_ref[...] == row, 1.0, 0.0)
    pick_t = jnp.where(tgt_ref[...] == row, 1.0, 0.0)
    k = off_ref[...].astype(f32)
    one, zero = jnp.ones_like(k), jnp.zeros_like(k)
    kx = jnp.where(k >= 9.0, one, zero) + jnp.where(k >= 18.0, one, zero)
    k = k - 9.0 * kx
    ky = jnp.where(k >= 3.0, one, zero) + jnp.where(k >= 6.0, one, zero)
    kz = k - 3.0 * ky
    picks = jnp.concatenate([pick_s, pick_t], axis=1).astype(bf16)
    shifts = (kx, ky, kz)
    for a in range(4):
        picked = dot_parts(post_ref[a], picks)
        s_ref[a] = picked[:, 0:128] + 2.0 * (shifts[a] - 1.0) if a < 3 else picked[:, 0:128]
        if a < 3:
            t_ref[a] = picked[:, 128:256]

    def chunk(q, carry):
        rows = pl.ds(pl.multiple_of(q * 32, 32), 32)
        tx, ty, tz = (t_ref[a, rows, :] for a in range(3))

        def source(j, state):
            p, ax, ay, az = state
            sx, sy, sz, m = (s_ref[a, pl.ds(j, 1), :] for a in range(4))
            rx, ry, rz = sx - tx, sy - ty, sz - tz
            inv = lax.rsqrt(rx * rx + ry * ry + rz * rz + SOFT)
            w = m * inv
            p = p - w
            w = w * (inv * inv)
            return p, ax + rx * w, ay + ry * w, az + rz * w

        done = lax.fori_loop(0, 128, source, (jnp.zeros((32, 128), f32),) * 4, unroll=32)
        for a in range(4):
            a_ref[a, rows, :] = done[a]
        return carry

    lax.fori_loop(0, 4, chunk, 0)
    into = pick_t.T.astype(bf16)
    for a in range(4):
        near_ref[a] = dot_parts(a_ref[a], into)


def near_field(post, target, source, offset):
    vm = pl.BlockSpec(memory_space=VMEM)
    return pl.pallas_call(
        near_kernel,
        out_shape=jax.ShapeDtypeStruct((4, BODIES, SLOTS), f32),
        in_specs=[vm] * 4,
        out_specs=vm,
        scratch_shapes=[VMEM((4, 128, 128), f32), VMEM((3, 128, 128), f32), VMEM((4, 128, 128), f32)],
        compiler_params=small(4),
        cost_estimate=pl.CostEstimate(flops=8 * 10**9, bytes_accessed=10**6, transcendentals=2 * 10**6),
        name="near",
    )(post, target, source, offset)


def field_kernel(counts_ref, left_ref, mt_ref, *rest):
    far_refs, rest = rest[:LEVELS], rest[LEVELS:]
    post_ref, near_ref, out_ref, src_ref, bt_ref, acc_ref, e_ref, f_ref = rest

    far = jnp.concatenate([r[...] for r in far_refs], axis=0)
    far = jnp.concatenate([far, jnp.zeros((32, 256), f32)], axis=0)
    parts = [mt_ref[...]]
    for q in range(2):
        block = far[q * 128 : q * 128 + 128, :]
        parts.append(jnp.concatenate([block[:, 0:128].T, block[:, 128:256].T[0 : ROWS - 128]], axis=0))
    sources = jnp.concatenate(parts, axis=1)
    high = sources.astype(bf16).astype(f32)
    high, low = high.astype(bf16), (sources - high).astype(bf16)
    src_ref[...] = jnp.concatenate([high, low], axis=1)

    def move(p, carry):
        counts = counts_ref[p]
        moved = dot(src_ref[...], jnp.concatenate([counts, jnp.zeros((32, 256), bf16), counts, jnp.zeros((32, 256), bf16)], axis=0))
        for k in range(2):
            bt_ref[pl.ds(2 * p + k, ROWS, stride=PITCH), :] = moved[:, k * 128 : k * 128 + 128]
        return carry

    lax.fori_loop(0, CLASSES // 2, move, 0, unroll=16)

    acc_ref[...] = jnp.zeros_like(acc_ref)

    def contract(jb, carry):
        right = [
            jnp.concatenate(split(bt_ref[pl.ds((jb * J_STEP + j) * PITCH, CLASSES), :]), axis=1)
            for j in range(J_STEP)
        ]
        acc_ref[...] += dot(left_ref[jb], jnp.concatenate(right, axis=0))
        return carry

    lax.fori_loop(0, J_BLOCKS, contract, 0, unroll=21)
    acc = acc_ref[...]
    e = (acc[I_ROWS:, 128:] + acc[I_ROWS:, :128]) + acc[:I_ROWS, 128:] + acc[:I_ROWS, :128]
    e_ref[...] = e[0:ROWS]

    present = jnp.where(post_ref[3, 0:1, :] > 0.0, 1.0, 0.0)

    def chunk(q, carry):
        rows = pl.ds(pl.multiple_of(q * 32, 32), 32)
        x, y, z = (post_ref[a, rows, :] for a in range(3))

        def coef(a, b, c):
            n = TERM[a, b, c]
            return jnp.broadcast_to(e_ref[n : n + 1, :] * NORM[a, b, c], (32, SLOTS))

        p = px = py = pz = None
        for a in range(ORDER, -1, -1):
            r = ry = rz = None
            for b in range(ORDER - a, -1, -1):
                top = ORDER - a - b
                v = coef(a, b, top)
                vz = None
                for c in range(top - 1, -1, -1):
                    vz = v if vz is None else vz * z + v
                    v = v * z + coef(a, b, c)
                if r is None:
                    r = v
                else:
                    ry = r if ry is None else ry * y + r
                    r = r * y + v
                    if vz is not None:
                        rz = vz if rz is None else rz * y + vz
            if p is None:
                p = r
            else:
                px = p if px is None else px * x + p
                p = p * x + r
                py = ry if py is None else py * x + ry
                pz = rz if pz is None else pz * x + rz
        for a, v in enumerate((p, -px, -py, -pz)):
            f_ref[a, rows, :] = (v + near_ref[a, rows, :]) * present
        return carry

    lax.fori_loop(0, BODIES // 32, chunk, 0)
    for a in range(4):
        out_ref[:, a, :] = f_ref[a].T


def field(counts, left, mt, far, post, near):
    vm = pl.BlockSpec(memory_space=VMEM)
    return pl.pallas_call(
        field_kernel,
        out_shape=jax.ShapeDtypeStruct((SLOTS, 4, BODIES), f32),
        in_specs=[vm] * (5 + LEVELS),
        out_specs=vm,
        scratch_shapes=[
            VMEM((ROWS, 768), bf16),
            VMEM((ROWS * PITCH, SLOTS), f32),
            VMEM((2 * I_ROWS, 256), f32),
            VMEM((ROWS, SLOTS), f32),
            VMEM((4, BODIES, SLOTS), f32),
        ],
        compiler_params=small(20),
        cost_estimate=pl.CostEstimate(flops=40 * 10**9, bytes_accessed=26 * 10**6, transcendentals=0),
        name="field",
    )(counts, left, mt, *far, post, near)


def body(
    positions,
    masses,
    owner,
    operators,
    m2l_target,
    far_source,
    local_source,
    export_slots,
    near_target,
    near_source,
    near_offset,
):
    axes = ("dom", "sub")
    devices = lax.axis_size(axes)
    lists, pieces = pack_tiles(owner, positions, masses, (m2l_target[0], far_source[0], local_source[0]))
    pieces = pieces[:1] + [
        lax.ppermute(pieces[k], "sub", [(i, i ^ k) for i in range(PEERS)]) for k in range(1, PEERS)
    ]
    counts, left, done = prepare(*lists, operators)
    mt, post, exported = multipoles_of(pieces, export_slots, done)
    far = [
        lax.ppermute(rows, axes, [(i, i ^ (1 << level)) for i in range(devices)])
        for level, rows in enumerate(exported)
    ]
    near = near_field(post, near_target, near_source, near_offset)
    return field(counts, left, mt, far, post, near)


def solution(mesh):
    both = ("dom", "sub")
    in_specs = (
        P(both, None, None),
        P(both, None),
        P(both, None),
        P(),
        P(both, None, None, None),
        P(both, None, None, None),
        P(both, None, None),
        P(both, None, None),
        P(both, None),
        P(both, None),
        P(both, None),
    )
    out_specs = P(both, None, None)
    return jax.shard_map(body, mesh=mesh, in_specs=in_specs, out_specs=out_specs, check_vma=False)
```

```python
import functools

import jax
import jax.numpy as jnp
import numpy as np
from jax import lax
from jax.experimental import pallas as pl
from jax.experimental.pallas import tpu as pltpu
from jax.sharding import PartitionSpec as P

ORDER = 8
TERMS = 165
ROWS = 168
TERMS_PAD = ROWS
SOFT = 0.01
SLOTS = 128
PEERS = 8
CAP = SLOTS // PEERS
BODIES = 128
KEXP = 32
LEVELS = 7
CLASSES = 128
SOURCES = SLOTS + LEVELS * KEXP
f32 = jnp.float32
bf16 = jnp.bfloat16
f8 = jnp.float8_e4m3fn
VMEM = pltpu.VMEM
SMEM = pltpu.SMEM


def term_list():
    triples = []
    for degree in range(ORDER + 1):
        for a in range(degree, -1, -1):
            for b in range(degree - a, -1, -1):
                triples.append((a, b, degree - a - b))
    return {t: n for n, t in enumerate(triples)}


TERM = term_list()
NORM = {t: float(np.float32(np.sqrt(np.prod(2.0 * np.array(t) + 1.0)))) for t in TERM}


def small(mib):
    return pltpu.CompilerParams(vmem_limit_bytes=mib * 2**20)


def in_hbm(x):
    return pltpu.with_memory_space_constraint(x, pltpu.HBM)


def iota(shape, axis):
    return lax.broadcasted_iota(jnp.int32, shape, axis)


def split(v):
    high = v.astype(bf16)
    return high, (v - high.astype(f32)).astype(bf16)


def dot(a, b):
    return jnp.dot(a, b, preferred_element_type=f32)


def dot_nt(a, b):
    return lax.dot_general(a, b, (((1,), (1,)), ((), ())), preferred_element_type=f32)


def dot_parts(a, b):
    high = a.astype(bf16).astype(f32)
    rest = a - high
    middle = rest.astype(bf16).astype(f32)
    parts = dot(jnp.concatenate([high, middle, rest - middle], axis=0).astype(bf16), b)
    n = a.shape[0]
    return (parts[2 * n :] + parts[n : 2 * n]) + parts[:n]


def pack_kernel(owner_hbm, pos_hbm, mass_hbm, tgt_hbm, far_hbm, local_hbm, *rest):
    list_refs, rest = rest[:3], rest[3:]
    out_refs, (owner_ref, pos_ref, mass_ref, sem, count_ref), slot_refs = rest[:2], rest[2:-4], rest[-4:]
    copies = [
        pltpu.make_async_copy(a, b, sem.at[k])
        for k, (a, b) in enumerate(((owner_hbm, owner_ref), (pos_hbm, pos_ref), (mass_hbm, mass_ref)))
    ]
    lists = [
        pltpu.make_async_copy(a, b, sem.at[3 + k])
        for k, (a, b) in enumerate(zip((tgt_hbm, far_hbm, local_hbm), list_refs))
    ]
    for c in copies + lists:
        c.start()
    for r in slot_refs:
        r[...] = jnp.zeros_like(r)
    for o in range(PEERS):
        count_ref[o] = 0
    me = lax.axis_index("sub")
    for c in copies:
        c.wait()

    def step(i, carry):
        o = owner_ref[0, i]
        rank = count_ref[o]
        count_ref[o] = rank + 1
        slot = (o ^ me) * CAP + rank
        for a in range(3):
            slot_refs[a][pl.ds(slot, 1), :] = pos_ref[a, pl.ds(i, 1), :]
        slot_refs[3][pl.ds(slot, 1), :] = mass_ref[pl.ds(i, 1), :]
        return carry

    lax.fori_loop(0, mass_ref.shape[0], step, 0)
    half = SLOTS // 2
    for k in range(2):
        for a in range(4):
            out_refs[k][:, a * BODIES : (a + 1) * BODIES] = slot_refs[a][k * half : (k + 1) * half, :]
    for c in lists:
        c.wait()


def pack_tiles(owner, positions, masses, lists):
    out = pl.pallas_call(
        pack_kernel,
        out_shape=[VMEM(x.shape, x.dtype) for x in lists]
        + [jax.ShapeDtypeStruct((SLOTS // 2, 4 * BODIES), f32)] * 2,
        in_specs=[pl.BlockSpec(memory_space=pltpu.HBM)] * 6,
        out_specs=[pl.BlockSpec(memory_space=VMEM)] * 5,
        scratch_shapes=[
            pltpu.SMEM((1, owner.shape[0]), jnp.int32),
            VMEM((3, owner.shape[0], BODIES), f32),
            VMEM((owner.shape[0], BODIES), f32),
            pltpu.SemaphoreType.DMA((6,)),
            pltpu.SMEM((PEERS,), jnp.int32),
        ]
        + [VMEM((SLOTS, BODIES), f32)] * 4,
        compiler_params=small(2),
        name="pack",
    )(*map(in_hbm, (owner.T, positions.transpose(1, 0, 2), masses, *lists)))
    return out[:3], out[3], out[4]


def merge_kernel(mine_ref, other_ref, after_ref, *out_refs):
    for q, ref in enumerate(out_refs, start=1):
        ref[0:CAP] = mine_ref[q * CAP : (q + 1) * CAP]
        ref[CAP : 2 * CAP] = other_ref[q * CAP : (q + 1) * CAP]


def merge(mine, other, after):
    vm = pl.BlockSpec(memory_space=VMEM)
    return pl.pallas_call(
        merge_kernel,
        out_shape=[jax.ShapeDtypeStruct((2 * CAP, 4 * BODIES), f32)] * 3,
        in_specs=[vm] * 3,
        out_specs=[vm] * 3,
        compiler_params=small(2),
        name="merge",
    )(mine, other, after)


I_STEP = 16
I_FULL = TERMS // I_STEP
PAIR_STEP = 32
I_ROWS = (I_FULL + 1) * I_STEP
J_STEP = 8
PITCH = CLASSES + 1
J_BLOCKS = ROWS // J_STEP


def operator_copy(op_hbm, buf_ref, sem, q):
    size = min(I_STEP, TERMS - q * I_STEP)
    return pltpu.make_async_copy(
        op_hbm.at[pl.ds(q * I_STEP, size)], buf_ref.at[q, pl.ds(0, size), pl.ds(0, TERMS)], sem.at[q]
    )


def count_kernel(tgt_ref, far_ref, local_ref, op_hbm, counts_ref, buf_ref, done_ref, tt_ref, st_ref, sem):
    for q in range(I_FULL + 1):
        operator_copy(op_hbm, buf_ref, sem, q).start()

    order = [7, 0, 1, 2, 3, 4, 5, 6]
    for pair in range(4):
        tgt, src = [], []
        for level in order[2 * pair : 2 * pair + 2]:
            tgt.append(tgt_ref[level].astype(f32))
            if level == 7:
                src.append(local_ref[...].astype(f32))
            else:
                offset = {0: SLOTS, 1: 0, 2: KEXP, 3: 0, 4: KEXP, 5: 0, 6: KEXP}[level]
                src.append((far_ref[level] + offset).astype(f32))
        tt_ref[pair] = jnp.concatenate(tgt, axis=0).T
        st_ref[pair] = jnp.concatenate(src, axis=0).T

    ids = iota((160, 128), 0).astype(f32).astype(bf16)

    def onehot(ref, part, c, first, size, total):
        row = jnp.broadcast_to(ref[part, pl.ds(c, 1), :].astype(bf16), (size, 128))
        hits = jnp.where(row == ids[0:size], jnp.ones((), bf16), jnp.zeros((), bf16))
        zeros = lambda n: [jnp.zeros((n, 128), bf16)] if n else []
        return jnp.concatenate(zeros(first) + [hits] + zeros(total - first - size), axis=0)

    def classes(p):
        for k in range(2):
            c = 2 * p + k
            for half, (first, size) in enumerate(((0, 224), (224, 128))):
                cut = 160 if half == 0 else 64
                target = jnp.concatenate([onehot(tt_ref, 2 * half + i, c, 0, 128, 128) for i in range(2)], axis=1)
                source = jnp.concatenate(
                    [
                        onehot(st_ref, 2 * half, c, 0, cut, size),
                        onehot(st_ref, 2 * half + 1, c, cut, size - cut, size),
                    ],
                    axis=1,
                )
                counts = dot_nt(source.astype(f8), target.astype(f8))
                counts_ref[p, first : first + size, k * 128 : k * 128 + 128] = counts.astype(bf16)

    def group(g, carry):
        for i in range(PAIR_STEP):
            classes(g * PAIR_STEP + i)
        return carry

    lax.fori_loop(0, CLASSES // 2 // PAIR_STEP, group, 0)
    done_ref[...] = jnp.zeros_like(done_ref)
    for q in range(I_FULL + 1):
        operator_copy(op_hbm, buf_ref, sem, q).wait()


def relay_kernel(buf_ref, after_ref, left_ref, done_ref):
    for j in range(TERMS, ROWS):
        left_ref[J_BLOCKS - 1, :, (j % J_STEP) * 128 : (j % J_STEP) * 128 + 128] = jnp.zeros((2 * I_ROWS, 128), bf16)

    def relay(q, carry):
        rows = buf_ref.at[q].reshape(I_STEP * TERMS_PAD, CLASSES)
        at = pl.multiple_of(q * I_STEP, I_STEP)
        for j in range(TERMS):
            v = rows[pl.ds(j, I_STEP, stride=TERMS_PAD), :]
            high, low = split(v)
            lanes = slice((j % J_STEP) * 128, (j % J_STEP) * 128 + 128)
            left_ref[j // J_STEP, pl.ds(at, I_STEP), lanes] = high
            left_ref[j // J_STEP, pl.ds(at + I_ROWS, I_STEP), lanes] = low
        return carry

    lax.fori_loop(0, I_FULL + 1, relay, 0)
    done_ref[...] = jnp.zeros_like(done_ref)


def count_pairs(m2l_target, far_source, local_source, operators):
    vm = pl.BlockSpec(memory_space=VMEM)
    return pl.pallas_call(
        count_kernel,
        out_shape=[
            VMEM((CLASSES // 2, SOURCES, 256), bf16),
            VMEM((I_FULL + 1, I_STEP, TERMS_PAD, CLASSES), f32),
            VMEM((8, 128), f32),
        ],
        in_specs=[vm] * 3 + [pl.BlockSpec(memory_space=pltpu.HBM)],
        out_specs=[vm] * 3,
        scratch_shapes=[
            VMEM((4, 128, 128), f32),
            VMEM((4, 128, 128), f32),
            pltpu.SemaphoreType.DMA((I_FULL + 1,)),
        ],
        compiler_params=small(4),
        cost_estimate=pl.CostEstimate(flops=6 * 10**9, bytes_accessed=14 * 10**6, transcendentals=0),
        name="counts",
    )(m2l_target, far_source, local_source, in_hbm(operators))


def relay_operators(rows, after):
    vm = pl.BlockSpec(memory_space=VMEM)
    return pl.pallas_call(
        relay_kernel,
        out_shape=[VMEM((J_BLOCKS, 2 * I_ROWS, J_STEP * CLASSES), bf16), VMEM((8, 128), f32)],
        in_specs=[vm] * 2,
        out_specs=[vm] * 2,
        compiler_params=small(4),
        cost_estimate=pl.CostEstimate(flops=4 * 10**9, bytes_accessed=10**6, transcendentals=0),
        name="relay",
    )(rows, after)


def multipole_kernel(*refs):
    (mine_ref, other_ref, *pieces), refs = refs[:5], refs[5:]
    slots_hbm, _, mt_ref, post_ref, *refs = refs
    exp_refs, (acc_ref, m_ref, rows_ref, slots_ref, sem, recv_ref) = refs[:LEVELS], refs[LEVELS:]
    slots_copy = pltpu.make_async_copy(slots_hbm, slots_ref, sem)
    slots_copy.start()
    me = lax.axis_index("sub")
    for k in range(PEERS):
        rows = pl.ds(pl.multiple_of((me ^ k) * CAP, CAP), CAP)
        if k % 4:
            piece, first = pieces[k % 4 - 1], k // 4 * CAP
        else:
            piece, first = (mine_ref, other_ref)[k // 4], 0
        for a in range(4):
            recv_ref[a, rows, :] = piece[first : first + CAP, a * BODIES : (a + 1) * BODIES]
    for a in range(4):
        post_ref[a] = recv_ref[a].T

    acc_ref[...] = jnp.zeros_like(acc_ref)

    def chunk(q, carry):
        rows = pl.ds(pl.multiple_of(q * 32, 32), 32)
        x, y, z, m = (post_ref[a, rows, :] for a in range(4))

        def fold(term, n):
            part = (term[0:8] + term[8:16]) + (term[16:24] + term[24:32])
            acc_ref[n] += part

        px = m
        for a in range(ORDER + 1):
            py = px
            for b in range(ORDER + 1 - a):
                pz = py
                for c in range(ORDER + 1 - a - b):
                    fold(pz, TERM[a, b, c])
                    if c < ORDER - a - b:
                        pz = pz * z
                if b < ORDER - a:
                    py = py * y
            if a < ORDER:
                px = px * x
        return carry

    lax.fori_loop(0, BODIES // 32, chunk, 0)
    mt_ref[TERMS - 5 :, :] = jnp.zeros((ROWS - TERMS + 5, SLOTS), f32)
    for (a, b, c), n in TERM.items():
        mt_ref[n : n + 1, :] = jnp.sum(acc_ref[n], axis=0, keepdims=True) * NORM[a, b, c]
    m_ref[0] = mt_ref[0:128, :].T
    m_ref[1] = jnp.concatenate([mt_ref[128:ROWS, :], jnp.zeros((256 - ROWS, SLOTS), f32)], axis=0).T
    slots_copy.wait()
    for level in range(LEVELS):

        def row(k, carry):
            slot = slots_ref[level, 0, k]
            for half in range(2):
                rows_ref[half, pl.ds(k, 1), :] = m_ref[half, pl.ds(slot, 1), :]
            return carry

        lax.fori_loop(0, KEXP, row, 0, unroll=8)
        for half in range(2):
            exp_refs[level][:, half * 128 : half * 128 + 128] = rows_ref[half]


def multipoles_of(pieces, export_slots, after):
    vm = pl.BlockSpec(memory_space=VMEM)
    out = pl.pallas_call(
        multipole_kernel,
        out_shape=[
            jax.ShapeDtypeStruct((ROWS, SLOTS), f32),
            jax.ShapeDtypeStruct((4, BODIES, SLOTS), f32),
        ]
        + [jax.ShapeDtypeStruct((KEXP, 256), f32)] * LEVELS,
        in_specs=[vm] * 5 + [pl.BlockSpec(memory_space=pltpu.HBM), vm],
        out_specs=[vm] * (2 + LEVELS),
        scratch_shapes=[
            pltpu.VMEM((TERMS, 8, SLOTS), f32),
            pltpu.VMEM((2, SLOTS, 128), f32),
            pltpu.VMEM((2, KEXP, 128), f32),
            pltpu.SMEM((LEVELS, 1, KEXP), jnp.int32),
            pltpu.SemaphoreType.DMA,
            VMEM((4, SLOTS, BODIES), f32),
        ],
        compiler_params=small(4),
        name="multipoles",
    )(*pieces, in_hbm(export_slots.transpose(1, 0, 2)), after)
    return out[0], out[1], out[2:]


def near_kernel(post_ref, tgt_ref, src_ref, off_ref, near_ref, s_ref, t_ref, a_ref):
    row = iota((128, 128), 0)
    pick_s = jnp.where(src_ref[...] == row, 1.0, 0.0)
    pick_t = jnp.where(tgt_ref[...] == row, 1.0, 0.0)
    k = off_ref[...].astype(f32)
    one, zero = jnp.ones_like(k), jnp.zeros_like(k)
    kx = jnp.where(k >= 9.0, one, zero) + jnp.where(k >= 18.0, one, zero)
    k = k - 9.0 * kx
    ky = jnp.where(k >= 3.0, one, zero) + jnp.where(k >= 6.0, one, zero)
    kz = k - 3.0 * ky
    picks = jnp.concatenate([pick_s, pick_t], axis=1).astype(bf16)
    shifts = (kx, ky, kz)
    for a in range(4):
        picked = dot_parts(post_ref[a], picks)
        s_ref[a] = picked[:, 0:128] + 2.0 * (shifts[a] - 1.0) if a < 3 else picked[:, 0:128]
        if a < 3:
            t_ref[a] = picked[:, 128:256]

    def chunk(q, carry):
        rows = pl.ds(pl.multiple_of(q * 32, 32), 32)
        tx, ty, tz = (t_ref[a, rows, :] for a in range(3))

        def source(j, state):
            p, ax, ay, az = state
            sx, sy, sz, m = (s_ref[a, pl.ds(j, 1), :] for a in range(4))
            rx, ry, rz = sx - tx, sy - ty, sz - tz
            inv = lax.rsqrt(rx * rx + ry * ry + rz * rz + SOFT)
            w = m * inv
            p = p - w
            w = w * (inv * inv)
            return p, ax + rx * w, ay + ry * w, az + rz * w

        done = lax.fori_loop(0, 128, source, (jnp.zeros((32, 128), f32),) * 4, unroll=32)
        for a in range(4):
            a_ref[a, rows, :] = done[a]
        return carry

    lax.fori_loop(0, 4, chunk, 0)
    into = pick_t.T.astype(bf16)
    for a in range(4):
        near_ref[a] = dot_parts(a_ref[a], into)


def near_field(post, target, source, offset):
    vm = pl.BlockSpec(memory_space=VMEM)
    return pl.pallas_call(
        near_kernel,
        out_shape=jax.ShapeDtypeStruct((4, BODIES, SLOTS), f32),
        in_specs=[vm] * 4,
        out_specs=vm,
        scratch_shapes=[VMEM((4, 128, 128), f32), VMEM((3, 128, 128), f32), VMEM((4, 128, 128), f32)],
        compiler_params=small(4),
        cost_estimate=pl.CostEstimate(flops=8 * 10**9, bytes_accessed=10**6, transcendentals=2 * 10**6),
        name="near",
    )(post, target, source, offset)


def field_kernel(counts_ref, left_ref, mt_ref, *rest):
    far_refs, rest = rest[:LEVELS], rest[LEVELS:]
    post_ref, near_ref, out_ref, src_ref, bt_ref, acc_ref, e_ref, f_ref = rest

    far = jnp.concatenate([r[...] for r in far_refs], axis=0)
    far = jnp.concatenate([far, jnp.zeros((32, 256), f32)], axis=0)
    parts = [mt_ref[...]]
    for q in range(2):
        block = far[q * 128 : q * 128 + 128, :]
        parts.append(jnp.concatenate([block[:, 0:128].T, block[:, 128:256].T[0 : ROWS - 128]], axis=0))
    sources = jnp.concatenate(parts, axis=1)
    high = sources.astype(bf16).astype(f32)
    high, low = high.astype(bf16), (sources - high).astype(bf16)
    src_ref[...] = jnp.concatenate([high, low], axis=1)

    def move(p, carry):
        counts = counts_ref[p]
        moved = dot(src_ref[...], jnp.concatenate([counts, jnp.zeros((32, 256), bf16), counts, jnp.zeros((32, 256), bf16)], axis=0))
        for k in range(2):
            bt_ref[pl.ds(2 * p + k, ROWS, stride=PITCH), :] = moved[:, k * 128 : k * 128 + 128]
        return carry

    lax.fori_loop(0, CLASSES // 2, move, 0, unroll=16)

    acc_ref[...] = jnp.zeros_like(acc_ref)

    def contract(jb, carry):
        right = [
            jnp.concatenate(split(bt_ref[pl.ds((jb * J_STEP + j) * PITCH, CLASSES), :]), axis=1)
            for j in range(J_STEP)
        ]
        acc_ref[...] += dot(left_ref[jb], jnp.concatenate(right, axis=0))
        return carry

    lax.fori_loop(0, J_BLOCKS, contract, 0, unroll=21)
    acc = acc_ref[...]
    e = (acc[I_ROWS:, 128:] + acc[I_ROWS:, :128]) + acc[:I_ROWS, 128:] + acc[:I_ROWS, :128]
    e_ref[...] = e[0:ROWS]

    present = jnp.where(post_ref[3, 0:1, :] > 0.0, 1.0, 0.0)

    def chunk(q, carry):
        rows = pl.ds(pl.multiple_of(q * 32, 32), 32)
        x, y, z = (post_ref[a, rows, :] for a in range(3))

        def coef(a, b, c):
            n = TERM[a, b, c]
            return jnp.broadcast_to(e_ref[n : n + 1, :] * NORM[a, b, c], (32, SLOTS))

        p = px = py = pz = None
        for a in range(ORDER, -1, -1):
            r = ry = rz = None
            for b in range(ORDER - a, -1, -1):
                top = ORDER - a - b
                v = coef(a, b, top)
                vz = None
                for c in range(top - 1, -1, -1):
                    vz = v if vz is None else vz * z + v
                    v = v * z + coef(a, b, c)
                if r is None:
                    r = v
                else:
                    ry = r if ry is None else ry * y + r
                    r = r * y + v
                    if vz is not None:
                        rz = vz if rz is None else rz * y + vz
            if p is None:
                p = r
            else:
                px = p if px is None else px * x + p
                p = p * x + r
                py = ry if py is None else py * x + ry
                pz = rz if pz is None else pz * x + rz
        for a, v in enumerate((p, -px, -py, -pz)):
            f_ref[a, rows, :] = (v + near_ref[a, rows, :]) * present
        return carry

    lax.fori_loop(0, BODIES // 32, chunk, 0)
    for a in range(4):
        out_ref[:, a, :] = f_ref[a].T


def field(counts, left, mt, far, post, near):
    vm = pl.BlockSpec(memory_space=VMEM)
    return pl.pallas_call(
        field_kernel,
        out_shape=jax.ShapeDtypeStruct((SLOTS, 4, BODIES), f32),
        in_specs=[vm] * (5 + LEVELS),
        out_specs=vm,
        scratch_shapes=[
            VMEM((ROWS, 768), bf16),
            VMEM((ROWS * PITCH, SLOTS), f32),
            VMEM((2 * I_ROWS, 256), f32),
            VMEM((ROWS, SLOTS), f32),
            VMEM((4, BODIES, SLOTS), f32),
        ],
        compiler_params=small(20),
        cost_estimate=pl.CostEstimate(flops=40 * 10**9, bytes_accessed=26 * 10**6, transcendentals=0),
        name="field",
    )(counts, left, mt, *far, post, near)


def body(
    positions,
    masses,
    owner,
    operators,
    m2l_target,
    far_source,
    local_source,
    export_slots,
    near_target,
    near_source,
    near_offset,
):
    axes = ("dom", "sub")
    devices = lax.axis_size(axes)
    lists, mine, sent = pack_tiles(owner, positions, masses, (m2l_target[0], far_source[0], local_source[0]))

    def swap(rows, k):
        return lax.ppermute(rows, "sub", [(i, i ^ k) for i in range(PEERS)])

    other = swap(sent, 4)
    counts, rows, done = count_pairs(*lists, operators)
    sent = merge(mine, other, done)
    pieces = [swap(sent[k - 1], k) for k in (1, 2, 3)]
    left, done = relay_operators(rows, sent[0])
    mt, post, exported = multipoles_of((mine, other, *pieces), export_slots, done)
    far = [
        lax.ppermute(rows, axes, [(i, i ^ (1 << level)) for i in range(devices)])
        for level, rows in enumerate(exported)
    ]
    near = near_field(post, near_target, near_source, near_offset)
    return field(counts, left, mt, far, post, near)


def solution(mesh):
    both = ("dom", "sub")
    in_specs = (
        P(both, None, None),
        P(both, None),
        P(both, None),
        P(),
        P(both, None, None, None),
        P(both, None, None, None),
        P(both, None, None),
        P(both, None, None),
        P(both, None),
        P(both, None),
        P(both, None),
    )
    out_specs = P(both, None, None)
    return jax.shard_map(body, mesh=mesh, in_specs=in_specs, out_specs=out_specs, check_vma=False)
```

```python
import functools

import jax
import jax.numpy as jnp
import numpy as np
from jax import lax
from jax.experimental import pallas as pl
from jax.experimental.pallas import tpu as pltpu
from jax.sharding import PartitionSpec as P

ORDER = 8
TERMS = 165
ROWS = 168
TERMS_PAD = ROWS
SOFT = 0.01
SLOTS = 128
PEERS = 8
CAP = SLOTS // PEERS
BODIES = 128
KEXP = 32
LEVELS = 7
CLASSES = 128
SOURCES = SLOTS + LEVELS * KEXP
f32 = jnp.float32
bf16 = jnp.bfloat16
f8 = jnp.float8_e4m3fn
VMEM = pltpu.VMEM
SMEM = pltpu.SMEM


def term_list():
    triples = []
    for degree in range(ORDER + 1):
        for a in range(degree, -1, -1):
            for b in range(degree - a, -1, -1):
                triples.append((a, b, degree - a - b))
    return {t: n for n, t in enumerate(triples)}


TERM = term_list()
NORM = {t: float(np.float32(np.sqrt(np.prod(2.0 * np.array(t) + 1.0)))) for t in TERM}


def small(mib):
    return pltpu.CompilerParams(vmem_limit_bytes=mib * 2**20)


def row(ref, n):
    return jnp.broadcast_to(ref[pl.ds(n, 1), :], (32, 128))


def in_hbm(x):
    return pltpu.with_memory_space_constraint(x, pltpu.HBM)


def iota(shape, axis):
    return lax.broadcasted_iota(jnp.int32, shape, axis)


def split(v):
    high = v.astype(bf16)
    return high, (v - high.astype(f32)).astype(bf16)


def dot(a, b):
    return jnp.dot(a, b, preferred_element_type=f32)


def dot_nt(a, b):
    return lax.dot_general(a, b, (((1,), (1,)), ((), ())), preferred_element_type=f32)


def dot_parts(a, b):
    high = a.astype(bf16).astype(f32)
    rest = a - high
    middle = rest.astype(bf16).astype(f32)
    parts = dot(jnp.concatenate([high, middle, rest - middle], axis=0).astype(bf16), b)
    n = a.shape[0]
    return (parts[2 * n :] + parts[n : 2 * n]) + parts[:n]


def pack_kernel(owner_hbm, pos_hbm, mass_hbm, tgt_hbm, far_hbm, local_hbm, *rest):
    list_refs, rest = rest[:3], rest[3:]
    out_refs, (owner_ref, pos_ref, mass_ref, sem, count_ref), slot_refs = rest[:2], rest[2:-4], rest[-4:]
    copies = [
        pltpu.make_async_copy(a, b, sem.at[k])
        for k, (a, b) in enumerate(((owner_hbm, owner_ref), (pos_hbm, pos_ref), (mass_hbm, mass_ref)))
    ]
    lists = [
        pltpu.make_async_copy(a, b, sem.at[3 + k])
        for k, (a, b) in enumerate(zip((tgt_hbm, far_hbm, local_hbm), list_refs))
    ]
    for c in copies + lists:
        c.start()
    for r in slot_refs:
        r[...] = jnp.zeros_like(r)
    for o in range(PEERS):
        count_ref[o] = 0
    me = lax.axis_index("sub")
    for c in copies:
        c.wait()

    def step(i, carry):
        o = owner_ref[0, i]
        rank = count_ref[o]
        count_ref[o] = rank + 1
        slot = (o ^ me) * CAP + rank
        for a in range(3):
            slot_refs[a][pl.ds(slot, 1), :] = pos_ref[a, pl.ds(i, 1), :]
        slot_refs[3][pl.ds(slot, 1), :] = mass_ref[pl.ds(i, 1), :]
        return carry

    lax.fori_loop(0, mass_ref.shape[0], step, 0)
    half = SLOTS // 2
    for k in range(2):
        for a in range(4):
            out_refs[k][:, a * BODIES : (a + 1) * BODIES] = slot_refs[a][k * half : (k + 1) * half, :]
    for c in lists:
        c.wait()


def pack_tiles(owner, positions, masses, lists):
    out = pl.pallas_call(
        pack_kernel,
        out_shape=[VMEM(x.shape, x.dtype) for x in lists]
        + [jax.ShapeDtypeStruct((SLOTS // 2, 4 * BODIES), f32)] * 2,
        in_specs=[pl.BlockSpec(memory_space=pltpu.HBM)] * 6,
        out_specs=[pl.BlockSpec(memory_space=VMEM)] * 5,
        scratch_shapes=[
            pltpu.SMEM((1, owner.shape[0]), jnp.int32),
            VMEM((3, owner.shape[0], BODIES), f32),
            VMEM((owner.shape[0], BODIES), f32),
            pltpu.SemaphoreType.DMA((6,)),
            pltpu.SMEM((PEERS,), jnp.int32),
        ]
        + [VMEM((SLOTS, BODIES), f32)] * 4,
        compiler_params=small(2),
        name="pack",
    )(*map(in_hbm, (owner.T, positions.transpose(1, 0, 2), masses, *lists)))
    return out[:3], out[3], out[4]


def merge_kernel(mine_ref, other_ref, after_ref, *out_refs):
    for q, ref in enumerate(out_refs, start=1):
        ref[0:CAP] = mine_ref[q * CAP : (q + 1) * CAP]
        ref[CAP : 2 * CAP] = other_ref[q * CAP : (q + 1) * CAP]


def merge(mine, other, after):
    vm = pl.BlockSpec(memory_space=VMEM)
    return pl.pallas_call(
        merge_kernel,
        out_shape=[jax.ShapeDtypeStruct((2 * CAP, 4 * BODIES), f32)] * 3,
        in_specs=[vm] * 3,
        out_specs=[vm] * 3,
        compiler_params=small(2),
        name="merge",
    )(mine, other, after)


I_STEP = 16
I_FULL = TERMS // I_STEP
PAIR_STEP = 32
I_ROWS = (I_FULL + 1) * I_STEP
J_STEP = 8
PITCH = CLASSES + 1
J_BLOCKS = ROWS // J_STEP


def operator_copy(op_hbm, buf_ref, sem, q):
    size = min(I_STEP, TERMS - q * I_STEP)
    return pltpu.make_async_copy(
        op_hbm.at[pl.ds(q * I_STEP, size)], buf_ref.at[q, pl.ds(0, size), pl.ds(0, TERMS)], sem.at[q]
    )


def count_kernel(tgt_ref, far_ref, local_ref, op_hbm, counts_ref, buf_ref, done_ref, tt_ref, st_ref, sem):
    for q in range(I_FULL + 1):
        operator_copy(op_hbm, buf_ref, sem, q).start()

    order = [7, 0, 1, 2, 3, 4, 5, 6]
    for pair in range(4):
        tgt, src = [], []
        for level in order[2 * pair : 2 * pair + 2]:
            tgt.append(tgt_ref[level].astype(f32))
            if level == 7:
                src.append(local_ref[...].astype(f32))
            else:
                offset = {0: SLOTS, 1: 0, 2: KEXP, 3: 0, 4: KEXP, 5: 0, 6: KEXP}[level]
                src.append((far_ref[level] + offset).astype(f32))
        tt_ref[pair] = jnp.concatenate(tgt, axis=0).T
        st_ref[pair] = jnp.concatenate(src, axis=0).T

    ids = iota((160, 128), 0).astype(f32).astype(bf16)

    def onehot(ref, part, c, first, size, total):
        row = jnp.broadcast_to(ref[part, pl.ds(c, 1), :].astype(bf16), (size, 128))
        hits = jnp.where(row == ids[0:size], jnp.ones((), bf16), jnp.zeros((), bf16))
        zeros = lambda n: [jnp.zeros((n, 128), bf16)] if n else []
        return jnp.concatenate(zeros(first) + [hits] + zeros(total - first - size), axis=0)

    def classes(p):
        for k in range(2):
            c = 2 * p + k
            for half, (first, size) in enumerate(((0, 224), (224, 128))):
                cut = 160 if half == 0 else 64
                target = jnp.concatenate([onehot(tt_ref, 2 * half + i, c, 0, 128, 128) for i in range(2)], axis=1)
                source = jnp.concatenate(
                    [
                        onehot(st_ref, 2 * half, c, 0, cut, size),
                        onehot(st_ref, 2 * half + 1, c, cut, size - cut, size),
                    ],
                    axis=1,
                )
                counts = dot_nt(source.astype(f8), target.astype(f8))
                counts_ref[p, first : first + size, k * 128 : k * 128 + 128] = counts.astype(bf16)

    def group(g, carry):
        for i in range(PAIR_STEP):
            classes(g * PAIR_STEP + i)
        return carry

    lax.fori_loop(0, CLASSES // 2 // PAIR_STEP, group, 0)
    done_ref[...] = jnp.zeros_like(done_ref)
    for q in range(I_FULL + 1):
        operator_copy(op_hbm, buf_ref, sem, q).wait()


def relay_kernel(buf_ref, after_ref, left_ref, done_ref):
    for j in range(TERMS, ROWS):
        left_ref[J_BLOCKS - 1, :, (j % J_STEP) * 128 : (j % J_STEP) * 128 + 128] = jnp.zeros((2 * I_ROWS, 128), bf16)

    def relay(q, carry):
        rows = buf_ref.at[q].reshape(I_STEP * TERMS_PAD, CLASSES)
        at = pl.multiple_of(q * I_STEP, I_STEP)
        for j in range(TERMS):
            v = rows[pl.ds(j, I_STEP, stride=TERMS_PAD), :]
            high, low = split(v)
            lanes = slice((j % J_STEP) * 128, (j % J_STEP) * 128 + 128)
            left_ref[j // J_STEP, pl.ds(at, I_STEP), lanes] = high
            left_ref[j // J_STEP, pl.ds(at + I_ROWS, I_STEP), lanes] = low
        return carry

    lax.fori_loop(0, I_FULL + 1, relay, 0)
    done_ref[...] = jnp.zeros_like(done_ref)


def count_pairs(m2l_target, far_source, local_source, operators):
    vm = pl.BlockSpec(memory_space=VMEM)
    return pl.pallas_call(
        count_kernel,
        out_shape=[
            VMEM((CLASSES // 2, SOURCES, 256), bf16),
            VMEM((I_FULL + 1, I_STEP, TERMS_PAD, CLASSES), f32),
            VMEM((8, 128), f32),
        ],
        in_specs=[vm] * 3 + [pl.BlockSpec(memory_space=pltpu.HBM)],
        out_specs=[vm] * 3,
        scratch_shapes=[
            VMEM((4, 128, 128), f32),
            VMEM((4, 128, 128), f32),
            pltpu.SemaphoreType.DMA((I_FULL + 1,)),
        ],
        compiler_params=small(4),
        cost_estimate=pl.CostEstimate(flops=6 * 10**9, bytes_accessed=14 * 10**6, transcendentals=0),
        name="counts",
    )(m2l_target, far_source, local_source, in_hbm(operators))


def relay_operators(rows, after):
    vm = pl.BlockSpec(memory_space=VMEM)
    return pl.pallas_call(
        relay_kernel,
        out_shape=[VMEM((J_BLOCKS, 2 * I_ROWS, J_STEP * CLASSES), bf16), VMEM((8, 128), f32)],
        in_specs=[vm] * 2,
        out_specs=[vm] * 2,
        compiler_params=small(4),
        cost_estimate=pl.CostEstimate(flops=4 * 10**9, bytes_accessed=10**6, transcendentals=0),
        name="relay",
    )(rows, after)


def multipole_kernel(*refs):
    (mine_ref, other_ref, *pieces), refs = refs[:5], refs[5:]
    slots_hbm, _, mt_ref, post_ref, *refs = refs
    exp_refs, (acc_ref, m_ref, rows_ref, slots_ref, sem, recv_ref) = refs[:LEVELS], refs[LEVELS:]
    slots_copy = pltpu.make_async_copy(slots_hbm, slots_ref, sem)
    slots_copy.start()
    me = lax.axis_index("sub")
    for k in range(PEERS):
        rows = pl.ds(pl.multiple_of((me ^ k) * CAP, CAP), CAP)
        if k % 4:
            piece, first = pieces[k % 4 - 1], k // 4 * CAP
        else:
            piece, first = (mine_ref, other_ref)[k // 4], 0
        for a in range(4):
            recv_ref[a, rows, :] = piece[first : first + CAP, a * BODIES : (a + 1) * BODIES]
    for a in range(4):
        post_ref[a] = recv_ref[a].T

    acc_ref[...] = jnp.zeros_like(acc_ref)

    def chunk(q, carry):
        rows = pl.ds(pl.multiple_of(q * 32, 32), 32)
        x, y, z, m = (post_ref[a, rows, :] for a in range(4))

        def fold(term, n):
            part = (term[0:8] + term[8:16]) + (term[16:24] + term[24:32])
            acc_ref[n] += part

        px = m
        for a in range(ORDER + 1):
            py = px
            for b in range(ORDER + 1 - a):
                pz = py
                for c in range(ORDER + 1 - a - b):
                    fold(pz, TERM[a, b, c])
                    if c < ORDER - a - b:
                        pz = pz * z
                if b < ORDER - a:
                    py = py * y
            if a < ORDER:
                px = px * x
        return carry

    lax.fori_loop(0, BODIES // 32, chunk, 0)
    mt_ref[TERMS - 5 :, :] = jnp.zeros((ROWS - TERMS + 5, SLOTS), f32)
    for (a, b, c), n in TERM.items():
        mt_ref[n : n + 1, :] = jnp.sum(acc_ref[n], axis=0, keepdims=True) * NORM[a, b, c]
    m_ref[0] = mt_ref[0:128, :].T
    m_ref[1] = jnp.concatenate([mt_ref[128:ROWS, :], jnp.zeros((256 - ROWS, SLOTS), f32)], axis=0).T
    slots_copy.wait()
    for level in range(LEVELS):

        def row(k, carry):
            slot = slots_ref[level, 0, k]
            for half in range(2):
                rows_ref[half, pl.ds(k, 1), :] = m_ref[half, pl.ds(slot, 1), :]
            return carry

        lax.fori_loop(0, KEXP, row, 0, unroll=8)
        for half in range(2):
            exp_refs[level][:, half * 128 : half * 128 + 128] = rows_ref[half]


def multipoles_of(pieces, export_slots, after):
    vm = pl.BlockSpec(memory_space=VMEM)
    out = pl.pallas_call(
        multipole_kernel,
        out_shape=[
            jax.ShapeDtypeStruct((ROWS, SLOTS), f32),
            jax.ShapeDtypeStruct((4, BODIES, SLOTS), f32),
        ]
        + [jax.ShapeDtypeStruct((KEXP, 256), f32)] * LEVELS,
        in_specs=[vm] * 5 + [pl.BlockSpec(memory_space=pltpu.HBM), vm],
        out_specs=[vm] * (2 + LEVELS),
        scratch_shapes=[
            pltpu.VMEM((TERMS, 8, SLOTS), f32),
            pltpu.VMEM((2, SLOTS, 128), f32),
            pltpu.VMEM((2, KEXP, 128), f32),
            pltpu.SMEM((LEVELS, 1, KEXP), jnp.int32),
            pltpu.SemaphoreType.DMA,
            VMEM((4, SLOTS, BODIES), f32),
        ],
        compiler_params=small(4),
        name="multipoles",
    )(*pieces, in_hbm(export_slots.transpose(1, 0, 2)), after)
    return out[0], out[1], out[2:]


def near_kernel(post_ref, tgt_ref, src_ref, off_ref, near_ref, s_ref, t_ref, a_ref):
    row = iota((128, 128), 0)
    pick_s = jnp.where(src_ref[...] == row, 1.0, 0.0)
    pick_t = jnp.where(tgt_ref[...] == row, 1.0, 0.0)
    k = off_ref[...].astype(f32)
    one, zero = jnp.ones_like(k), jnp.zeros_like(k)
    kx = jnp.where(k >= 9.0, one, zero) + jnp.where(k >= 18.0, one, zero)
    k = k - 9.0 * kx
    ky = jnp.where(k >= 3.0, one, zero) + jnp.where(k >= 6.0, one, zero)
    kz = k - 3.0 * ky
    picks = jnp.concatenate([pick_s, pick_t], axis=1).astype(bf16)
    shifts = (kx, ky, kz)
    for a in range(4):
        picked = dot_parts(post_ref[a], picks)
        s_ref[a] = picked[:, 0:128] + 2.0 * (shifts[a] - 1.0) if a < 3 else picked[:, 0:128]
        if a < 3:
            t_ref[a] = picked[:, 128:256]

    def chunk(q, carry):
        rows = pl.ds(pl.multiple_of(q * 32, 32), 32)
        tx, ty, tz = (t_ref[a, rows, :] for a in range(3))

        def source(j, state):
            p, ax, ay, az = state
            sx, sy, sz, m = (s_ref[a, pl.ds(j, 1), :] for a in range(4))
            rx, ry, rz = sx - tx, sy - ty, sz - tz
            inv = lax.rsqrt(rx * rx + ry * ry + rz * rz + SOFT)
            w = m * inv
            p = p - w
            w = w * (inv * inv)
            return p, ax + rx * w, ay + ry * w, az + rz * w

        done = lax.fori_loop(0, 128, source, (jnp.zeros((32, 128), f32),) * 4, unroll=32)
        for a in range(4):
            a_ref[a, rows, :] = done[a]
        return carry

    lax.fori_loop(0, 4, chunk, 0)
    into = pick_t.T.astype(bf16)
    for a in range(4):
        near_ref[a] = dot_parts(a_ref[a], into)


def near_field(post, target, source, offset):
    vm = pl.BlockSpec(memory_space=VMEM)
    return pl.pallas_call(
        near_kernel,
        out_shape=jax.ShapeDtypeStruct((4, BODIES, SLOTS), f32),
        in_specs=[vm] * 4,
        out_specs=vm,
        scratch_shapes=[VMEM((4, 128, 128), f32), VMEM((3, 128, 128), f32), VMEM((4, 128, 128), f32)],
        compiler_params=small(4),
        cost_estimate=pl.CostEstimate(flops=8 * 10**9, bytes_accessed=10**6, transcendentals=2 * 10**6),
        name="near",
    )(post, target, source, offset)


def field_kernel(counts_ref, left_ref, mt_ref, *rest):
    far_refs, rest = rest[:LEVELS], rest[LEVELS:]
    post_ref, near_ref, norm_ref, out_ref, src_ref, bt_ref, acc_ref, e_ref, f_ref = rest

    far = jnp.concatenate([r[...] for r in far_refs], axis=0)
    far = jnp.concatenate([far, jnp.zeros((32, 256), f32)], axis=0)
    parts = [mt_ref[...]]
    for q in range(2):
        block = far[q * 128 : q * 128 + 128, :]
        parts.append(jnp.concatenate([block[:, 0:128].T, block[:, 128:256].T[0 : ROWS - 128]], axis=0))
    sources = jnp.concatenate(parts, axis=1)
    high = sources.astype(bf16).astype(f32)
    high, low = high.astype(bf16), (sources - high).astype(bf16)
    src_ref[...] = jnp.concatenate([high, low], axis=1)

    def move(p, carry):
        counts = counts_ref[p]
        moved = dot(src_ref[...], jnp.concatenate([counts, jnp.zeros((32, 256), bf16), counts, jnp.zeros((32, 256), bf16)], axis=0))
        for k in range(2):
            bt_ref[pl.ds(2 * p + k, ROWS, stride=PITCH), :] = moved[:, k * 128 : k * 128 + 128]
        return carry

    lax.fori_loop(0, CLASSES // 2, move, 0, unroll=64)

    acc_ref[...] = jnp.zeros_like(acc_ref)

    def contract(jb, carry):
        right = [
            jnp.concatenate(split(bt_ref[pl.ds((jb * J_STEP + j) * PITCH, CLASSES), :]), axis=1)
            for j in range(J_STEP)
        ]
        acc_ref[...] += dot(left_ref[jb], jnp.concatenate(right, axis=0))
        return carry

    lax.fori_loop(0, J_BLOCKS, contract, 0, unroll=21)
    acc = acc_ref[...]
    e = (acc[I_ROWS:, 128:] + acc[I_ROWS:, :128]) + acc[:I_ROWS, 128:] + acc[:I_ROWS, :128]
    e_ref[...] = e[0:ROWS] * norm_ref[...]

    present = jnp.where(post_ref[3, 0:1, :] > 0.0, 1.0, 0.0)

    def chunk(q, carry):
        rows = pl.ds(pl.multiple_of(q * 32, 32), 32)
        x, y, z = (post_ref[a, rows, :] for a in range(3))

        def coef(a, b, c):
            return row(e_ref, TERM[a, b, c])

        p = px = py = pz = None
        for a in range(ORDER, -1, -1):
            r = ry = rz = None
            for b in range(ORDER - a, -1, -1):
                top = ORDER - a - b
                v = coef(a, b, top)
                vz = None
                for c in range(top - 1, -1, -1):
                    vz = v if vz is None else vz * z + v
                    v = v * z + coef(a, b, c)
                if r is None:
                    r = v
                else:
                    ry = r if ry is None else ry * y + r
                    r = r * y + v
                    if vz is not None:
                        rz = vz if rz is None else rz * y + vz
            if p is None:
                p = r
            else:
                px = p if px is None else px * x + p
                p = p * x + r
                py = ry if py is None else py * x + ry
                pz = rz if pz is None else pz * x + rz
        for a, v in enumerate((p, -px, -py, -pz)):
            f_ref[a, rows, :] = (v + near_ref[a, rows, :]) * present
        return carry

    lax.fori_loop(0, BODIES // 32, chunk, 0)
    for a in range(4):
        out_ref[:, a, :] = f_ref[a].T


def field(counts, left, mt, far, post, near):
    vm = pl.BlockSpec(memory_space=VMEM)
    norms = np.zeros((ROWS, SLOTS), np.float32)
    for t, n in TERM.items():
        norms[n] = NORM[t]
    return pl.pallas_call(
        field_kernel,
        out_shape=jax.ShapeDtypeStruct((SLOTS, 4, BODIES), f32),
        in_specs=[vm] * (6 + LEVELS),
        out_specs=vm,
        scratch_shapes=[
            VMEM((ROWS, 768), bf16),
            VMEM((ROWS * PITCH, SLOTS), f32),
            VMEM((2 * I_ROWS, 256), f32),
            VMEM((ROWS, SLOTS), f32),
            VMEM((4, BODIES, SLOTS), f32),
        ],
        compiler_params=small(20),
        cost_estimate=pl.CostEstimate(flops=40 * 10**9, bytes_accessed=26 * 10**6, transcendentals=0),
        name="field",
    )(counts, left, mt, *far, post, near, norms)


def body(
    positions,
    masses,
    owner,
    operators,
    m2l_target,
    far_source,
    local_source,
    export_slots,
    near_target,
    near_source,
    near_offset,
):
    axes = ("dom", "sub")
    devices = lax.axis_size(axes)
    lists, mine, sent = pack_tiles(owner, positions, masses, (m2l_target[0], far_source[0], local_source[0]))

    def swap(rows, k):
        return lax.ppermute(rows, "sub", [(i, i ^ k) for i in range(PEERS)])

    other = swap(sent, 4)
    counts, rows, done = count_pairs(*lists, operators)
    sent = merge(mine, other, done)
    pieces = [swap(sent[k - 1], k) for k in (1, 2, 3)]
    left, done = relay_operators(rows, sent[0])
    mt, post, exported = multipoles_of((mine, other, *pieces), export_slots, done)
    far = [
        lax.ppermute(rows, axes, [(i, i ^ (1 << level)) for i in range(devices)])
        for level, rows in enumerate(exported)
    ]
    near = near_field(post, near_target, near_source, near_offset)
    return field(counts, left, mt, far, post, near)


def solution(mesh):
    both = ("dom", "sub")
    in_specs = (
        P(both, None, None),
        P(both, None),
        P(both, None),
        P(),
        P(both, None, None, None),
        P(both, None, None, None),
        P(both, None, None),
        P(both, None, None),
        P(both, None),
        P(both, None),
        P(both, None),
    )
    out_specs = P(both, None, None)
    return jax.shard_map(body, mesh=mesh, in_specs=in_specs, out_specs=out_specs, check_vma=False)
```

```python
import functools

import jax
import jax.numpy as jnp
import numpy as np
from jax import lax
from jax.experimental import pallas as pl
from jax.experimental.pallas import tpu as pltpu
from jax.sharding import PartitionSpec as P

ORDER = 8
TERMS = 165
ROWS = 168
TERMS_PAD = ROWS
SOFT = 0.01
SLOTS = 128
PEERS = 8
CAP = SLOTS // PEERS
BODIES = 128
KEXP = 32
LEVELS = 7
CLASSES = 128
SOURCES = SLOTS + LEVELS * KEXP
f32 = jnp.float32
bf16 = jnp.bfloat16
f8 = jnp.float8_e4m3fn
VMEM = pltpu.VMEM
SMEM = pltpu.SMEM


def term_list():
    triples = []
    for degree in range(ORDER + 1):
        for a in range(degree, -1, -1):
            for b in range(degree - a, -1, -1):
                triples.append((a, b, degree - a - b))
    return {t: n for n, t in enumerate(triples)}


TERM = term_list()
NORM = {t: float(np.float32(np.sqrt(np.prod(2.0 * np.array(t) + 1.0)))) for t in TERM}


def norm_rows():
    norms = np.zeros((ROWS, SLOTS), np.float32)
    for t, n in TERM.items():
        norms[n] = NORM[t]
    return norms


def small(mib):
    return pltpu.CompilerParams(vmem_limit_bytes=mib * 2**20)


def row(ref, n):
    return jnp.broadcast_to(ref[pl.ds(n, 1), :], (32, 128))


def in_hbm(x):
    return pltpu.with_memory_space_constraint(x, pltpu.HBM)


def iota(shape, axis):
    return lax.broadcasted_iota(jnp.int32, shape, axis)


def split(v):
    high = v.astype(bf16)
    return high, (v - high.astype(f32)).astype(bf16)


def dot(a, b):
    return jnp.dot(a, b, preferred_element_type=f32)


def dot_nt(a, b):
    return lax.dot_general(a, b, (((1,), (1,)), ((), ())), preferred_element_type=f32)


def dot_parts(a, b):
    high = a.astype(bf16).astype(f32)
    rest = a - high
    middle = rest.astype(bf16).astype(f32)
    parts = dot(jnp.concatenate([high, middle, rest - middle], axis=0).astype(bf16), b)
    n = a.shape[0]
    return (parts[2 * n :] + parts[n : 2 * n]) + parts[:n]


def pack_kernel(owner_hbm, pos_hbm, mass_hbm, tgt_hbm, far_hbm, local_hbm, slots_hbm, *rest):
    list_refs, rest = rest[:4], rest[4:]
    out_refs, (owner_ref, pos_ref, mass_ref, sem, count_ref), slot_refs = rest[:2], rest[2:-4], rest[-4:]
    copies = [
        pltpu.make_async_copy(a, b, sem.at[k])
        for k, (a, b) in enumerate(((owner_hbm, owner_ref), (pos_hbm, pos_ref), (mass_hbm, mass_ref)))
    ]
    lists = [
        pltpu.make_async_copy(a, b, sem.at[3 + k])
        for k, (a, b) in enumerate(zip((tgt_hbm, far_hbm, local_hbm, slots_hbm), list_refs))
    ]
    for c in copies + lists:
        c.start()
    for r in slot_refs:
        r[...] = jnp.zeros_like(r)
    for o in range(PEERS):
        count_ref[o] = 0
    me = lax.axis_index("sub")
    for c in copies:
        c.wait()

    def step(i, carry):
        o = owner_ref[0, i]
        rank = count_ref[o]
        count_ref[o] = rank + 1
        slot = (o ^ me) * CAP + rank
        for a in range(3):
            slot_refs[a][pl.ds(slot, 1), :] = pos_ref[a, pl.ds(i, 1), :]
        slot_refs[3][pl.ds(slot, 1), :] = mass_ref[pl.ds(i, 1), :]
        return carry

    lax.fori_loop(0, mass_ref.shape[0], step, 0)
    half = SLOTS // 2
    for k in range(2):
        for a in range(4):
            out_refs[k][:, a * BODIES : (a + 1) * BODIES] = slot_refs[a][k * half : (k + 1) * half, :]
    for c in lists:
        c.wait()


def pack_tiles(owner, positions, masses, lists):
    out = pl.pallas_call(
        pack_kernel,
        out_shape=[VMEM(x.shape, x.dtype) for x in lists]
        + [jax.ShapeDtypeStruct((SLOTS // 2, 4 * BODIES), f32)] * 2,
        in_specs=[pl.BlockSpec(memory_space=pltpu.HBM)] * 7,
        out_specs=[pl.BlockSpec(memory_space=VMEM)] * 6,
        scratch_shapes=[
            pltpu.SMEM((1, owner.shape[0]), jnp.int32),
            VMEM((3, owner.shape[0], BODIES), f32),
            VMEM((owner.shape[0], BODIES), f32),
            pltpu.SemaphoreType.DMA((7,)),
            pltpu.SMEM((PEERS,), jnp.int32),
        ]
        + [VMEM((SLOTS, BODIES), f32)] * 4,
        compiler_params=small(2),
        name="pack",
    )(*map(in_hbm, (owner.T, positions.transpose(1, 0, 2), masses, *lists)))
    return out[:4], out[4], out[5]


def merge_kernel(mine_ref, other_ref, after_ref, *out_refs):
    for q, ref in enumerate(out_refs, start=1):
        ref[0:CAP] = mine_ref[q * CAP : (q + 1) * CAP]
        ref[CAP : 2 * CAP] = other_ref[q * CAP : (q + 1) * CAP]


def merge(mine, other, after):
    vm = pl.BlockSpec(memory_space=VMEM)
    return pl.pallas_call(
        merge_kernel,
        out_shape=[jax.ShapeDtypeStruct((2 * CAP, 4 * BODIES), f32)] * 3,
        in_specs=[vm] * 3,
        out_specs=[vm] * 3,
        compiler_params=small(2),
        name="merge",
    )(mine, other, after)


I_STEP = 16
I_FULL = TERMS // I_STEP
PAIR_STEP = 32
I_ROWS = (I_FULL + 1) * I_STEP
J_STEP = 8
PITCH = CLASSES + 1
J_BLOCKS = ROWS // J_STEP


def operator_copy(op_hbm, buf_ref, sem, q):
    size = min(I_STEP, TERMS - q * I_STEP)
    return pltpu.make_async_copy(
        op_hbm.at[pl.ds(q * I_STEP, size)], buf_ref.at[q, pl.ds(0, size), pl.ds(0, TERMS)], sem.at[q]
    )


def count_kernel(tgt_ref, far_ref, local_ref, op_hbm, counts_ref, buf_ref, done_ref, tt_ref, st_ref, sem):
    for q in range(I_FULL + 1):
        operator_copy(op_hbm, buf_ref, sem, q).start()

    order = [7, 0, 1, 2, 3, 4, 5, 6]
    for pair in range(4):
        tgt, src = [], []
        for level in order[2 * pair : 2 * pair + 2]:
            tgt.append(tgt_ref[level].astype(f32))
            if level == 7:
                src.append(local_ref[...].astype(f32))
            else:
                offset = {0: SLOTS, 1: 0, 2: KEXP, 3: 0, 4: KEXP, 5: 0, 6: KEXP}[level]
                src.append((far_ref[level] + offset).astype(f32))
        tt_ref[pair] = jnp.concatenate(tgt, axis=0).T
        st_ref[pair] = jnp.concatenate(src, axis=0).T

    ids = iota((160, 128), 0).astype(f32).astype(bf16)

    def onehot(ref, part, c, first, size, total):
        row = jnp.broadcast_to(ref[part, pl.ds(c, 1), :].astype(bf16), (size, 128))
        hits = jnp.where(row == ids[0:size], jnp.ones((), bf16), jnp.zeros((), bf16))
        zeros = lambda n: [jnp.zeros((n, 128), bf16)] if n else []
        return jnp.concatenate(zeros(first) + [hits] + zeros(total - first - size), axis=0)

    def classes(p):
        for k in range(2):
            c = 2 * p + k
            for half, (first, size) in enumerate(((0, 224), (224, 128))):
                cut = 160 if half == 0 else 64
                target = jnp.concatenate([onehot(tt_ref, 2 * half + i, c, 0, 128, 128) for i in range(2)], axis=1)
                source = jnp.concatenate(
                    [
                        onehot(st_ref, 2 * half, c, 0, cut, size),
                        onehot(st_ref, 2 * half + 1, c, cut, size - cut, size),
                    ],
                    axis=1,
                )
                counts = dot_nt(source.astype(f8), target.astype(f8))
                counts_ref[p, first : first + size, k * 128 : k * 128 + 128] = counts.astype(bf16)

    def group(g, carry):
        for i in range(PAIR_STEP):
            classes(g * PAIR_STEP + i)
        return carry

    lax.fori_loop(0, CLASSES // 2 // PAIR_STEP, group, 0)
    done_ref[...] = jnp.zeros_like(done_ref)
    for q in range(I_FULL + 1):
        operator_copy(op_hbm, buf_ref, sem, q).wait()


def relay_kernel(buf_ref, after_ref, left_ref, done_ref):
    for j in range(TERMS, ROWS):
        left_ref[J_BLOCKS - 1, :, (j % J_STEP) * 128 : (j % J_STEP) * 128 + 128] = jnp.zeros((2 * I_ROWS, 128), bf16)

    def relay(q, carry):
        rows = buf_ref.at[q].reshape(I_STEP * TERMS_PAD, CLASSES)
        at = pl.multiple_of(q * I_STEP, I_STEP)
        for j in range(TERMS):
            v = rows[pl.ds(j, I_STEP, stride=TERMS_PAD), :]
            high, low = split(v)
            lanes = slice((j % J_STEP) * 128, (j % J_STEP) * 128 + 128)
            left_ref[j // J_STEP, pl.ds(at, I_STEP), lanes] = high
            left_ref[j // J_STEP, pl.ds(at + I_ROWS, I_STEP), lanes] = low
        return carry

    lax.fori_loop(0, I_FULL + 1, relay, 0)
    done_ref[...] = jnp.zeros_like(done_ref)


def count_pairs(m2l_target, far_source, local_source, operators):
    vm = pl.BlockSpec(memory_space=VMEM)
    return pl.pallas_call(
        count_kernel,
        out_shape=[
            VMEM((CLASSES // 2, SOURCES, 256), bf16),
            VMEM((I_FULL + 1, I_STEP, TERMS_PAD, CLASSES), f32),
            VMEM((8, 128), f32),
        ],
        in_specs=[vm] * 3 + [pl.BlockSpec(memory_space=pltpu.HBM)],
        out_specs=[vm] * 3,
        scratch_shapes=[
            VMEM((4, 128, 128), f32),
            VMEM((4, 128, 128), f32),
            pltpu.SemaphoreType.DMA((I_FULL + 1,)),
        ],
        compiler_params=small(4),
        cost_estimate=pl.CostEstimate(flops=6 * 10**9, bytes_accessed=14 * 10**6, transcendentals=0),
        name="counts",
    )(m2l_target, far_source, local_source, in_hbm(operators))


def relay_operators(rows, after):
    vm = pl.BlockSpec(memory_space=VMEM)
    return pl.pallas_call(
        relay_kernel,
        out_shape=[VMEM((J_BLOCKS, 2 * I_ROWS, J_STEP * CLASSES), bf16), VMEM((8, 128), f32)],
        in_specs=[vm] * 2,
        out_specs=[vm] * 2,
        compiler_params=small(4),
        cost_estimate=pl.CostEstimate(flops=4 * 10**9, bytes_accessed=10**6, transcendentals=0),
        name="relay",
    )(rows, after)


def multipole_kernel(*refs):
    (mine_ref, other_ref, *pieces), refs = refs[:5], refs[5:]
    slots_hbm, _, norm_ref, mt_ref, post_ref, *refs = refs
    exp_refs, (acc_ref, m_ref, rows_ref, slots_ref, sem, recv_ref) = refs[:LEVELS], refs[LEVELS:]
    slots_copy = pltpu.make_async_copy(slots_hbm, slots_ref, sem)
    slots_copy.start()
    me = lax.axis_index("sub")
    for k in range(PEERS):
        rows = pl.ds(pl.multiple_of((me ^ k) * CAP, CAP), CAP)
        if k % 4:
            piece, first = pieces[k % 4 - 1], k // 4 * CAP
        else:
            piece, first = (mine_ref, other_ref)[k // 4], 0
        for a in range(4):
            recv_ref[a, rows, :] = piece[first : first + CAP, a * BODIES : (a + 1) * BODIES]
    for a in range(4):
        post_ref[a] = recv_ref[a].T

    acc_ref[...] = jnp.zeros_like(acc_ref)

    def chunk(q, carry):
        rows = pl.ds(pl.multiple_of(q * 32, 32), 32)
        x, y, z, m = (post_ref[a, rows, :] for a in range(4))

        def fold(term, n):
            part = (term[0:8] + term[8:16]) + (term[16:24] + term[24:32])
            acc_ref[n] += part

        px = m
        for a in range(ORDER + 1):
            py = px
            for b in range(ORDER + 1 - a):
                pz = py
                for c in range(ORDER + 1 - a - b):
                    fold(pz, TERM[a, b, c])
                    if c < ORDER - a - b:
                        pz = pz * z
                if b < ORDER - a:
                    py = py * y
            if a < ORDER:
                px = px * x
        return carry

    lax.fori_loop(0, BODIES // 32, chunk, 0)
    parts = acc_ref.reshape(ROWS * 8, SLOTS)
    for n in range(0, ROWS, 8):
        v = [parts[pl.ds(8 * n + k, 8, stride=8), :] for k in range(8)]
        total = ((v[0] + v[1]) + (v[2] + v[3])) + ((v[4] + v[5]) + (v[6] + v[7]))
        mt_ref[n : n + 8, :] = total * norm_ref[n : n + 8, :]
    m_ref[0] = mt_ref[0:128, :].T
    m_ref[1] = jnp.concatenate([mt_ref[128:ROWS, :], jnp.zeros((256 - ROWS, SLOTS), f32)], axis=0).T
    slots_copy.wait()
    for level in range(LEVELS):

        def row(k, carry):
            slot = slots_ref[level, 0, k]
            for half in range(2):
                rows_ref[half, pl.ds(k, 1), :] = m_ref[half, pl.ds(slot, 1), :]
            return carry

        lax.fori_loop(0, KEXP, row, 0, unroll=32)
        for half in range(2):
            exp_refs[level][:, half * 128 : half * 128 + 128] = rows_ref[half]


def multipoles_of(pieces, export_slots, after):
    vm = pl.BlockSpec(memory_space=VMEM)
    out = pl.pallas_call(
        multipole_kernel,
        out_shape=[
            jax.ShapeDtypeStruct((ROWS, SLOTS), f32),
            jax.ShapeDtypeStruct((4, BODIES, SLOTS), f32),
        ]
        + [jax.ShapeDtypeStruct((KEXP, 256), f32)] * LEVELS,
        in_specs=[vm] * 8,
        out_specs=[vm] * (2 + LEVELS),
        scratch_shapes=[
            pltpu.VMEM((ROWS, 8, SLOTS), f32),
            pltpu.VMEM((2, SLOTS, 128), f32),
            pltpu.VMEM((2, KEXP, 128), f32),
            pltpu.SMEM((LEVELS, 1, KEXP), jnp.int32),
            pltpu.SemaphoreType.DMA,
            VMEM((4, SLOTS, BODIES), f32),
        ],
        compiler_params=small(4),
        name="multipoles",
    )(*pieces, export_slots, after, norm_rows())
    return out[0], out[1], out[2:]


def near_kernel(post_ref, tgt_ref, src_ref, off_ref, near_ref, s_ref, t_ref, a_ref):
    row = iota((128, 128), 0)
    pick_s = jnp.where(src_ref[...] == row, 1.0, 0.0)
    pick_t = jnp.where(tgt_ref[...] == row, 1.0, 0.0)
    k = off_ref[...].astype(f32)
    one, zero = jnp.ones_like(k), jnp.zeros_like(k)
    kx = jnp.where(k >= 9.0, one, zero) + jnp.where(k >= 18.0, one, zero)
    k = k - 9.0 * kx
    ky = jnp.where(k >= 3.0, one, zero) + jnp.where(k >= 6.0, one, zero)
    kz = k - 3.0 * ky
    picks = jnp.concatenate([pick_s, pick_t], axis=1).astype(bf16)
    shifts = (kx, ky, kz)
    for a in range(4):
        picked = dot_parts(post_ref[a], picks)
        s_ref[a] = picked[:, 0:128] + 2.0 * (shifts[a] - 1.0) if a < 3 else picked[:, 0:128]
        if a < 3:
            t_ref[a] = picked[:, 128:256]

    def chunk(q, carry):
        rows = pl.ds(pl.multiple_of(q * 32, 32), 32)
        tx, ty, tz = (t_ref[a, rows, :] for a in range(3))

        def source(j, state):
            p, ax, ay, az = state
            sx, sy, sz, m = (s_ref[a, pl.ds(j, 1), :] for a in range(4))
            rx, ry, rz = sx - tx, sy - ty, sz - tz
            inv = lax.rsqrt(rx * rx + ry * ry + rz * rz + SOFT)
            w = m * inv
            p = p - w
            w = w * (inv * inv)
            return p, ax + rx * w, ay + ry * w, az + rz * w

        done = lax.fori_loop(0, 128, source, (jnp.zeros((32, 128), f32),) * 4, unroll=32)
        for a in range(4):
            a_ref[a, rows, :] = done[a]
        return carry

    lax.fori_loop(0, 4, chunk, 0)
    into = pick_t.T.astype(bf16)
    for a in range(4):
        near_ref[a] = dot_parts(a_ref[a], into)


def near_field(post, target, source, offset):
    vm = pl.BlockSpec(memory_space=VMEM)
    return pl.pallas_call(
        near_kernel,
        out_shape=jax.ShapeDtypeStruct((4, BODIES, SLOTS), f32),
        in_specs=[vm] * 4,
        out_specs=vm,
        scratch_shapes=[VMEM((4, 128, 128), f32), VMEM((3, 128, 128), f32), VMEM((4, 128, 128), f32)],
        compiler_params=small(4),
        cost_estimate=pl.CostEstimate(flops=8 * 10**9, bytes_accessed=10**6, transcendentals=2 * 10**6),
        name="near",
    )(post, target, source, offset)


def field_kernel(counts_ref, left_ref, mt_ref, *rest):
    far_refs, rest = rest[:LEVELS], rest[LEVELS:]
    post_ref, near_ref, norm_ref, out_ref, src_ref, bt_ref, acc_ref, e_ref, f_ref = rest

    far = jnp.concatenate([r[...] for r in far_refs], axis=0)
    far = jnp.concatenate([far, jnp.zeros((32, 256), f32)], axis=0)
    parts = [mt_ref[...]]
    for q in range(2):
        block = far[q * 128 : q * 128 + 128, :]
        parts.append(jnp.concatenate([block[:, 0:128].T, block[:, 128:256].T[0 : ROWS - 128]], axis=0))
    sources = jnp.concatenate(parts, axis=1)
    high = sources.astype(bf16).astype(f32)
    high, low = high.astype(bf16), (sources - high).astype(bf16)
    src_ref[...] = jnp.concatenate([high, low], axis=1)

    def move(p, carry):
        counts = counts_ref[p]
        moved = dot(src_ref[...], jnp.concatenate([counts, jnp.zeros((32, 256), bf16), counts, jnp.zeros((32, 256), bf16)], axis=0))
        for k in range(2):
            bt_ref[pl.ds(2 * p + k, ROWS, stride=PITCH), :] = moved[:, k * 128 : k * 128 + 128]
        return carry

    lax.fori_loop(0, CLASSES // 2, move, 0, unroll=64)

    acc_ref[...] = jnp.zeros_like(acc_ref)

    def contract(jb, carry):
        right = [
            jnp.concatenate(split(bt_ref[pl.ds((jb * J_STEP + j) * PITCH, CLASSES), :]), axis=1)
            for j in range(J_STEP)
        ]
        acc_ref[...] += dot(left_ref[jb], jnp.concatenate(right, axis=0))
        return carry

    lax.fori_loop(0, J_BLOCKS, contract, 0, unroll=21)
    acc = acc_ref[...]
    e = (acc[I_ROWS:, 128:] + acc[I_ROWS:, :128]) + acc[:I_ROWS, 128:] + acc[:I_ROWS, :128]
    e_ref[...] = e[0:ROWS] * norm_ref[...]

    present = jnp.where(post_ref[3, 0:1, :] > 0.0, 1.0, 0.0)

    def chunk(q, carry):
        rows = pl.ds(pl.multiple_of(q * 32, 32), 32)
        x, y, z = (post_ref[a, rows, :] for a in range(3))

        def coef(a, b, c):
            return row(e_ref, TERM[a, b, c])

        p = px = py = pz = None
        for a in range(ORDER, -1, -1):
            r = ry = rz = None
            for b in range(ORDER - a, -1, -1):
                top = ORDER - a - b
                v = coef(a, b, top)
                vz = None
                for c in range(top - 1, -1, -1):
                    vz = v if vz is None else vz * z + v
                    v = v * z + coef(a, b, c)
                if r is None:
                    r = v
                else:
                    ry = r if ry is None else ry * y + r
                    r = r * y + v
                    if vz is not None:
                        rz = vz if rz is None else rz * y + vz
            if p is None:
                p = r
            else:
                px = p if px is None else px * x + p
                p = p * x + r
                py = ry if py is None else py * x + ry
                pz = rz if pz is None else pz * x + rz
        for a, v in enumerate((p, -px, -py, -pz)):
            f_ref[a, rows, :] = (v + near_ref[a, rows, :]) * present
        return carry

    lax.fori_loop(0, BODIES // 32, chunk, 0)
    for a in range(4):
        out_ref[:, a, :] = f_ref[a].T


def field(counts, left, mt, far, post, near):
    vm = pl.BlockSpec(memory_space=VMEM)
    return pl.pallas_call(
        field_kernel,
        out_shape=jax.ShapeDtypeStruct((SLOTS, 4, BODIES), f32),
        in_specs=[vm] * (6 + LEVELS),
        out_specs=vm,
        scratch_shapes=[
            VMEM((ROWS, 768), bf16),
            VMEM((ROWS * PITCH, SLOTS), f32),
            VMEM((2 * I_ROWS, 256), f32),
            VMEM((ROWS, SLOTS), f32),
            VMEM((4, BODIES, SLOTS), f32),
        ],
        compiler_params=small(20),
        cost_estimate=pl.CostEstimate(flops=40 * 10**9, bytes_accessed=26 * 10**6, transcendentals=0),
        name="field",
    )(counts, left, mt, *far, post, near, norm_rows())


def body(
    positions,
    masses,
    owner,
    operators,
    m2l_target,
    far_source,
    local_source,
    export_slots,
    near_target,
    near_source,
    near_offset,
):
    axes = ("dom", "sub")
    devices = lax.axis_size(axes)
    lists = (m2l_target[0], far_source[0], local_source[0], export_slots.transpose(1, 0, 2))
    (*lists, exports), mine, sent = pack_tiles(owner, positions, masses, lists)

    def swap(rows, k):
        return lax.ppermute(rows, "sub", [(i, i ^ k) for i in range(PEERS)])

    other = swap(sent, 4)
    counts, rows, done = count_pairs(*lists, operators)
    sent = merge(mine, other, done)
    pieces = [swap(sent[k - 1], k) for k in (1, 2, 3)]
    left, done = relay_operators(rows, sent[0])
    mt, post, exported = multipoles_of((mine, other, *pieces), exports, done)
    far = [
        lax.ppermute(rows, axes, [(i, i ^ (1 << level)) for i in range(devices)])
        for level, rows in enumerate(exported)
    ]
    near = near_field(post, near_target, near_source, near_offset)
    return field(counts, left, mt, far, post, near)


def solution(mesh):
    both = ("dom", "sub")
    in_specs = (
        P(both, None, None),
        P(both, None),
        P(both, None),
        P(),
        P(both, None, None, None),
        P(both, None, None, None),
        P(both, None, None),
        P(both, None, None),
        P(both, None),
        P(both, None),
        P(both, None),
    )
    out_specs = P(both, None, None)
    return jax.shard_map(body, mesh=mesh, in_specs=in_specs, out_specs=out_specs, check_vma=False)
```

```python
import functools

import jax
import jax.numpy as jnp
import numpy as np
from jax import lax
from jax.experimental import pallas as pl
from jax.experimental.pallas import tpu as pltpu
from jax.sharding import PartitionSpec as P

ORDER = 8
TERMS = 165
ROWS = 168
TERMS_PAD = ROWS
SOFT = 0.01
SLOTS = 128
PEERS = 8
CAP = SLOTS // PEERS
BODIES = 128
KEXP = 32
LEVELS = 7
CLASSES = 128
SOURCES = SLOTS + LEVELS * KEXP
f32 = jnp.float32
bf16 = jnp.bfloat16
f8 = jnp.float8_e4m3fn
VMEM = pltpu.VMEM
SMEM = pltpu.SMEM


def term_list():
    triples = []
    for degree in range(ORDER + 1):
        for a in range(degree, -1, -1):
            for b in range(degree - a, -1, -1):
                triples.append((a, b, degree - a - b))
    return {t: n for n, t in enumerate(triples)}


TERM = term_list()
NORM = {t: float(np.float32(np.sqrt(np.prod(2.0 * np.array(t) + 1.0)))) for t in TERM}


def norm_rows():
    norms = np.zeros((ROWS, SLOTS), np.float32)
    for t, n in TERM.items():
        norms[n] = NORM[t]
    return norms


def small(mib):
    return pltpu.CompilerParams(vmem_limit_bytes=mib * 2**20)


def row(ref, n):
    return jnp.broadcast_to(ref[pl.ds(n, 1), :], (32, 128))


def in_hbm(x):
    return pltpu.with_memory_space_constraint(x, pltpu.HBM)


def iota(shape, axis):
    return lax.broadcasted_iota(jnp.int32, shape, axis)


def split(v):
    high = v.astype(bf16)
    return high, (v - high.astype(f32)).astype(bf16)


def dot(a, b):
    return jnp.dot(a, b, preferred_element_type=f32)


def dot_nt(a, b):
    return lax.dot_general(a, b, (((1,), (1,)), ((), ())), preferred_element_type=f32)


def dot_parts(a, b):
    high = a.astype(bf16).astype(f32)
    rest = a - high
    middle = rest.astype(bf16).astype(f32)
    parts = dot(jnp.concatenate([high, middle, rest - middle], axis=0).astype(bf16), b)
    n = a.shape[0]
    return (parts[2 * n :] + parts[n : 2 * n]) + parts[:n]


def pack_kernel(owner_hbm, pos_hbm, mass_hbm, tgt_hbm, far_hbm, local_hbm, slots_hbm, *rest):
    list_refs, rest = rest[:4], rest[4:]
    out_refs, (owner_ref, pos_ref, mass_ref, sem, count_ref), slot_refs = rest[:2], rest[2:-4], rest[-4:]
    copies = [
        pltpu.make_async_copy(a, b, sem.at[k])
        for k, (a, b) in enumerate(((owner_hbm, owner_ref), (pos_hbm, pos_ref), (mass_hbm, mass_ref)))
    ]
    lists = [
        pltpu.make_async_copy(a, b, sem.at[3 + k])
        for k, (a, b) in enumerate(zip((tgt_hbm, far_hbm, local_hbm, slots_hbm), list_refs))
    ]
    for c in copies + lists:
        c.start()
    for r in slot_refs:
        r[...] = jnp.zeros_like(r)
    for o in range(PEERS):
        count_ref[o] = 0
    me = lax.axis_index("sub")
    for c in copies:
        c.wait()

    def step(i, carry):
        o = owner_ref[0, i]
        rank = count_ref[o]
        count_ref[o] = rank + 1
        slot = (o ^ me) * CAP + rank
        for a in range(3):
            slot_refs[a][pl.ds(slot, 1), :] = pos_ref[a, pl.ds(i, 1), :]
        slot_refs[3][pl.ds(slot, 1), :] = mass_ref[pl.ds(i, 1), :]
        return carry

    lax.fori_loop(0, mass_ref.shape[0], step, 0)
    half = SLOTS // 2
    for k in range(2):
        for a in range(4):
            out_refs[k][:, a * BODIES : (a + 1) * BODIES] = slot_refs[a][k * half : (k + 1) * half, :]
    for c in lists:
        c.wait()


def pack_tiles(owner, positions, masses, lists):
    out = pl.pallas_call(
        pack_kernel,
        out_shape=[VMEM(x.shape, x.dtype) for x in lists]
        + [jax.ShapeDtypeStruct((SLOTS // 2, 4 * BODIES), f32)] * 2,
        in_specs=[pl.BlockSpec(memory_space=pltpu.HBM)] * 7,
        out_specs=[pl.BlockSpec(memory_space=VMEM)] * 6,
        scratch_shapes=[
            pltpu.SMEM((1, owner.shape[0]), jnp.int32),
            VMEM((3, owner.shape[0], BODIES), f32),
            VMEM((owner.shape[0], BODIES), f32),
            pltpu.SemaphoreType.DMA((7,)),
            pltpu.SMEM((PEERS,), jnp.int32),
        ]
        + [VMEM((SLOTS, BODIES), f32)] * 4,
        compiler_params=small(2),
        name="pack",
    )(*map(in_hbm, (owner.T, positions.transpose(1, 0, 2), masses, *lists)))
    return out[:4], out[4], out[5]


def merge_kernel(mine_ref, other_ref, after_ref, *out_refs):
    for q, ref in enumerate(out_refs, start=1):
        ref[0:CAP] = mine_ref[q * CAP : (q + 1) * CAP]
        ref[CAP : 2 * CAP] = other_ref[q * CAP : (q + 1) * CAP]


def merge(mine, other, after):
    vm = pl.BlockSpec(memory_space=VMEM)
    return pl.pallas_call(
        merge_kernel,
        out_shape=[jax.ShapeDtypeStruct((2 * CAP, 4 * BODIES), f32)] * 3,
        in_specs=[vm] * 3,
        out_specs=[vm] * 3,
        compiler_params=small(2),
        name="merge",
    )(mine, other, after)


I_STEP = 16
I_FULL = TERMS // I_STEP
PAIR_STEP = 32
I_ROWS = (I_FULL + 1) * I_STEP
J_STEP = 8
PITCH = CLASSES + 1
J_BLOCKS = ROWS // J_STEP


EARLY = 7


def operator_copy(op_hbm, buf_ref, sem, q, first=0):
    size = min(I_STEP, TERMS - q * I_STEP)
    return pltpu.make_async_copy(
        op_hbm.at[pl.ds(q * I_STEP, size)],
        buf_ref.at[q - first, pl.ds(0, size), pl.ds(0, TERMS)],
        sem.at[q - first],
    )


def count_kernel(tgt_ref, far_ref, local_ref, op_hbm, counts_ref, buf_ref, done_ref, tt_ref, st_ref, sem):
    for q in range(EARLY):
        operator_copy(op_hbm, buf_ref, sem, q).start()

    order = [7, 0, 1, 2, 3, 4, 5, 6]
    for pair in range(4):
        tgt, src = [], []
        for level in order[2 * pair : 2 * pair + 2]:
            tgt.append(tgt_ref[level].astype(f32))
            if level == 7:
                src.append(local_ref[...].astype(f32))
            else:
                offset = {0: SLOTS, 1: 0, 2: KEXP, 3: 0, 4: KEXP, 5: 0, 6: KEXP}[level]
                src.append((far_ref[level] + offset).astype(f32))
        tt_ref[pair] = jnp.concatenate(tgt, axis=0).T
        st_ref[pair] = jnp.concatenate(src, axis=0).T

    ids = iota((160, 128), 0).astype(f32).astype(bf16)

    def onehot(ref, part, c, first, size, total):
        row = jnp.broadcast_to(ref[part, pl.ds(c, 1), :].astype(bf16), (size, 128))
        hits = jnp.where(row == ids[0:size], jnp.ones((), bf16), jnp.zeros((), bf16))
        zeros = lambda n: [jnp.zeros((n, 128), bf16)] if n else []
        return jnp.concatenate(zeros(first) + [hits] + zeros(total - first - size), axis=0)

    def classes(p):
        for k in range(2):
            c = 2 * p + k
            for half, (first, size) in enumerate(((0, 224), (224, 128))):
                cut = 160 if half == 0 else 64
                target = jnp.concatenate([onehot(tt_ref, 2 * half + i, c, 0, 128, 128) for i in range(2)], axis=1)
                source = jnp.concatenate(
                    [
                        onehot(st_ref, 2 * half, c, 0, cut, size),
                        onehot(st_ref, 2 * half + 1, c, cut, size - cut, size),
                    ],
                    axis=1,
                )
                counts = dot_nt(source.astype(f8), target.astype(f8))
                counts_ref[p, first : first + size, k * 128 : k * 128 + 128] = counts.astype(bf16)

    def group(g, carry):
        for i in range(PAIR_STEP):
            classes(g * PAIR_STEP + i)
        return carry

    lax.fori_loop(0, CLASSES // 2 // PAIR_STEP, group, 0)
    done_ref[...] = jnp.zeros_like(done_ref)
    for q in range(EARLY):
        operator_copy(op_hbm, buf_ref, sem, q).wait()


def relay_kernel(buf_ref, op_hbm, after_ref, left_ref, done_ref, late_ref, sem):
    late = [operator_copy(op_hbm, late_ref, sem, q, EARLY) for q in range(EARLY, I_FULL + 1)]
    for c in late:
        c.start()
    for j in range(TERMS, ROWS):
        left_ref[J_BLOCKS - 1, :, (j % J_STEP) * 128 : (j % J_STEP) * 128 + 128] = jnp.zeros((2 * I_ROWS, 128), bf16)

    def relay(q, ref, first):
        rows = ref.at[q - first].reshape(I_STEP * TERMS_PAD, CLASSES)
        at = pl.multiple_of(q * I_STEP, I_STEP)
        for j in range(TERMS):
            v = rows[pl.ds(j, I_STEP, stride=TERMS_PAD), :]
            high, low = split(v)
            lanes = slice((j % J_STEP) * 128, (j % J_STEP) * 128 + 128)
            left_ref[j // J_STEP, pl.ds(at, I_STEP), lanes] = high
            left_ref[j // J_STEP, pl.ds(at + I_ROWS, I_STEP), lanes] = low

    lax.fori_loop(0, EARLY, lambda q, _: (relay(q, buf_ref, 0), 0)[1], 0)
    for c in late:
        c.wait()
    lax.fori_loop(EARLY, I_FULL + 1, lambda q, _: (relay(q, late_ref, EARLY), 0)[1], 0)
    done_ref[...] = jnp.zeros_like(done_ref)


def count_pairs(m2l_target, far_source, local_source, operators):
    vm = pl.BlockSpec(memory_space=VMEM)
    return pl.pallas_call(
        count_kernel,
        out_shape=[
            VMEM((CLASSES // 2, SOURCES, 256), bf16),
            VMEM((EARLY, I_STEP, TERMS_PAD, CLASSES), f32),
            VMEM((8, 128), f32),
        ],
        in_specs=[vm] * 3 + [pl.BlockSpec(memory_space=pltpu.HBM)],
        out_specs=[vm] * 3,
        scratch_shapes=[
            VMEM((4, 128, 128), f32),
            VMEM((4, 128, 128), f32),
            pltpu.SemaphoreType.DMA((EARLY,)),
        ],
        compiler_params=small(4),
        cost_estimate=pl.CostEstimate(flops=6 * 10**9, bytes_accessed=14 * 10**6, transcendentals=0),
        name="counts",
    )(m2l_target, far_source, local_source, in_hbm(operators))


def relay_operators(rows, operators, after):
    vm = pl.BlockSpec(memory_space=VMEM)
    return pl.pallas_call(
        relay_kernel,
        out_shape=[VMEM((J_BLOCKS, 2 * I_ROWS, J_STEP * CLASSES), bf16), VMEM((8, 128), f32)],
        in_specs=[vm, pl.BlockSpec(memory_space=pltpu.HBM), vm],
        out_specs=[vm] * 2,
        scratch_shapes=[
            VMEM((I_FULL + 1 - EARLY, I_STEP, TERMS_PAD, CLASSES), f32),
            pltpu.SemaphoreType.DMA((I_FULL + 1 - EARLY,)),
        ],
        compiler_params=small(8),
        cost_estimate=pl.CostEstimate(flops=4 * 10**9, bytes_accessed=10**6, transcendentals=0),
        name="relay",
    )(rows, in_hbm(operators), after)


def multipole_kernel(*refs):
    (mine_ref, other_ref, *pieces), refs = refs[:5], refs[5:]
    slots_hbm, _, norm_ref, mt_ref, post_ref, *refs = refs
    exp_refs, (acc_ref, m_ref, rows_ref, slots_ref, sem, recv_ref) = refs[:LEVELS], refs[LEVELS:]
    slots_copy = pltpu.make_async_copy(slots_hbm, slots_ref, sem)
    slots_copy.start()
    me = lax.axis_index("sub")
    for k in range(PEERS):
        rows = pl.ds(pl.multiple_of((me ^ k) * CAP, CAP), CAP)
        if k % 4:
            piece, first = pieces[k % 4 - 1], k // 4 * CAP
        else:
            piece, first = (mine_ref, other_ref)[k // 4], 0
        for a in range(4):
            recv_ref[a, rows, :] = piece[first : first + CAP, a * BODIES : (a + 1) * BODIES]
    for a in range(4):
        post_ref[a] = recv_ref[a].T

    acc_ref[...] = jnp.zeros_like(acc_ref)

    def chunk(q, carry):
        rows = pl.ds(pl.multiple_of(q * 32, 32), 32)
        x, y, z, m = (post_ref[a, rows, :] for a in range(4))

        def fold(term, n):
            part = (term[0:8] + term[8:16]) + (term[16:24] + term[24:32])
            acc_ref[n] += part

        px = m
        for a in range(ORDER + 1):
            py = px
            for b in range(ORDER + 1 - a):
                pz = py
                for c in range(ORDER + 1 - a - b):
                    fold(pz, TERM[a, b, c])
                    if c < ORDER - a - b:
                        pz = pz * z
                if b < ORDER - a:
                    py = py * y
            if a < ORDER:
                px = px * x
        return carry

    lax.fori_loop(0, BODIES // 32, chunk, 0)
    parts = acc_ref.reshape(ROWS * 8, SLOTS)
    for n in range(0, ROWS, 8):
        v = [parts[pl.ds(8 * n + k, 8, stride=8), :] for k in range(8)]
        total = ((v[0] + v[1]) + (v[2] + v[3])) + ((v[4] + v[5]) + (v[6] + v[7]))
        mt_ref[n : n + 8, :] = total * norm_ref[n : n + 8, :]
    m_ref[0] = mt_ref[0:128, :].T
    m_ref[1] = jnp.concatenate([mt_ref[128:ROWS, :], jnp.zeros((256 - ROWS, SLOTS), f32)], axis=0).T
    slots_copy.wait()
    for level in range(LEVELS):

        def row(k, carry):
            slot = slots_ref[level, 0, k]
            for half in range(2):
                rows_ref[half, pl.ds(k, 1), :] = m_ref[half, pl.ds(slot, 1), :]
            return carry

        lax.fori_loop(0, KEXP, row, 0, unroll=32)
        for half in range(2):
            exp_refs[level][:, half * 128 : half * 128 + 128] = rows_ref[half]


def multipoles_of(pieces, export_slots, after):
    vm = pl.BlockSpec(memory_space=VMEM)
    out = pl.pallas_call(
        multipole_kernel,
        out_shape=[
            jax.ShapeDtypeStruct((ROWS, SLOTS), f32),
            jax.ShapeDtypeStruct((4, BODIES, SLOTS), f32),
        ]
        + [jax.ShapeDtypeStruct((KEXP, 256), f32)] * LEVELS,
        in_specs=[vm] * 8,
        out_specs=[vm] * (2 + LEVELS),
        scratch_shapes=[
            pltpu.VMEM((ROWS, 8, SLOTS), f32),
            pltpu.VMEM((2, SLOTS, 128), f32),
            pltpu.VMEM((2, KEXP, 128), f32),
            pltpu.SMEM((LEVELS, 1, KEXP), jnp.int32),
            pltpu.SemaphoreType.DMA,
            VMEM((4, SLOTS, BODIES), f32),
        ],
        compiler_params=small(4),
        name="multipoles",
    )(*pieces, export_slots, after, norm_rows())
    return out[0], out[1], out[2:]


def near_kernel(post_ref, tgt_ref, src_ref, off_ref, near_ref, s_ref, t_ref, a_ref):
    row = iota((128, 128), 0)
    pick_s = jnp.where(src_ref[...] == row, 1.0, 0.0)
    pick_t = jnp.where(tgt_ref[...] == row, 1.0, 0.0)
    k = off_ref[...].astype(f32)
    one, zero = jnp.ones_like(k), jnp.zeros_like(k)
    kx = jnp.where(k >= 9.0, one, zero) + jnp.where(k >= 18.0, one, zero)
    k = k - 9.0 * kx
    ky = jnp.where(k >= 3.0, one, zero) + jnp.where(k >= 6.0, one, zero)
    kz = k - 3.0 * ky
    picks = jnp.concatenate([pick_s, pick_t], axis=1).astype(bf16)
    shifts = (kx, ky, kz)
    for a in range(4):
        picked = dot_parts(post_ref[a], picks)
        s_ref[a] = picked[:, 0:128] + 2.0 * (shifts[a] - 1.0) if a < 3 else picked[:, 0:128]
        if a < 3:
            t_ref[a] = picked[:, 128:256]

    def chunk(q, carry):
        rows = pl.ds(pl.multiple_of(q * 32, 32), 32)
        tx, ty, tz = (t_ref[a, rows, :] for a in range(3))

        def source(j, state):
            p, ax, ay, az = state
            sx, sy, sz, m = (s_ref[a, pl.ds(j, 1), :] for a in range(4))
            rx, ry, rz = sx - tx, sy - ty, sz - tz
            inv = lax.rsqrt(rx * rx + ry * ry + rz * rz + SOFT)
            w = m * inv
            p = p - w
            w = w * (inv * inv)
            return p, ax + rx * w, ay + ry * w, az + rz * w

        done = lax.fori_loop(0, 128, source, (jnp.zeros((32, 128), f32),) * 4, unroll=32)
        for a in range(4):
            a_ref[a, rows, :] = done[a]
        return carry

    lax.fori_loop(0, 4, chunk, 0)
    into = pick_t.T.astype(bf16)
    for a in range(4):
        near_ref[a] = dot_parts(a_ref[a], into)


def near_field(post, target, source, offset):
    vm = pl.BlockSpec(memory_space=VMEM)
    return pl.pallas_call(
        near_kernel,
        out_shape=jax.ShapeDtypeStruct((4, BODIES, SLOTS), f32),
        in_specs=[vm] * 4,
        out_specs=vm,
        scratch_shapes=[VMEM((4, 128, 128), f32), VMEM((3, 128, 128), f32), VMEM((4, 128, 128), f32)],
        compiler_params=small(4),
        cost_estimate=pl.CostEstimate(flops=8 * 10**9, bytes_accessed=10**6, transcendentals=2 * 10**6),
        name="near",
    )(post, target, source, offset)


def field_kernel(counts_ref, left_ref, mt_ref, *rest):
    far_refs, rest = rest[:LEVELS], rest[LEVELS:]
    post_ref, near_ref, norm_ref, out_ref, src_ref, bt_ref, acc_ref, e_ref, f_ref = rest

    far = jnp.concatenate([r[...] for r in far_refs], axis=0)
    far = jnp.concatenate([far, jnp.zeros((32, 256), f32)], axis=0)
    parts = [mt_ref[...]]
    for q in range(2):
        block = far[q * 128 : q * 128 + 128, :]
        parts.append(jnp.concatenate([block[:, 0:128].T, block[:, 128:256].T[0 : ROWS - 128]], axis=0))
    sources = jnp.concatenate(parts, axis=1)
    high = sources.astype(bf16).astype(f32)
    high, low = high.astype(bf16), (sources - high).astype(bf16)
    src_ref[...] = jnp.concatenate([high, low], axis=1)

    def move(p, carry):
        counts = counts_ref[p]
        moved = dot(src_ref[...], jnp.concatenate([counts, jnp.zeros((32, 256), bf16), counts, jnp.zeros((32, 256), bf16)], axis=0))
        for k in range(2):
            bt_ref[pl.ds(2 * p + k, ROWS, stride=PITCH), :] = moved[:, k * 128 : k * 128 + 128]
        return carry

    lax.fori_loop(0, CLASSES // 2, move, 0, unroll=64)

    acc_ref[...] = jnp.zeros_like(acc_ref)

    def contract(jb, carry):
        right = [
            jnp.concatenate(split(bt_ref[pl.ds((jb * J_STEP + j) * PITCH, CLASSES), :]), axis=1)
            for j in range(J_STEP)
        ]
        acc_ref[...] += dot(left_ref[jb], jnp.concatenate(right, axis=0))
        return carry

    lax.fori_loop(0, J_BLOCKS, contract, 0, unroll=21)
    acc = acc_ref[...]
    e = (acc[I_ROWS:, 128:] + acc[I_ROWS:, :128]) + acc[:I_ROWS, 128:] + acc[:I_ROWS, :128]
    e_ref[...] = e[0:ROWS] * norm_ref[...]

    present = jnp.where(post_ref[3, 0:1, :] > 0.0, 1.0, 0.0)

    def chunk(q, carry):
        rows = pl.ds(pl.multiple_of(q * 32, 32), 32)
        x, y, z = (post_ref[a, rows, :] for a in range(3))

        def coef(a, b, c):
            return row(e_ref, TERM[a, b, c])

        p = px = py = pz = None
        for a in range(ORDER, -1, -1):
            r = ry = rz = None
            for b in range(ORDER - a, -1, -1):
                top = ORDER - a - b
                v = coef(a, b, top)
                vz = None
                for c in range(top - 1, -1, -1):
                    vz = v if vz is None else vz * z + v
                    v = v * z + coef(a, b, c)
                if r is None:
                    r = v
                else:
                    ry = r if ry is None else ry * y + r
                    r = r * y + v
                    if vz is not None:
                        rz = vz if rz is None else rz * y + vz
            if p is None:
                p = r
            else:
                px = p if px is None else px * x + p
                p = p * x + r
                py = ry if py is None else py * x + ry
                pz = rz if pz is None else pz * x + rz
        for a, v in enumerate((p, -px, -py, -pz)):
            f_ref[a, rows, :] = (v + near_ref[a, rows, :]) * present
        return carry

    lax.fori_loop(0, BODIES // 32, chunk, 0)
    for a in range(4):
        out_ref[:, a, :] = f_ref[a].T


def field(counts, left, mt, far, post, near):
    vm = pl.BlockSpec(memory_space=VMEM)
    return pl.pallas_call(
        field_kernel,
        out_shape=jax.ShapeDtypeStruct((SLOTS, 4, BODIES), f32),
        in_specs=[vm] * (6 + LEVELS),
        out_specs=vm,
        scratch_shapes=[
            VMEM((ROWS, 768), bf16),
            VMEM((ROWS * PITCH, SLOTS), f32),
            VMEM((2 * I_ROWS, 256), f32),
            VMEM((ROWS, SLOTS), f32),
            VMEM((4, BODIES, SLOTS), f32),
        ],
        compiler_params=small(20),
        cost_estimate=pl.CostEstimate(flops=40 * 10**9, bytes_accessed=26 * 10**6, transcendentals=0),
        name="field",
    )(counts, left, mt, *far, post, near, norm_rows())


def body(
    positions,
    masses,
    owner,
    operators,
    m2l_target,
    far_source,
    local_source,
    export_slots,
    near_target,
    near_source,
    near_offset,
):
    axes = ("dom", "sub")
    devices = lax.axis_size(axes)
    lists = (m2l_target[0], far_source[0], local_source[0], export_slots.transpose(1, 0, 2))
    (*lists, exports), mine, sent = pack_tiles(owner, positions, masses, lists)

    def swap(rows, k):
        return lax.ppermute(rows, "sub", [(i, i ^ k) for i in range(PEERS)])

    other = swap(sent, 4)
    counts, rows, done = count_pairs(*lists, operators)
    sent = merge(mine, other, done)
    pieces = [swap(sent[k - 1], k) for k in (1, 2, 3)]
    left, done = relay_operators(rows, operators, sent[0])
    mt, post, exported = multipoles_of((mine, other, *pieces), exports, done)
    far = [
        lax.ppermute(rows, axes, [(i, i ^ (1 << level)) for i in range(devices)])
        for level, rows in enumerate(exported)
    ]
    near = near_field(post, near_target, near_source, near_offset)
    return field(counts, left, mt, far, post, near)


def solution(mesh):
    both = ("dom", "sub")
    in_specs = (
        P(both, None, None),
        P(both, None),
        P(both, None),
        P(),
        P(both, None, None, None),
        P(both, None, None, None),
        P(both, None, None),
        P(both, None, None),
        P(both, None),
        P(both, None),
        P(both, None),
    )
    out_specs = P(both, None, None)
    return jax.shard_map(body, mesh=mesh, in_specs=in_specs, out_specs=out_specs, check_vma=False)
```

```python
import functools

import jax
import jax.numpy as jnp
import numpy as np
from jax import lax
from jax.experimental import pallas as pl
from jax.experimental.pallas import tpu as pltpu
from jax.sharding import PartitionSpec as P

ORDER = 8
TERMS = 165
ROWS = 168
TERMS_PAD = ROWS
SOFT = 0.01
SLOTS = 128
PEERS = 8
CAP = SLOTS // PEERS
BODIES = 128
KEXP = 32
LEVELS = 7
CLASSES = 128
SOURCES = SLOTS + LEVELS * KEXP
f32 = jnp.float32
bf16 = jnp.bfloat16
f8 = jnp.float8_e4m3fn
VMEM = pltpu.VMEM
SMEM = pltpu.SMEM


def term_list():
    triples = []
    for degree in range(ORDER + 1):
        for a in range(degree, -1, -1):
            for b in range(degree - a, -1, -1):
                triples.append((a, b, degree - a - b))
    return {t: n for n, t in enumerate(triples)}


TERM = term_list()
NORM = {t: float(np.float32(np.sqrt(np.prod(2.0 * np.array(t) + 1.0)))) for t in TERM}


def norm_rows():
    norms = np.zeros((ROWS, SLOTS), np.float32)
    for t, n in TERM.items():
        norms[n] = NORM[t]
    return norms


def small(mib):
    return pltpu.CompilerParams(vmem_limit_bytes=mib * 2**20)


def row(ref, n):
    return jnp.broadcast_to(ref[pl.ds(n, 1), :], (32, 128))


def in_hbm(x):
    return pltpu.with_memory_space_constraint(x, pltpu.HBM)


def iota(shape, axis):
    return lax.broadcasted_iota(jnp.int32, shape, axis)


def split(v):
    high = v.astype(bf16)
    return high, (v - high.astype(f32)).astype(bf16)


def dot(a, b):
    return jnp.dot(a, b, preferred_element_type=f32)


def dot_nt(a, b):
    return lax.dot_general(a, b, (((1,), (1,)), ((), ())), preferred_element_type=f32)


def dot_parts(a, b):
    high = a.astype(bf16).astype(f32)
    rest = a - high
    middle = rest.astype(bf16).astype(f32)
    parts = dot(jnp.concatenate([high, middle, rest - middle], axis=0).astype(bf16), b)
    n = a.shape[0]
    return (parts[2 * n :] + parts[n : 2 * n]) + parts[:n]


def pack_kernel(owner_hbm, pos_hbm, mass_hbm, tgt_hbm, far_hbm, local_hbm, slots_hbm, *rest):
    list_refs, rest = rest[:4], rest[4:]
    out_refs, (owner_ref, pos_ref, mass_ref, sem, count_ref), slot_refs = rest[:2], rest[2:-4], rest[-4:]
    copies = [
        pltpu.make_async_copy(a, b, sem.at[k])
        for k, (a, b) in enumerate(((owner_hbm, owner_ref), (pos_hbm, pos_ref), (mass_hbm, mass_ref)))
    ]
    lists = [
        pltpu.make_async_copy(a, b, sem.at[3 + k])
        for k, (a, b) in enumerate(zip((tgt_hbm, far_hbm, local_hbm, slots_hbm), list_refs))
    ]
    for c in copies + lists:
        c.start()
    for r in slot_refs:
        r[...] = jnp.zeros_like(r)
    for o in range(PEERS):
        count_ref[o] = 0
    me = lax.axis_index("sub")
    for c in copies:
        c.wait()

    def step(i, carry):
        o = owner_ref[0, i]
        rank = count_ref[o]
        count_ref[o] = rank + 1
        slot = (o ^ me) * CAP + rank
        for a in range(3):
            slot_refs[a][pl.ds(slot, 1), :] = pos_ref[a, pl.ds(i, 1), :]
        slot_refs[3][pl.ds(slot, 1), :] = mass_ref[pl.ds(i, 1), :]
        return carry

    lax.fori_loop(0, mass_ref.shape[0], step, 0)
    half = SLOTS // 2
    for k in range(2):
        for a in range(4):
            out_refs[k][:, a * BODIES : (a + 1) * BODIES] = slot_refs[a][k * half : (k + 1) * half, :]
    for c in lists:
        c.wait()


def pack_tiles(owner, positions, masses, lists):
    out = pl.pallas_call(
        pack_kernel,
        out_shape=[VMEM(x.shape, x.dtype) for x in lists]
        + [jax.ShapeDtypeStruct((SLOTS // 2, 4 * BODIES), f32)] * 2,
        in_specs=[pl.BlockSpec(memory_space=pltpu.HBM)] * 7,
        out_specs=[pl.BlockSpec(memory_space=VMEM)] * 6,
        scratch_shapes=[
            pltpu.SMEM((1, owner.shape[0]), jnp.int32),
            VMEM((3, owner.shape[0], BODIES), f32),
            VMEM((owner.shape[0], BODIES), f32),
            pltpu.SemaphoreType.DMA((7,)),
            pltpu.SMEM((PEERS,), jnp.int32),
        ]
        + [VMEM((SLOTS, BODIES), f32)] * 4,
        compiler_params=small(2),
        name="pack",
    )(*map(in_hbm, (owner.T, positions.transpose(1, 0, 2), masses, *lists)))
    return out[:4], out[4], out[5]


def merge_kernel(mine_ref, other_ref, after_ref, *out_refs):
    for q, ref in enumerate(out_refs, start=1):
        ref[0:CAP] = mine_ref[q * CAP : (q + 1) * CAP]
        ref[CAP : 2 * CAP] = other_ref[q * CAP : (q + 1) * CAP]


def merge(mine, other, after):
    vm = pl.BlockSpec(memory_space=VMEM)
    return pl.pallas_call(
        merge_kernel,
        out_shape=[jax.ShapeDtypeStruct((2 * CAP, 4 * BODIES), f32)] * 3,
        in_specs=[vm] * 3,
        out_specs=[vm] * 3,
        compiler_params=small(2),
        name="merge",
    )(mine, other, after)


I_STEP = 16
I_FULL = TERMS // I_STEP
PAIR_STEP = 32
I_ROWS = (I_FULL + 1) * I_STEP
J_STEP = 8
PITCH = CLASSES + 1
J_BLOCKS = ROWS // J_STEP


EARLY = 9


def operator_copy(op_hbm, buf_ref, sem, q, first=0):
    size = min(I_STEP, TERMS - q * I_STEP)
    return pltpu.make_async_copy(
        op_hbm.at[pl.ds(q * I_STEP, size)],
        buf_ref.at[q - first, pl.ds(0, size), pl.ds(0, TERMS)],
        sem.at[q - first],
    )


def count_kernel(tgt_ref, far_ref, local_ref, op_hbm, counts_ref, buf_ref, done_ref, tt_ref, st_ref, sem):
    for q in range(EARLY):
        operator_copy(op_hbm, buf_ref, sem, q).start()

    order = [7, 0, 1, 2, 3, 4, 5, 6]
    for pair in range(4):
        tgt, src = [], []
        for level in order[2 * pair : 2 * pair + 2]:
            tgt.append(tgt_ref[level].astype(f32))
            if level == 7:
                src.append(local_ref[...].astype(f32))
            else:
                offset = {0: SLOTS, 1: 0, 2: KEXP, 3: 0, 4: KEXP, 5: 0, 6: KEXP}[level]
                src.append((far_ref[level] + offset).astype(f32))
        tt_ref[pair] = jnp.concatenate(tgt, axis=0).T
        st_ref[pair] = jnp.concatenate(src, axis=0).T

    ids = iota((160, 128), 0).astype(f32).astype(bf16)

    def onehot(ref, part, c, first, size, total):
        row = jnp.broadcast_to(ref[part, pl.ds(c, 1), :].astype(bf16), (size, 128))
        hits = jnp.where(row == ids[0:size], jnp.ones((), bf16), jnp.zeros((), bf16))
        zeros = lambda n: [jnp.zeros((n, 128), bf16)] if n else []
        return jnp.concatenate(zeros(first) + [hits] + zeros(total - first - size), axis=0)

    def classes(p):
        for k in range(2):
            c = 2 * p + k
            for half, (first, size) in enumerate(((0, 224), (224, 128))):
                cut = 160 if half == 0 else 64
                target = jnp.concatenate([onehot(tt_ref, 2 * half + i, c, 0, 128, 128) for i in range(2)], axis=1)
                source = jnp.concatenate(
                    [
                        onehot(st_ref, 2 * half, c, 0, cut, size),
                        onehot(st_ref, 2 * half + 1, c, cut, size - cut, size),
                    ],
                    axis=1,
                )
                counts = dot_nt(source.astype(f8), target.astype(f8))
                counts_ref[p, first : first + size, k * 128 : k * 128 + 128] = counts.astype(bf16)

    def group(g, carry):
        for i in range(PAIR_STEP):
            classes(g * PAIR_STEP + i)
        return carry

    lax.fori_loop(0, CLASSES // 2 // PAIR_STEP, group, 0)
    done_ref[...] = jnp.zeros_like(done_ref)
    for q in range(EARLY):
        operator_copy(op_hbm, buf_ref, sem, q).wait()


def relay_kernel(buf_ref, op_hbm, after_ref, left_ref, done_ref, late_ref, sem):
    late = [operator_copy(op_hbm, late_ref, sem, q, EARLY) for q in range(EARLY, I_FULL + 1)]
    for c in late:
        c.start()
    for j in range(TERMS, ROWS):
        left_ref[J_BLOCKS - 1, :, (j % J_STEP) * 128 : (j % J_STEP) * 128 + 128] = jnp.zeros((2 * I_ROWS, 128), bf16)

    def relay(q, ref, first):
        rows = ref.at[q - first].reshape(I_STEP * TERMS_PAD, CLASSES)
        at = pl.multiple_of(q * I_STEP, I_STEP)
        for j in range(TERMS):
            v = rows[pl.ds(j, I_STEP, stride=TERMS_PAD), :]
            high, low = split(v)
            lanes = slice((j % J_STEP) * 128, (j % J_STEP) * 128 + 128)
            left_ref[j // J_STEP, pl.ds(at, I_STEP), lanes] = high
            left_ref[j // J_STEP, pl.ds(at + I_ROWS, I_STEP), lanes] = low

    lax.fori_loop(0, EARLY, lambda q, _: (relay(q, buf_ref, 0), 0)[1], 0)
    for c in late:
        c.wait()
    lax.fori_loop(EARLY, I_FULL + 1, lambda q, _: (relay(q, late_ref, EARLY), 0)[1], 0)
    done_ref[...] = jnp.zeros_like(done_ref)


def count_pairs(m2l_target, far_source, local_source, operators):
    vm = pl.BlockSpec(memory_space=VMEM)
    return pl.pallas_call(
        count_kernel,
        out_shape=[
            VMEM((CLASSES // 2, SOURCES, 256), bf16),
            VMEM((EARLY, I_STEP, TERMS_PAD, CLASSES), f32),
            VMEM((8, 128), f32),
        ],
        in_specs=[vm] * 3 + [pl.BlockSpec(memory_space=pltpu.HBM)],
        out_specs=[vm] * 3,
        scratch_shapes=[
            VMEM((4, 128, 128), f32),
            VMEM((4, 128, 128), f32),
            pltpu.SemaphoreType.DMA((EARLY,)),
        ],
        compiler_params=small(4),
        cost_estimate=pl.CostEstimate(flops=6 * 10**9, bytes_accessed=14 * 10**6, transcendentals=0),
        name="counts",
    )(m2l_target, far_source, local_source, in_hbm(operators))


def relay_operators(rows, operators, after):
    vm = pl.BlockSpec(memory_space=VMEM)
    return pl.pallas_call(
        relay_kernel,
        out_shape=[VMEM((J_BLOCKS, 2 * I_ROWS, J_STEP * CLASSES), bf16), VMEM((8, 128), f32)],
        in_specs=[vm, pl.BlockSpec(memory_space=pltpu.HBM), vm],
        out_specs=[vm] * 2,
        scratch_shapes=[
            VMEM((I_FULL + 1 - EARLY, I_STEP, TERMS_PAD, CLASSES), f32),
            pltpu.SemaphoreType.DMA((I_FULL + 1 - EARLY,)),
        ],
        compiler_params=small(8),
        cost_estimate=pl.CostEstimate(flops=4 * 10**9, bytes_accessed=10**6, transcendentals=0),
        name="relay",
    )(rows, in_hbm(operators), after)


def multipole_kernel(*refs):
    (mine_ref, other_ref, *pieces), refs = refs[:5], refs[5:]
    slots_hbm, _, norm_ref, mt_ref, post_ref, *refs = refs
    exp_refs, (acc_ref, m_ref, rows_ref, slots_ref, sem, recv_ref) = refs[:LEVELS], refs[LEVELS:]
    slots_copy = pltpu.make_async_copy(slots_hbm, slots_ref, sem)
    slots_copy.start()
    me = lax.axis_index("sub")
    for k in range(PEERS):
        rows = pl.ds(pl.multiple_of((me ^ k) * CAP, CAP), CAP)
        if k % 4:
            piece, first = pieces[k % 4 - 1], k // 4 * CAP
        else:
            piece, first = (mine_ref, other_ref)[k // 4], 0
        for a in range(4):
            recv_ref[a, rows, :] = piece[first : first + CAP, a * BODIES : (a + 1) * BODIES]
    for a in range(4):
        post_ref[a] = recv_ref[a].T

    acc_ref[...] = jnp.zeros_like(acc_ref)

    def chunk(q, carry):
        rows = pl.ds(pl.multiple_of(q * 32, 32), 32)
        x, y, z, m = (post_ref[a, rows, :] for a in range(4))

        def fold(term, n):
            part = (term[0:8] + term[8:16]) + (term[16:24] + term[24:32])
            acc_ref[n] += part

        px = m
        for a in range(ORDER + 1):
            py = px
            for b in range(ORDER + 1 - a):
                pz = py
                for c in range(ORDER + 1 - a - b):
                    fold(pz, TERM[a, b, c])
                    if c < ORDER - a - b:
                        pz = pz * z
                if b < ORDER - a:
                    py = py * y
            if a < ORDER:
                px = px * x
        return carry

    lax.fori_loop(0, BODIES // 32, chunk, 0)
    parts = acc_ref.reshape(ROWS * 8, SLOTS)
    for n in range(0, ROWS, 8):
        v = [parts[pl.ds(8 * n + k, 8, stride=8), :] for k in range(8)]
        total = ((v[0] + v[1]) + (v[2] + v[3])) + ((v[4] + v[5]) + (v[6] + v[7]))
        mt_ref[n : n + 8, :] = total * norm_ref[n : n + 8, :]
    m_ref[0] = mt_ref[0:128, :].T
    m_ref[1] = jnp.concatenate([mt_ref[128:ROWS, :], jnp.zeros((256 - ROWS, SLOTS), f32)], axis=0).T
    slots_copy.wait()
    for level in range(LEVELS):

        def row(k, carry):
            slot = slots_ref[level, 0, k]
            for half in range(2):
                rows_ref[half, pl.ds(k, 1), :] = m_ref[half, pl.ds(slot, 1), :]
            return carry

        lax.fori_loop(0, KEXP, row, 0, unroll=32)
        for half in range(2):
            exp_refs[level][:, half * 128 : half * 128 + 128] = rows_ref[half]


def multipoles_of(pieces, export_slots, after):
    vm = pl.BlockSpec(memory_space=VMEM)
    out = pl.pallas_call(
        multipole_kernel,
        out_shape=[
            jax.ShapeDtypeStruct((ROWS, SLOTS), f32),
            jax.ShapeDtypeStruct((4, BODIES, SLOTS), f32),
        ]
        + [jax.ShapeDtypeStruct((KEXP, 256), f32)] * LEVELS,
        in_specs=[vm] * 8,
        out_specs=[vm] * (2 + LEVELS),
        scratch_shapes=[
            pltpu.VMEM((ROWS, 8, SLOTS), f32),
            pltpu.VMEM((2, SLOTS, 128), f32),
            pltpu.VMEM((2, KEXP, 128), f32),
            pltpu.SMEM((LEVELS, 1, KEXP), jnp.int32),
            pltpu.SemaphoreType.DMA,
            VMEM((4, SLOTS, BODIES), f32),
        ],
        compiler_params=small(4),
        name="multipoles",
    )(*pieces, export_slots, after, norm_rows())
    return out[0], out[1], out[2:]


def near_kernel(post_ref, tgt_ref, src_ref, off_ref, near_ref, s_ref, t_ref, a_ref):
    row = iota((128, 128), 0)
    pick_s = jnp.where(src_ref[...] == row, 1.0, 0.0)
    pick_t = jnp.where(tgt_ref[...] == row, 1.0, 0.0)
    k = off_ref[...].astype(f32)
    one, zero = jnp.ones_like(k), jnp.zeros_like(k)
    kx = jnp.where(k >= 9.0, one, zero) + jnp.where(k >= 18.0, one, zero)
    k = k - 9.0 * kx
    ky = jnp.where(k >= 3.0, one, zero) + jnp.where(k >= 6.0, one, zero)
    kz = k - 3.0 * ky
    picks = jnp.concatenate([pick_s, pick_t], axis=1).astype(bf16)
    shifts = (kx, ky, kz)
    for a in range(4):
        picked = dot_parts(post_ref[a], picks)
        s_ref[a] = picked[:, 0:128] + 2.0 * (shifts[a] - 1.0) if a < 3 else picked[:, 0:128]
        if a < 3:
            t_ref[a] = picked[:, 128:256]

    def chunk(q, carry):
        rows = pl.ds(pl.multiple_of(q * 32, 32), 32)
        tx, ty, tz = (t_ref[a, rows, :] for a in range(3))

        def source(j, state):
            p, ax, ay, az = state
            sx, sy, sz, m = (s_ref[a, pl.ds(j, 1), :] for a in range(4))
            rx, ry, rz = sx - tx, sy - ty, sz - tz
            inv = lax.rsqrt(rx * rx + ry * ry + rz * rz + SOFT)
            w = m * inv
            p = p - w
            w = w * (inv * inv)
            return p, ax + rx * w, ay + ry * w, az + rz * w

        done = lax.fori_loop(0, 128, source, (jnp.zeros((32, 128), f32),) * 4, unroll=32)
        for a in range(4):
            a_ref[a, rows, :] = done[a]
        return carry

    lax.fori_loop(0, 4, chunk, 0)
    into = pick_t.T.astype(bf16)
    for a in range(4):
        near_ref[a] = dot_parts(a_ref[a], into)


def near_field(post, target, source, offset):
    vm = pl.BlockSpec(memory_space=VMEM)
    return pl.pallas_call(
        near_kernel,
        out_shape=jax.ShapeDtypeStruct((4, BODIES, SLOTS), f32),
        in_specs=[vm] * 4,
        out_specs=vm,
        scratch_shapes=[VMEM((4, 128, 128), f32), VMEM((3, 128, 128), f32), VMEM((4, 128, 128), f32)],
        compiler_params=small(4),
        cost_estimate=pl.CostEstimate(flops=8 * 10**9, bytes_accessed=10**6, transcendentals=2 * 10**6),
        name="near",
    )(post, target, source, offset)


def field_kernel(counts_ref, left_ref, mt_ref, *rest):
    far_refs, rest = rest[:LEVELS], rest[LEVELS:]
    post_ref, near_ref, norm_ref, out_ref, src_ref, bt_ref, acc_ref, e_ref, f_ref = rest

    far = jnp.concatenate([r[...] for r in far_refs], axis=0)
    far = jnp.concatenate([far, jnp.zeros((32, 256), f32)], axis=0)
    parts = [mt_ref[...]]
    for q in range(2):
        block = far[q * 128 : q * 128 + 128, :]
        parts.append(jnp.concatenate([block[:, 0:128].T, block[:, 128:256].T[0 : ROWS - 128]], axis=0))
    sources = jnp.concatenate(parts, axis=1)
    high = sources.astype(bf16).astype(f32)
    high, low = high.astype(bf16), (sources - high).astype(bf16)
    src_ref[...] = jnp.concatenate([high, low], axis=1)

    def move(p, carry):
        counts = counts_ref[p]
        moved = dot(src_ref[...], jnp.concatenate([counts, jnp.zeros((32, 256), bf16), counts, jnp.zeros((32, 256), bf16)], axis=0))
        for k in range(2):
            bt_ref[pl.ds(2 * p + k, ROWS, stride=PITCH), :] = moved[:, k * 128 : k * 128 + 128]
        return carry

    lax.fori_loop(0, CLASSES // 2, move, 0, unroll=64)

    acc_ref[...] = jnp.zeros_like(acc_ref)

    def contract(jb, carry):
        right = [
            jnp.concatenate(split(bt_ref[pl.ds((jb * J_STEP + j) * PITCH, CLASSES), :]), axis=1)
            for j in range(J_STEP)
        ]
        acc_ref[...] += dot(left_ref[jb], jnp.concatenate(right, axis=0))
        return carry

    lax.fori_loop(0, J_BLOCKS, contract, 0, unroll=21)
    acc = acc_ref[...]
    e = (acc[I_ROWS:, 128:] + acc[I_ROWS:, :128]) + acc[:I_ROWS, 128:] + acc[:I_ROWS, :128]
    e_ref[...] = e[0:ROWS] * norm_ref[...]

    present = jnp.where(post_ref[3, 0:1, :] > 0.0, 1.0, 0.0)

    def chunk(q, carry):
        rows = pl.ds(pl.multiple_of(q * 32, 32), 32)
        x, y, z = (post_ref[a, rows, :] for a in range(3))

        def coef(a, b, c):
            return row(e_ref, TERM[a, b, c])

        p = px = py = pz = None
        for a in range(ORDER, -1, -1):
            r = ry = rz = None
            for b in range(ORDER - a, -1, -1):
                top = ORDER - a - b
                v = coef(a, b, top)
                vz = None
                for c in range(top - 1, -1, -1):
                    vz = v if vz is None else vz * z + v
                    v = v * z + coef(a, b, c)
                if r is None:
                    r = v
                else:
                    ry = r if ry is None else ry * y + r
                    r = r * y + v
                    if vz is not None:
                        rz = vz if rz is None else rz * y + vz
            if p is None:
                p = r
            else:
                px = p if px is None else px * x + p
                p = p * x + r
                py = ry if py is None else py * x + ry
                pz = rz if pz is None else pz * x + rz
        for a, v in enumerate((p, -px, -py, -pz)):
            f_ref[a, rows, :] = (v + near_ref[a, rows, :]) * present
        return carry

    lax.fori_loop(0, BODIES // 32, chunk, 0)
    for a in range(4):
        out_ref[:, a, :] = f_ref[a].T


def field(counts, left, mt, far, post, near):
    vm = pl.BlockSpec(memory_space=VMEM)
    return pl.pallas_call(
        field_kernel,
        out_shape=jax.ShapeDtypeStruct((SLOTS, 4, BODIES), f32),
        in_specs=[vm] * (6 + LEVELS),
        out_specs=vm,
        scratch_shapes=[
            VMEM((ROWS, 768), bf16),
            VMEM((ROWS * PITCH, SLOTS), f32),
            VMEM((2 * I_ROWS, 256), f32),
            VMEM((ROWS, SLOTS), f32),
            VMEM((4, BODIES, SLOTS), f32),
        ],
        compiler_params=small(20),
        cost_estimate=pl.CostEstimate(flops=40 * 10**9, bytes_accessed=26 * 10**6, transcendentals=0),
        name="field",
    )(counts, left, mt, *far, post, near, norm_rows())


def body(
    positions,
    masses,
    owner,
    operators,
    m2l_target,
    far_source,
    local_source,
    export_slots,
    near_target,
    near_source,
    near_offset,
):
    axes = ("dom", "sub")
    devices = lax.axis_size(axes)
    lists = (m2l_target[0], far_source[0], local_source[0], export_slots.transpose(1, 0, 2))
    (*lists, exports), mine, sent = pack_tiles(owner, positions, masses, lists)

    def swap(rows, k):
        return lax.ppermute(rows, "sub", [(i, i ^ k) for i in range(PEERS)])

    other = swap(sent, 4)
    counts, rows, done = count_pairs(*lists, operators)
    sent = merge(mine, other, done)
    pieces = [swap(sent[k - 1], k) for k in (1, 2, 3)]
    left, done = relay_operators(rows, operators, sent[0])
    mt, post, exported = multipoles_of((mine, other, *pieces), exports, done)
    far = [
        lax.ppermute(rows, axes, [(i, i ^ (1 << level)) for i in range(devices)])
        for level, rows in enumerate(exported)
    ]
    near = near_field(post, near_target, near_source, near_offset)
    return field(counts, left, mt, far, post, near)


def solution(mesh):
    both = ("dom", "sub")
    in_specs = (
        P(both, None, None),
        P(both, None),
        P(both, None),
        P(),
        P(both, None, None, None),
        P(both, None, None, None),
        P(both, None, None),
        P(both, None, None),
        P(both, None),
        P(both, None),
        P(both, None),
    )
    out_specs = P(both, None, None)
    return jax.shard_map(body, mesh=mesh, in_specs=in_specs, out_specs=out_specs, check_vma=False)
```
